32 devices in a mesh: grp: 8 (over y, x, core), ep: 4 (over z).
Axes of the slice: x: 2, y: 2, z: 4, core: 2. Of those that a mesh axis runs over, the one named last changes fastest.
Arguments:
- tokens: bfloat16 [8, 1024, 2048], P('grp', 'ep'), may hold values from -6 to 6
- attn_norm: bfloat16 [2048], P('grp'), may hold values from 0.5 to 1.5
- query_weight: bfloat16 [2048, 2048], P('grp', 'ep'), may hold values from -0.125 to 0.125
- key_weight: bfloat16 [2048, 2048], P('grp', 'ep'), may hold values from -0.125 to 0.125
- value_weight: bfloat16 [2048, 2048], P('grp', 'ep'), may hold values from -0.125 to 0.125
- query_bias: bfloat16 [16, 128], P('ep', 'grp'), may hold values from -2.5 to 2.5
- key_bias: bfloat16 [16, 128], P('ep', 'grp'), may hold values from -2.5 to 2.5
- value_bias: bfloat16 [16, 128], P('ep', 'grp'), may hold values from -2.5 to 2.5
- out_weight: bfloat16 [2048, 2048], P('ep', 'grp'), may hold values from -0.5 to 0.5
- ffn_norm: bfloat16 [2048], P('grp'), may hold values from 0.5 to 1.5
- router_weight: bfloat16 [2048, 8], P('grp'), may hold values from -0.0625 to 0.0625
- shared_switch: bfloat16 [2048], P('grp'), may hold values from -0.125 to 0.125
- shared_gate: bfloat16 [2048, 5632], P('grp', 'ep'), may hold values from -0.125 to 0.125
- shared_up: bfloat16 [2048, 5632], P('grp', 'ep'), may hold values from -0.125 to 0.125
- shared_down: bfloat16 [5632, 2048], P('ep', 'grp'), may hold values from -0.15625 to 0.15625
- expert_gate: bfloat16 [8, 2048, 1408], P('ep'), may hold values from -0.125 to 0.125
- expert_up: bfloat16 [8, 2048, 1408], P('ep'), may hold values from -0.125 to 0.125
- expert_down: bfloat16 [8, 1408, 2048], P('ep'), may hold values from -0.625 to 0.625
- routes: int32 [8, 1024, 4], P('grp', 'ep'), may hold values from 0 to 7, all different within a row
- pieces: int32 [8, 1024], P('grp'), may hold values from 0 to 3, as said below
- documents: int32 [8, 1024], P('grp'), may hold values from 0 to 3, never falling along the last dimension, each value on 1 to 512 neighbouring positions
- cotangent: bfloat16 [8, 1024, 2048], P('grp', 'ep'), may hold values from -6 to 6
Outputs:
- layer_out: bfloat16 [8, 1024, 2048], P('grp', 'ep')
- tokens_grad: float32 [8, 1024, 2048], P('grp', 'ep')
- attn_norm_grad: float32 [2048], P('grp')
- query_grad: float32 [2048, 2048], P('grp', 'ep')
- key_grad: float32 [2048, 2048], P('grp', 'ep')
- value_grad: float32 [2048, 2048], P('grp', 'ep')
- query_bias_grad: float32 [16, 128], P('ep', 'grp')
- key_bias_grad: float32 [16, 128], P('ep', 'grp')
- value_bias_grad: float32 [16, 128], P('ep', 'grp')
- out_grad: float32 [2048, 2048], P('ep', 'grp')
- ffn_norm_grad: float32 [2048], P('grp')
- router_grad: float32 [2048, 8], P('grp')
- switch_grad: float32 [2048], P('grp')
- shared_gate_grad: float32 [2048, 5632], P('grp', 'ep')
- shared_up_grad: float32 [2048, 5632], P('grp', 'ep')
- shared_down_grad: float32 [5632, 2048], P('ep', 'grp')
- expert_gate_grad: float32 [8, 2048, 1408], P('ep', 'grp')
- expert_up_grad: float32 [8, 2048, 1408], P('ep', 'grp')
- expert_down_grad: float32 [8, 1408, 2048], P('ep', None, 'grp')
The draws below stay inside these ranges and needn't reach their ends.
Inputs may be any that keep to these rules, and one draw needn't show every extreme that they name: `routes`: each token names 4 distinct experts; every expert is named by some token. Each aligned run of 256 positions of a sequence holds one number: 0 for text, or the run's index plus one for a picture piece. The first run of every sequence and the run before the last are picture pieces, and the last is text. `documents`: document numbers never fall along a sequence; a document spans 1 to 1024 // 2 positions, and one spans exactly 1024 // 2.
All inputs are finite; a program needn't handle non-finite values.
Results may differ from the reference program's by a relative error of at most 0.025.
Values may be sent and summed in bfloat16 or wider, within the bound.
No kernel may reach another device: no remote copies, remote signals or barrier semaphores. Data moves between devices by JAX's collectives and lax.ppermute only.
A program may use at most 384 MiB of HBM per device.

```python
import math
import jax
import jax.numpy as jnp
import numpy as np
from jax import lax

MODEL_DIM = 2048
HEADS = 16
HEAD = 128
FF_E = 1408
FF_S = 5632
TOP = 4
SEQUENCE_TOKENS = 1024
PIECE = 256
DOCS = 4
ROWS = 1
SEQUENCE_COUNT = 8
TOK_DEV = 256
EXPERTS = 8
CAP = 160
N_GRP = 8
N_EP = 4


def draw_pieces(key, part):
    block_count = SEQUENCE_TOKENS // PIECE
    picks = jax.random.randint(key, (SEQUENCE_COUNT, block_count), 0, 3)
    block_pos = jnp.arange(block_count, dtype=jnp.int32)[None, :]
    picks = jnp.where(block_pos == block_count - 2, 1, picks)
    picks = jnp.where(block_pos == 0, 1, picks)
    picks = jnp.where(block_pos == block_count - 1, 0, picks)
    number = jnp.where(picks == 0, 0, block_pos + 1)
    return jnp.repeat(number, PIECE, axis=1).astype(jnp.int32)


def levels(key, extent, cuts, smallest, largest):
    loudness, own = 1.0, jax.random.fold_in(key, 6)
    for dim, blocks in cuts:
        draws = jnp.exp(jax.random.uniform(jax.random.fold_in(own, dim), (blocks,), jnp.float32, smallest / len(cuts), largest / len(cuts)))
        loudness = loudness * jnp.repeat(draws, extent[dim] // blocks).reshape([-1 if axis == dim else 1 for axis in range(len(extent))])
    return loudness


def different_ones(own_key, rows, number_of, top, lift):
    sequence = jax.random.permutation(jax.random.fold_in(own_key, 1), number_of)
    boost = sequence
    for power in range(3):
        boost = boost * boost // number_of
    boost = boost * lift // number_of
    chance = jax.random.randint(jax.random.fold_in(own_key, 2), (rows, number_of), 0, 4096) + boost
    fixed_rows = jax.random.permutation(jax.random.fold_in(own_key, 3), rows)[jnp.arange(number_of) % rows]
    chance = jnp.where(jnp.arange(rows)[:, None] == fixed_rows[None, :], 1 << 14, chance)
    score = chance * number_of + jnp.arange(number_of)
    return lax.top_k(score.astype(jnp.int32), top)[1].astype(jnp.int32)


def length_profile(count, total, most, slope):
    weights = [(1 << 20) // math.isqrt(grade ** slope) + 1 for grade in range(2, count + 1)]
    rest, given = total - most - (count - 1), [1] * (count - 1)
    while rest > 0:
        movable = [i for i in range(count - 1) if given[i] < most]
        whole, left = sum([weights[i] for i in movable]), rest
        for i in movable:
            more = min(most - given[i], max(1, left * weights[i] // whole), rest)
            given[i] = given[i] + more
            rest = rest - more
    return np.array([most] + given)


def ragged(own_key, number_of, total, bound, skew):
    if number_of == 2:
        one = jax.random.randint(own_key, (), max(1, total - bound), min(bound, total - 1) + 1)
        return jnp.stack([one, total - one])
    lengths = jnp.asarray(length_profile(number_of, total, bound, skew), jnp.int32)
    twos = (number_of - 1) // 2
    giver, taker = lengths[1:1 + 2 * twos:2], lengths[2:2 + 2 * twos:2]
    room = jnp.minimum(giver - 1, bound - taker)
    moved = jax.random.randint(jax.random.fold_in(own_key, 1), (twos,), 0, 1 << 20) % (room + 1)
    lengths = lengths.at[1:1 + 2 * twos:2].set(giver - moved).at[2:2 + 2 * twos:2].set(taker + moved)
    return lengths[jax.random.permutation(jax.random.fold_in(own_key, 2), number_of)]


def noise(rng, dims, spread, limit, cuts=(), held_as=jnp.bfloat16):
    values = spread * jax.random.normal(rng, dims, jnp.float32)
    if cuts:
        values = values * levels(rng, dims, cuts, -0.22, 0.18)
    return jnp.clip(values, -limit, limit).astype(held_as)


def setup_inputs(seed: int = 0) -> dict:
    key_of = jax.random.split(jax.random.key(seed), 23)
    tokens = noise(key_of[0], (SEQUENCE_COUNT, SEQUENCE_TOKENS, MODEL_DIM), 1.0, 6.0, ((0, 8), (1, 4)))
    attn_norm = jnp.clip(1.0 + 0.1 * jax.random.normal(key_of[1], (MODEL_DIM,), jnp.float32), 0.5, 1.5).astype(jnp.bfloat16)
    query_weight = noise(key_of[2], (MODEL_DIM, MODEL_DIM), MODEL_DIM ** -0.5, 0.125, ((0, 8), (1, 4)))
    key_weight = noise(key_of[3], (MODEL_DIM, MODEL_DIM), MODEL_DIM ** -0.5, 0.125, ((0, 8), (1, 4)))
    value_weight = noise(key_of[4], (MODEL_DIM, MODEL_DIM), MODEL_DIM ** -0.5, 0.125, ((0, 8), (1, 4)))
    query_bias = noise(key_of[5], (HEADS, HEAD), 0.3, 2.5, ((0, 4), (1, 8)))
    key_bias = noise(key_of[6], (HEADS, HEAD), 0.3, 2.5, ((0, 4), (1, 8)))
    value_bias = noise(key_of[7], (HEADS, HEAD), 0.3, 2.5, ((0, 4), (1, 8)))
    out_weight = noise(key_of[8], (MODEL_DIM, MODEL_DIM), (MODEL_DIM // 16) ** -0.5, 0.5, ((0, 4), (1, 8)))
    ffn_norm = jnp.clip(1.0 + 0.1 * jax.random.normal(key_of[9], (MODEL_DIM,), jnp.float32), 0.5, 1.5).astype(jnp.bfloat16)
    router_weight = noise(key_of[10], (MODEL_DIM, EXPERTS), (4 * MODEL_DIM) ** -0.5, 0.0625, ((0, 8),))
    shared_switch = noise(key_of[11], (MODEL_DIM,), MODEL_DIM ** -0.5, 0.125, ((0, 8),))
    shared_gate = noise(key_of[12], (MODEL_DIM, FF_S), MODEL_DIM ** -0.5, 0.125, ((0, 8), (1, 4)))
    shared_up = noise(key_of[13], (MODEL_DIM, FF_S), MODEL_DIM ** -0.5, 0.125, ((0, 8), (1, 4)))
    shared_down = noise(key_of[14], (FF_S, MODEL_DIM), (FF_S // 4) ** -0.5, 0.15625, ((0, 4), (1, 8)))
    expert_gate = noise(key_of[15], (EXPERTS, MODEL_DIM, FF_E), MODEL_DIM ** -0.5, 0.125, ((0, 4),))
    expert_up = noise(key_of[16], (EXPERTS, MODEL_DIM, FF_E), MODEL_DIM ** -0.5, 0.125, ((0, 4),))
    expert_down = noise(key_of[17], (EXPERTS, FF_E, MODEL_DIM), (FF_E // 16) ** -0.5, 0.625, ((0, 4),))
    routes = different_ones(key_of[18], SEQUENCE_COUNT * SEQUENCE_TOKENS, EXPERTS, TOP, 4096).reshape((SEQUENCE_COUNT, SEQUENCE_TOKENS, TOP))
    pieces = draw_pieces(jax.random.fold_in(key_of[22], 71), 0)
    documents = jax.vmap(lambda own: jnp.searchsorted(jnp.cumsum(ragged(own, DOCS, SEQUENCE_TOKENS, SEQUENCE_TOKENS // 2, 0)), jnp.arange(SEQUENCE_TOKENS), side="right"))(jax.random.split(key_of[20], SEQUENCE_COUNT)).reshape((SEQUENCE_COUNT, SEQUENCE_TOKENS)).astype(jnp.int32)
    cotangent = noise(key_of[21], (SEQUENCE_COUNT, SEQUENCE_TOKENS, MODEL_DIM), 1.0, 6.0, ((0, 8), (1, 4)))
    return dict(tokens=tokens, attn_norm=attn_norm, query_weight=query_weight, key_weight=key_weight, value_weight=value_weight, query_bias=query_bias, key_bias=key_bias, value_bias=value_bias, out_weight=out_weight, ffn_norm=ffn_norm, router_weight=router_weight, shared_switch=shared_switch, shared_gate=shared_gate, shared_up=shared_up, shared_down=shared_down, expert_gate=expert_gate, expert_up=expert_up, expert_down=expert_down, routes=routes, pieces=pieces, documents=documents, cotangent=cotangent)


EPS = 1e-06
THETA = 1000000.0
NEG = -1e+30
HIGH = lax.Precision.HIGHEST

@jax.custom_vjp
def low(v):
    return lax.optimization_barrier(v.astype(jnp.bfloat16)).astype(jnp.float32)

@jax.custom_vjp
def low_back(v):
    return v

def low_keep(v):
    return (low(v), None)

def low_pass(kept, grad):
    return (grad,)

def back_keep(v):
    return (v, None)

def back_low(kept, grad):
    return (low(grad),)
low.defvjp(low_keep, low_pass)
low_back.defvjp(back_keep, back_low)

def matmul(left_side, right_side):
    return jnp.dot(left_side, right_side, precision=HIGH, preferred_element_type=jnp.float32)

def normed(values):
    return values * lax.rsqrt(lax.optimization_barrier(jnp.mean(values * values, axis=-1, keepdims=True)) + EPS)

def rotary_tables(length, head_size):
    position = jnp.arange(length, dtype=jnp.float32)
    frequency = THETA ** (-(jnp.arange(head_size // 2, dtype=jnp.float32) * 2.0 / head_size))
    angle = position[:, None] * frequency[None, :]
    return (jnp.cos(angle)[:, None, :], jnp.sin(angle)[:, None, :])

def rotate(values, cosine_table, sine_table):
    front_half, back_half = jnp.split(values, 2, axis=-1)
    return jnp.concatenate([front_half * cosine_table - back_half * sine_table, back_half * cosine_table + front_half * sine_table], axis=-1)

def permitted(pieces, documents):
    position = jnp.arange(pieces.shape[-1], dtype=jnp.int32)
    causal = position[:, None] >= position[None, :]
    same_doc = documents[:, :, None] == documents[:, None, :]
    picture = (pieces[:, :, None] == pieces[:, None, :]) & (pieces[:, :, None] > 0)
    return same_doc & (causal[None, :, :] | picture)

def route_slots(routes):
    row_count = routes.shape[0]
    blocks = routes.reshape(row_count, N_EP, TOK_DEV, TOP).transpose(1, 0, 2, 3).reshape(N_EP, row_count * TOK_DEV * TOP)
    one_hot = (blocks[:, :, None] == jnp.arange(EXPERTS, dtype=jnp.int32)[None, None, :]).astype(jnp.int32)
    pair_rank = lax.optimization_barrier(jnp.sum((jnp.cumsum(one_hot, axis=1) - one_hot) * one_hot, axis=2))
    source = jnp.arange(N_EP, dtype=jnp.int32)[:, None]
    keep_mask = pair_rank < CAP
    slot_index = jnp.where(keep_mask, blocks * (N_EP * CAP) + source * CAP + pair_rank, EXPERTS * N_EP * CAP).astype(jnp.int32)
    slot_index = slot_index.reshape(N_EP, row_count, TOK_DEV, TOP).transpose(1, 0, 2, 3).reshape(row_count * SEQUENCE_TOKENS, TOP)
    keep_mask = keep_mask.reshape(N_EP, row_count, TOK_DEV, TOP).transpose(1, 0, 2, 3).reshape(row_count * SEQUENCE_TOKENS, TOP)
    return (slot_index, keep_mask)

def forward(inputs, weights, routes, pieces, documents):
    attn_norm, query_weight, key_weight, value_weight, query_bias, key_bias, value_bias, out_weight, ffn_norm, router_weight, shared_switch, shared_gate, shared_up, shared_down, expert_gate, expert_up, expert_down = weights
    row_count = inputs.shape[0]
    all_count = row_count * SEQUENCE_TOKENS
    flat = inputs.reshape(all_count, MODEL_DIM)
    h_one = low(normed(flat) * attn_norm)
    cosine_table, sine_table = rotary_tables(SEQUENCE_TOKENS, HEAD)
    q_pre = low_back(matmul(h_one, query_weight) + query_bias.reshape(-1))
    k_pre = low_back(matmul(h_one, key_weight) + key_bias.reshape(-1))
    v_pre = low_back(matmul(h_one, value_weight) + value_bias.reshape(-1))
    q_rot = low(rotate(q_pre.reshape(row_count, SEQUENCE_TOKENS, HEADS, HEAD), cosine_table, sine_table))
    k_rot = low(rotate(k_pre.reshape(row_count, SEQUENCE_TOKENS, HEADS, HEAD), cosine_table, sine_table))
    v_val = low(v_pre.reshape(row_count, SEQUENCE_TOKENS, HEADS, HEAD))
    scores = low_back(jnp.einsum('rqhd,rkhd->rhqk', q_rot, k_rot, precision=HIGH) * (1.0 / math.sqrt(HEAD)))
    scores = jnp.where(permitted(pieces, documents)[:, None, :, :], scores, NEG)
    exponent = jnp.exp(scores - lax.optimization_barrier(jnp.max(scores, axis=-1, keepdims=True)))
    weights_low = low(exponent / lax.optimization_barrier(jnp.sum(exponent, axis=-1, keepdims=True)))
    o_pre = low_back(jnp.einsum('rhqk,rkhd->rqhd', weights_low, v_val, precision=HIGH))
    o_low = low(o_pre).reshape(all_count, MODEL_DIM)
    x_one = flat + low_back(matmul(o_low, out_weight))
    h_two = low(normed(x_one) * ffn_norm)
    route_probs = jax.nn.softmax(low_back(matmul(h_two, router_weight)), axis=-1)
    gate_pre = low_back(matmul(h_two, shared_gate))
    up_pre = low_back(matmul(h_two, shared_up))
    s_hidden = low(jax.nn.silu(gate_pre) * up_pre)
    s_out = low_back(matmul(s_hidden, shared_down))
    switch = jax.nn.sigmoid(low_back(matmul(h_two, shared_switch)))
    slot_index, keep_mask = route_slots(routes)
    slot_total = EXPERTS * N_EP * CAP
    owners = jnp.broadcast_to(jnp.arange(all_count, dtype=jnp.int32)[:, None], (all_count, TOP))
    table = jnp.full((slot_total + 1,), all_count, dtype=jnp.int32).at[slot_index.reshape(-1)].set(owners.reshape(-1))[:slot_total]
    h_pad = jnp.concatenate([h_two, jnp.zeros((1, MODEL_DIM), h_two.dtype)], axis=0)
    sent = low_back(h_pad[table]).reshape(EXPERTS, N_EP * CAP, MODEL_DIM)
    e_gate = low_back(jnp.einsum('erd,edf->erf', sent, expert_gate, precision=HIGH))
    e_up = low_back(jnp.einsum('erd,edf->erf', sent, expert_up, precision=HIGH))
    e_hidden = low(jax.nn.silu(e_gate) * e_up)
    e_out = low(low_back(jnp.einsum('erf,efd->erd', e_hidden, expert_down, precision=HIGH))).reshape(slot_total, MODEL_DIM)
    out_pad = jnp.concatenate([e_out, jnp.zeros((1, MODEL_DIM), e_out.dtype)], axis=0)
    picked = out_pad[slot_index]
    chosen = routes.reshape(all_count, TOP)
    gate_value = jnp.take_along_axis(route_probs, chosen, axis=1) * keep_mask.astype(route_probs.dtype)
    mixture = lax.optimization_barrier(jnp.sum(gate_value[:, :, None] * picked, axis=1))
    result = x_one + mixture + switch[:, None] * s_out
    return result.reshape(row_count, SEQUENCE_TOKENS, MODEL_DIM)

def reference(tokens, attn_norm, query_weight, key_weight, value_weight, query_bias, key_bias, value_bias, out_weight, ffn_norm, router_weight, shared_switch, shared_gate, shared_up, shared_down, expert_gate, expert_up, expert_down, routes, pieces, documents, cotangent):
    weights = tuple((member.astype(jnp.float32) for member in (attn_norm, query_weight, key_weight, value_weight, query_bias, key_bias, value_bias, out_weight, ffn_norm, router_weight, shared_switch, shared_gate, shared_up, shared_down, expert_gate, expert_up, expert_down)))
    inputs = tokens.astype(jnp.float32).reshape(N_GRP, ROWS, SEQUENCE_TOKENS, MODEL_DIM)
    upstream = cotangent.astype(jnp.float32).reshape(N_GRP, ROWS, SEQUENCE_TOKENS, MODEL_DIM)
    route_groups = routes.reshape(N_GRP, ROWS, SEQUENCE_TOKENS, TOP)
    piece_groups = pieces.reshape(N_GRP, ROWS, SEQUENCE_TOKENS)
    doc_groups = documents.reshape(N_GRP, ROWS, SEQUENCE_TOKENS)

    def group_step(running, group_item):
        group_in, group_up, group_routes, group_pieces, group_docs = group_item

        def apply_layer(group_x, *params):
            return forward(group_x, params, group_routes, group_pieces, group_docs)
        outcome, pullback = jax.vjp(apply_layer, group_in, *weights)
        grad_list = pullback(group_up)
        running = tuple((run_total + new_grad for run_total, new_grad in zip(running, grad_list[1:])))
        return (running, (outcome.astype(jnp.bfloat16), grad_list[0]))
    zero_grads = tuple((jnp.zeros_like(member) for member in weights))
    gradient_totals, (layer_results, input_gradients) = lax.scan(group_step, zero_grads, (inputs, upstream, route_groups, piece_groups, doc_groups))
    attention_norm_gradient, query_weight_gradient, key_weight_gradient, value_weight_gradient, query_bias_gradient, key_bias_gradient, value_bias_gradient, output_weight_gradient, feedforward_norm_gradient, router_weight_gradient, switch_weight_gradient, shared_gate_gradient, shared_up_gradient, shared_down_gradient, expert_gate_gradient, expert_up_gradient, expert_down_gradient = gradient_totals
    return (layer_results.reshape(SEQUENCE_COUNT, SEQUENCE_TOKENS, MODEL_DIM), input_gradients.reshape(SEQUENCE_COUNT, SEQUENCE_TOKENS, MODEL_DIM), attention_norm_gradient, query_weight_gradient, key_weight_gradient, value_weight_gradient, query_bias_gradient, key_bias_gradient, value_bias_gradient, output_weight_gradient, feedforward_norm_gradient, router_weight_gradient, switch_weight_gradient, shared_gate_gradient, shared_up_gradient, shared_down_gradient, expert_gate_gradient, expert_up_gradient, expert_down_gradient)
```

```python
import math

import jax
import jax.numpy as jnp
from jax import lax
from jax.experimental import pallas as pl
from jax.experimental.pallas import tpu as pltpu
from jax.sharding import PartitionSpec as P

EPS = 1e-06
THETA = 1000000.0
NEG = -1e30
QUERY_ROWS = 512
F32 = jnp.float32
BF16 = jnp.bfloat16


def inverse_rms(values):
    return lax.rsqrt(jnp.mean(values * values, axis=-1, keepdims=True) + EPS)


def norm_back(values, gain_vec, upstream):
    inverse = inverse_rms(values)
    scaled = values * inverse
    weighted = upstream * gain_vec
    return inverse * (weighted - scaled * jnp.mean(weighted * scaled, axis=-1, keepdims=True))


def rotary_tables(position, head_size):
    frequency = THETA ** (-(jnp.arange(head_size // 2, dtype=F32) * 2.0 / head_size))
    angle = position.astype(F32)[:, None] * frequency[None, :]
    return (jnp.cos(angle)[:, None, :], jnp.sin(angle)[:, None, :])


def rotate(values, cosine_table, sine_table):
    front_half, back_half = jnp.split(values, 2, axis=-1)
    return jnp.concatenate(
        [
            front_half * cosine_table - back_half * sine_table,
            back_half * cosine_table + front_half * sine_table,
        ],
        axis=-1,
    )


def unrotate(values, cosine_table, sine_table):
    front_half, back_half = jnp.split(values, 2, axis=-1)
    return jnp.concatenate(
        [
            front_half * cosine_table + back_half * sine_table,
            back_half * cosine_table - front_half * sine_table,
        ],
        axis=-1,
    )


def inner_rows(left_side, right_side):
    return lax.dot_general(
        left_side, right_side, (((0,), (0,)), ((), ())), preferred_element_type=F32
    )


def times_trans(left_side, right_side):
    return lax.dot_general(
        left_side, right_side, (((1,), (1,)), ((), ())), preferred_element_type=F32
    )


def times(left_side, right_side):
    return jnp.dot(left_side, right_side, preferred_element_type=F32)


def ring_gather(own_block, axis):
    count = lax.axis_size(axis)
    pairs = [(j, (j + 1) % count) for j in range(count)]
    blocks = [own_block]
    for _ in range(count - 1):
        blocks.append(lax.ppermute(blocks[-1], axis, pairs))
    return blocks


def ring_reduce(part_of, axis):
    count = lax.axis_size(axis)
    pairs = [(j, (j + 1) % count) for j in range(count)]
    running = part_of(1 % count).astype(BF16)
    for step in range(1, count):
        arrived = lax.ppermute(running, axis, pairs)
        running = arrived.astype(F32) + part_of((step + 1) % count)
        if step < count - 1:
            running = running.astype(BF16)
    return running


def select_kernel(rank_ref, data_ref, out_ref):
    slots = out_ref.shape[2]
    tokens = data_ref.shape[1]
    slot = lax.broadcasted_iota(jnp.int32, (slots, tokens), 0)
    hot = jnp.where(slot == rank_ref[0], 1.0, 0.0).astype(BF16)
    out_ref[0, 0] = jnp.dot(hot, data_ref[0], preferred_element_type=F32).astype(BF16)


def select_rows(rank, data, slots):
    experts, blocks, tokens = rank.shape
    width = data.shape[-1]
    return pl.pallas_call(
        select_kernel,
        grid=(blocks, experts),
        in_specs=[
            pl.BlockSpec((1, 1, tokens), lambda s, e: (e * blocks + s, 0, 0)),
            pl.BlockSpec((1, tokens, width), lambda s, e: (s, 0, 0)),
        ],
        out_specs=pl.BlockSpec((1, 1, slots, width), lambda s, e: (e, s, 0, 0)),
        out_shape=jax.ShapeDtypeStruct((experts, blocks, slots, width), BF16),
        cost_estimate=pl.CostEstimate(
            flops=2 * experts * blocks * slots * tokens * width,
            bytes_accessed=2 * (experts * blocks * slots + blocks * tokens) * width,
            transcendentals=0,
        ),
        name="select_rows",
    )(rank.reshape(experts * blocks, 1, tokens), data.reshape(blocks, tokens, width))


def spread_kernel(rank_ref, rows_ref, out_ref):
    experts, _, slots, _ = rows_ref.shape
    tokens = out_ref.shape[1]
    slot = lax.broadcasted_iota(jnp.int32, (tokens, slots), 1)
    total = None
    for e in range(experts):
        hot = jnp.where(slot == rank_ref[e, 0], 1.0, 0.0).astype(BF16)
        part = jnp.dot(hot, rows_ref[e, 0], preferred_element_type=F32)
        total = part if total is None else total + part
    out_ref[0] = total


def spread_rows(rank, rows):
    experts, blocks, tokens = rank.shape
    slots, width = rows.shape[2:]
    return pl.pallas_call(
        spread_kernel,
        grid=(blocks,),
        in_specs=[
            pl.BlockSpec((experts, 1, tokens, 1), lambda s: (0, s, 0, 0)),
            pl.BlockSpec((experts, 1, slots, width), lambda s: (0, s, 0, 0)),
        ],
        out_specs=pl.BlockSpec((1, tokens, width), lambda s: (s, 0, 0)),
        out_shape=jax.ShapeDtypeStruct((blocks, tokens, width), F32),
        cost_estimate=pl.CostEstimate(
            flops=2 * experts * blocks * slots * tokens * width,
            bytes_accessed=(2 * experts * blocks * slots + 4 * blocks * tokens) * width,
            transcendentals=0,
        ),
        name="spread_rows",
    )(rank.reshape(experts, blocks, tokens, 1), rows)


def attend(queries, keys, values, allowed, score_scale):
    length = queries.shape[0]
    block_rows = math.gcd(length, QUERY_ROWS)
    outputs = []
    log_totals = []
    for block_start in range(0, length, block_rows):
        finish = block_start + block_rows
        query_part = queries[block_start:finish]
        scores = (
            jnp.einsum("qhd,khd->hqk", query_part, keys, preferred_element_type=F32) * score_scale
        )
        scores = jnp.where(allowed[None, block_start:finish, :], scores, NEG)
        highest = jnp.max(scores, axis=-1, keepdims=True)
        exponent = jnp.exp(scores - highest)
        denominator = jnp.sum(exponent, axis=-1, keepdims=True)
        weights_low = (exponent / denominator).astype(BF16)
        outputs.append(jnp.einsum("hqk,khd->qhd", weights_low, values, preferred_element_type=F32))
        log_totals.append(highest + jnp.log(denominator))
    return (jnp.concatenate(outputs, axis=0), jnp.concatenate(log_totals, axis=1))


def attend_back(queries, keys, values, allowed, score_scale, log_total, grad_out):
    length = queries.shape[0]
    block_rows = math.gcd(length, QUERY_ROWS)
    grad_queries = []
    grad_keys = jnp.zeros(keys.shape, F32)
    grad_values = jnp.zeros(values.shape, F32)
    for block_start in range(0, length, block_rows):
        finish = block_start + block_rows
        query_part = queries[block_start:finish]
        grad_part = grad_out[block_start:finish]
        scores = (
            jnp.einsum("qhd,khd->hqk", query_part, keys, preferred_element_type=F32) * score_scale
        )
        probs = jnp.where(
            allowed[None, block_start:finish, :],
            jnp.exp(scores - log_total[:, block_start:finish]),
            0.0,
        )
        grad_probs = jnp.einsum("qhd,khd->hqk", grad_part, values, preferred_element_type=F32)
        centre = jnp.sum(probs * grad_probs, axis=-1, keepdims=True)
        grad_scores = (probs * (grad_probs - centre)).astype(BF16)
        grad_queries.append(
            jnp.einsum("hqk,khd->qhd", grad_scores, keys, preferred_element_type=F32) * score_scale
        )
        grad_keys = (
            grad_keys
            + jnp.einsum("hqk,qhd->khd", grad_scores, query_part, preferred_element_type=F32)
            * score_scale
        )
        grad_values = grad_values + jnp.einsum(
            "hqk,qhd->khd", probs.astype(BF16), grad_part, preferred_element_type=F32
        )
    return (jnp.concatenate(grad_queries, axis=0), grad_keys, grad_values)


def scatter_sum(values, dimension):
    return lax.psum_scatter(
        values.astype(BF16), "grp", scatter_dimension=dimension, tiled=True
    ).astype(F32)


def per_device(
    tokens,
    attn_norm,
    query_weight,
    key_weight,
    value_weight,
    query_bias,
    key_bias,
    value_bias,
    out_weight,
    ffn_norm,
    router_weight,
    shared_switch,
    shared_gate,
    shared_up,
    shared_down,
    expert_gate,
    expert_up,
    expert_down,
    routes,
    pieces,
    documents,
    cotangent,
):
    ep_count = lax.axis_size("ep")
    grp_count = lax.axis_size("grp")
    place = lax.axis_index("ep")
    row_count, own_count, model_width = tokens.shape
    length = own_count * ep_count
    heads_here = query_bias.shape[0]
    head_size = query_bias.shape[1] * grp_count
    head_width = heads_here * head_size
    hidden_width = shared_gate.shape[1]
    experts_here = expert_gate.shape[0]
    experts_all = experts_here * ep_count
    top_count = routes.shape[2]
    capacity = (own_count * top_count // experts_all * 5 + 3) // 4
    order = (place - jnp.arange(ep_count, dtype=jnp.int32)) % ep_count

    w_qkv = lax.all_gather(
        jnp.concatenate([query_weight, key_weight, value_weight], axis=1),
        "grp",
        axis=0,
        tiled=True,
    )
    small_sizes = [
        attn_norm.size,
        query_bias.size,
        key_bias.size,
        value_bias.size,
        ffn_norm.size,
        router_weight.size,
        shared_switch.size,
    ]
    small = lax.all_gather(
        jnp.concatenate(
            [
                part.reshape(-1)
                for part in (
                    attn_norm,
                    query_bias,
                    key_bias,
                    value_bias,
                    ffn_norm,
                    router_weight,
                    shared_switch,
                )
            ]
        ),
        "grp",
        axis=0,
    )
    pieces_of_small = []
    begin = 0
    for size in small_sizes:
        pieces_of_small.append(small[:, begin : begin + size])
        begin += size
    gain_first = pieces_of_small[0].reshape(-1).astype(F32)
    biases = [
        part.reshape(grp_count, heads_here, -1).transpose(1, 0, 2).reshape(-1)
        for part in pieces_of_small[1:4]
    ]
    bias_qkv = jnp.concatenate(biases).astype(F32)
    gain_second = pieces_of_small[4].reshape(-1).astype(F32)
    w_router = pieces_of_small[5].reshape(model_width, experts_all)
    w_switch = pieces_of_small[6].reshape(model_width)
    w_out = lax.all_gather(out_weight, "grp", axis=1, tiled=True)
    w_sgu = lax.all_gather(
        jnp.concatenate([shared_gate, shared_up], axis=1), "grp", axis=0, tiled=True
    )
    w_sdown = lax.all_gather(shared_down, "grp", axis=1, tiled=True)

    tokens_own = tokens.reshape(own_count, model_width)
    x_blocks = ring_gather(tokens_own, "ep")
    h_parts = []
    for block in x_blocks:
        wide = block.astype(F32)
        h_parts.append((wide * inverse_rms(wide) * gain_first).astype(BF16))
    h_one = jnp.concatenate(h_parts, axis=0)
    own_places = jnp.arange(own_count, dtype=jnp.int32)
    position = (order[:, None] * own_count + own_places[None, :]).reshape(length)
    piece = jnp.take(pieces.reshape(ep_count, own_count), order, axis=0).reshape(length)
    document = jnp.take(documents.reshape(ep_count, own_count), order, axis=0).reshape(length)
    allowed = (document[:, None] == document[None, :]) & (
        (position[:, None] >= position[None, :])
        | ((piece[:, None] == piece[None, :]) & (piece[:, None] > 0))
    )
    cosine_table, sine_table = rotary_tables(position, head_size)
    qkv_pre = times(h_one, w_qkv) + bias_qkv
    head_shape = (length, heads_here, head_size)
    q_rot = rotate(qkv_pre[:, :head_width].reshape(head_shape), cosine_table, sine_table).astype(
        BF16
    )
    k_rot = rotate(
        qkv_pre[:, head_width : 2 * head_width].reshape(head_shape), cosine_table, sine_table
    ).astype(BF16)
    v_val = qkv_pre[:, 2 * head_width :].reshape(head_shape).astype(BF16)
    score_scale = 1.0 / math.sqrt(head_size)
    o_pre, log_total = attend(q_rot, k_rot, v_val, allowed, score_scale)
    o_low = o_pre.reshape(length, head_width).astype(BF16)

    def block_of(values, k):
        return values[k * own_count : (k + 1) * own_count]

    attn_own = ring_reduce(lambda k: times(block_of(o_low, k), w_out), "ep")
    x_own = tokens_own.astype(F32)
    x1_own = x_own + attn_own
    inverse_two = inverse_rms(x1_own)
    hat_two = x1_own * inverse_two
    h_own = (hat_two * gain_second).astype(BF16)
    h_two = jnp.concatenate(ring_gather(h_own, "ep"), axis=0)
    grad_own_low = cotangent.reshape(own_count, model_width)
    grad_low = jnp.concatenate(ring_gather(grad_own_low, "ep"), axis=0)
    grad_all = grad_low.astype(F32)

    logits = times(h_two, jnp.concatenate([w_router, w_switch[:, None]], axis=1))
    route_probs = jax.nn.softmax(logits[:, :experts_all], axis=-1)
    switch = jax.nn.sigmoid(logits[:, experts_all])
    chosen = jnp.take(
        lax.all_gather(routes.reshape(own_count, top_count), "ep", axis=0), order, axis=0
    )
    expert_ids = place * experts_here + jnp.arange(experts_here, dtype=jnp.int32)
    named = jnp.any(chosen[None] == expert_ids[:, None, None, None], axis=-1)
    before = (own_places[:, None] < own_places[None, :]).astype(BF16)
    rank = jnp.einsum("est,tu->esu", named.astype(BF16), before, preferred_element_type=F32).astype(
        jnp.int32
    )
    rank = jnp.where(named & (rank < capacity), rank, -1)
    local_probs = lax.dynamic_slice_in_dim(route_probs, place * experts_here, experts_here, 1)
    local_probs = local_probs.reshape(ep_count, own_count, experts_here).transpose(2, 0, 1)
    hot = (
        rank[:, :, None, :] == jnp.arange(capacity, dtype=jnp.int32)[None, None, :, None]
    )
    gate_slot = jnp.sum(jnp.where(hot, local_probs[:, :, None, :], 0.0), axis=-1)
    slot_shape = (experts_here, ep_count * capacity, model_width)
    gate_rows = gate_slot.reshape(experts_here, ep_count * capacity, 1)

    s_pre = times(h_two, w_sgu)
    s_gate = s_pre[:, :hidden_width]
    s_up = s_pre[:, hidden_width:]
    sig_shared = jax.nn.sigmoid(s_gate)
    silu_shared = s_gate * sig_shared
    s_hidden = (silu_shared * s_up).astype(BF16)
    s_part = times(s_hidden, w_sdown)
    grad_sout = (switch[:, None] * grad_all).astype(BF16)
    grad_shidden = times_trans(grad_sout, w_sdown)
    slope_shared = sig_shared * (1.0 + s_gate * (1.0 - sig_shared))
    grad_s = jnp.concatenate(
        [
            (grad_shidden * s_up * slope_shared).astype(BF16),
            (grad_shidden * silu_shared).astype(BF16),
        ],
        axis=1,
    )
    sum_sdown = scatter_sum(inner_rows(s_hidden, grad_sout), 1)
    sum_sgu = scatter_sum(inner_rows(h_two, grad_s), 0)

    flat_rows = select_rows(rank, h_two, capacity).reshape(slot_shape)
    grad_rows = select_rows(rank, grad_low, capacity).reshape(slot_shape)
    gate_pre = jnp.einsum("erd,edf->erf", flat_rows, expert_gate, preferred_element_type=F32)
    up_pre = jnp.einsum("erd,edf->erf", flat_rows, expert_up, preferred_element_type=F32)
    sig_expert = jax.nn.sigmoid(gate_pre)
    silu_gate = gate_pre * sig_expert
    hidden = (silu_gate * up_pre).astype(BF16)
    result = jnp.einsum("erf,efd->erd", hidden, expert_down, preferred_element_type=F32).astype(
        BF16
    )
    result_wide = result.astype(F32)
    grad_wide = grad_rows.astype(F32)
    grad_gate = jnp.sum(grad_wide * result_wide, axis=-1)
    mixture = spread_rows(
        rank,
        (gate_rows * result_wide)
        .astype(BF16)
        .reshape(experts_here, ep_count, capacity, model_width),
    ).reshape(length, model_width)
    arrived = (gate_rows * grad_wide).astype(BF16)
    grad_hidden = jnp.einsum("erd,efd->erf", arrived, expert_down, preferred_element_type=F32)
    slope_expert = sig_expert * (1.0 + gate_pre * (1.0 - sig_expert))
    grad_gate_pre = (grad_hidden * up_pre * slope_expert).astype(BF16)
    grad_up_pre = (grad_hidden * silu_gate).astype(BF16)
    grad_inputs = (
        jnp.einsum("erf,edf->erd", grad_gate_pre, expert_gate, preferred_element_type=F32)
        + jnp.einsum("erf,edf->erd", grad_up_pre, expert_up, preferred_element_type=F32)
    ).astype(BF16)
    grad_moe = spread_rows(
        rank, grad_inputs.reshape(experts_here, ep_count, capacity, model_width)
    ).reshape(length, model_width)
    sum_edown = scatter_sum(
        jnp.einsum("erf,erd->efd", hidden, arrived, preferred_element_type=F32), 2
    )
    sum_egate = scatter_sum(
        jnp.einsum("erd,erf->edf", flat_rows, grad_gate_pre, preferred_element_type=F32), 1
    )
    sum_eup = scatter_sum(
        jnp.einsum("erd,erf->edf", flat_rows, grad_up_pre, preferred_element_type=F32), 1
    )

    y_part = switch[:, None] * s_part + mixture
    layer_own = x1_own + ring_reduce(lambda k: block_of(y_part, k), "ep")
    layer_out = layer_own.reshape(row_count, own_count, model_width).astype(BF16)

    shared_dot = jnp.sum(grad_all * s_part, axis=-1).reshape(1, ep_count, own_count)
    grad_probs_part = jnp.sum(
        jnp.where(
            hot, grad_gate.reshape(experts_here, ep_count, capacity)[:, :, :, None], 0.0
        ),
        axis=2,
    )
    scalars = jnp.concatenate([grad_probs_part, shared_dot], axis=0)
    home = [scalars[:, 0]]
    for k in range(1, ep_count):
        home.append(
            lax.ppermute(scalars[:, k], "ep", [(j, (j - k) % ep_count) for j in range(ep_count)])
        )
    home = jnp.stack(home)
    grad_probs = jnp.take(
        home[:, :experts_here],
        (jnp.arange(ep_count, dtype=jnp.int32) - place) % ep_count,
        axis=0,
    )
    grad_probs = grad_probs.reshape(experts_all, own_count).T
    probs_own = route_probs[:own_count]
    switch_own = switch[:own_count]
    grad_logit = (
        probs_own * (grad_probs - jnp.sum(probs_own * grad_probs, axis=-1, keepdims=True))
    ).astype(BF16)
    grad_switch = (
        jnp.sum(home[:, experts_here], axis=0) * switch_own * (1.0 - switch_own)
    ).astype(BF16)

    w_small = jnp.concatenate([w_router, w_switch[:, None]], axis=1)
    grad_small = jnp.concatenate([grad_logit, grad_switch[:, None]], axis=1)
    grad_h2 = ring_reduce(
        lambda k: times_trans(block_of(grad_s, k), w_sgu) + block_of(grad_moe, k), "ep"
    ) + times_trans(grad_small, w_small)
    weighted = grad_h2 * gain_second
    grad_x1 = grad_own_low.astype(F32) + inverse_two * (
        weighted - hat_two * jnp.mean(weighted * hat_two, axis=-1, keepdims=True)
    )
    grad_attn = jnp.concatenate(ring_gather(grad_x1.astype(BF16), "ep"), axis=0)
    gain_two_part = jnp.sum(grad_h2 * hat_two, axis=0)
    small_part = jnp.concatenate(
        [inner_rows(h_own, grad_small), gain_two_part[:, None]], axis=1
    )
    small_sum = lax.psum(lax.psum_scatter(small_part, "grp", scatter_dimension=0, tiled=True), "ep")

    sum_out = scatter_sum(inner_rows(o_low, grad_attn), 1)
    grad_o = times_trans(grad_attn, w_out).astype(BF16).reshape(head_shape)
    grad_q_rot, grad_k_rot, grad_v = attend_back(
        q_rot, k_rot, v_val, allowed, score_scale, log_total, grad_o
    )
    grad_qkv = jnp.concatenate(
        [
            unrotate(grad_q_rot, cosine_table, sine_table).astype(BF16).reshape(length, head_width),
            unrotate(grad_k_rot, cosine_table, sine_table).astype(BF16).reshape(length, head_width),
            grad_v.astype(BF16).reshape(length, head_width),
        ],
        axis=1,
    )
    sum_qkv = scatter_sum(inner_rows(h_one, grad_qkv), 0)
    bias_sum = jnp.sum(grad_qkv.astype(F32), axis=0).reshape(3 * heads_here, head_size)
    sum_bias = lax.psum_scatter(bias_sum, "grp", scatter_dimension=1, tiled=True)
    grad_h1 = ring_reduce(lambda k: times_trans(block_of(grad_qkv, k), w_qkv), "ep")
    grad_tokens = grad_x1 + norm_back(x_own, gain_first, grad_h1)
    tokens_grad = grad_tokens.reshape(row_count, own_count, model_width)
    w_own = jnp.concatenate([query_weight, key_weight, value_weight], axis=1).astype(F32)
    gain_one = lax.psum(jnp.sum(sum_qkv * w_own, axis=1) / attn_norm.astype(F32), "ep")

    return (
        layer_out,
        tokens_grad,
        gain_one,
        sum_qkv[:, :head_width],
        sum_qkv[:, head_width : 2 * head_width],
        sum_qkv[:, 2 * head_width :],
        sum_bias[:heads_here],
        sum_bias[heads_here : 2 * heads_here],
        sum_bias[2 * heads_here :],
        sum_out,
        small_sum[:, experts_all + 1],
        small_sum[:, :experts_all],
        small_sum[:, experts_all],
        sum_sgu[:, :hidden_width],
        sum_sgu[:, hidden_width:],
        sum_sdown,
        sum_egate,
        sum_eup,
        sum_edown,
    )


def solution(mesh):
    return jax.shard_map(
        per_device,
        mesh=mesh,
        in_specs=(
            P("grp", "ep", None),
            P("grp"),
            P("grp", "ep"),
            P("grp", "ep"),
            P("grp", "ep"),
            P("ep", "grp"),
            P("ep", "grp"),
            P("ep", "grp"),
            P("ep", "grp"),
            P("grp"),
            P("grp", None),
            P("grp"),
            P("grp", "ep"),
            P("grp", "ep"),
            P("ep", "grp"),
            P("ep", None, None),
            P("ep", None, None),
            P("ep", None, None),
            P("grp", "ep", None),
            P("grp", None),
            P("grp", None),
            P("grp", "ep", None),
        ),
        out_specs=(
            P("grp", "ep", None),
            P("grp", "ep", None),
            P("grp"),
            P("grp", "ep"),
            P("grp", "ep"),
            P("grp", "ep"),
            P("ep", "grp"),
            P("ep", "grp"),
            P("ep", "grp"),
            P("ep", "grp"),
            P("grp"),
            P("grp", None),
            P("grp"),
            P("grp", "ep"),
            P("grp", "ep"),
            P("ep", "grp"),
            P("ep", "grp", None),
            P("ep", "grp", None),
            P("ep", None, "grp"),
        ),
        check_vma=False,
    )
```

```python
import math

import jax
import jax.numpy as jnp
from jax import lax
from jax.experimental import pallas as pl
from jax.experimental.pallas import tpu as pltpu
from jax.sharding import PartitionSpec as P

EPS = 1e-06
THETA = 1000000.0
NEG = -1e30
LOG2E = 1.4426950408889634
F32 = jnp.float32
BF16 = jnp.bfloat16


def inverse_rms(values):
    return lax.rsqrt(jnp.mean(values * values, axis=-1, keepdims=True) + EPS)


def norm_back(values, gain_vec, upstream):
    inverse = inverse_rms(values)
    scaled = values * inverse
    weighted = upstream * gain_vec
    return inverse * (weighted - scaled * jnp.mean(weighted * scaled, axis=-1, keepdims=True))


def rotary_tables(position, head_size):
    frequency = THETA ** (-(jnp.arange(head_size // 2, dtype=F32) * 2.0 / head_size))
    angle = position.astype(F32)[:, None] * frequency[None, :]
    cosine, sine = jnp.cos(angle), jnp.sin(angle)
    return (
        jnp.concatenate([cosine, cosine], axis=1),
        jnp.concatenate([-sine, sine], axis=1),
    )


def after(values, *others):
    return lax.optimization_barrier((values, *others))[0]


def by_head(queries, keys, values, heads):
    rows = queries.shape[0]
    parts = [part.reshape(rows, heads, -1) for part in (queries, keys, values)]
    return jnp.concatenate(parts, axis=2).reshape(rows, -1)


def inner_rows(left_side, right_side):
    return lax.dot_general(
        left_side, right_side, (((0,), (0,)), ((), ())), preferred_element_type=F32
    )


def times_trans(left_side, right_side):
    return lax.dot_general(
        left_side, right_side, (((1,), (1,)), ((), ())), preferred_element_type=F32
    )


def times(left_side, right_side):
    return jnp.dot(left_side, right_side, preferred_element_type=F32)


def ring_gather(own_block, axis):
    count = lax.axis_size(axis)
    pairs = [(j, (j + 1) % count) for j in range(count)]
    blocks = [own_block]
    for _ in range(count - 1):
        blocks.append(lax.ppermute(blocks[-1], axis, pairs))
    return blocks


def ring_reduce(part_of, axis, first=None):
    count = lax.axis_size(axis)
    pairs = [(j, (j + 1) % count) for j in range(count)]
    running = part_of(1 % count).astype(BF16) if first is None else first
    for step in range(1, count):
        arrived = lax.ppermute(running, axis, pairs)
        part = lax.optimization_barrier(part_of((step + 1) % count))
        running = arrived.astype(F32) + part
        if step < count - 1:
            running = running.astype(BF16)
    return running


def bits_of(axis):
    return range(lax.axis_size(axis).bit_length() - 1)


def swap(values, axis, bit):
    count = lax.axis_size(axis)
    return lax.ppermute(values, axis, [(j, j ^ (1 << bit)) for j in range(count)])


def sum_all(values, axis):
    for bit in bits_of(axis):
        values = values + swap(values, axis, bit)
    return values


def gather_small(values, axis):
    count = lax.axis_size(axis)
    blocks = values[None, :]
    for bit in bits_of(axis):
        blocks = jnp.concatenate([blocks, swap(blocks, axis, bit)], axis=0)
    index = jnp.arange(count, dtype=jnp.int32)
    apart = index[:, None] ^ lax.axis_index(axis)
    return times((apart == index[None, :]).astype(values.dtype), blocks).astype(values.dtype)


def column_kernel(order_ref, *refs):
    out_ref = refs[-1]
    begin = 0
    for data_ref in refs[:-1]:
        out_ref[begin : begin + data_ref.shape[0], :] = data_ref[...]
        begin += data_ref.shape[0]


def column_chunks(blocks, order):
    rows = sum(block.shape[0] for block in blocks)
    count = order.shape[0]
    chunk = blocks[0].shape[1] // count
    return pl.pallas_call(
        column_kernel,
        grid_spec=pltpu.PrefetchScalarGridSpec(
            num_scalar_prefetch=1,
            grid=(count,),
            in_specs=[
                pl.BlockSpec((block.shape[0], chunk), lambda r, order_ref: (0, order_ref[r]))
                for block in blocks
            ],
            out_specs=pl.BlockSpec((rows, chunk), lambda r, order_ref: (0, r)),
        ),
        out_shape=jax.ShapeDtypeStruct((rows, count * chunk), blocks[0].dtype),
        cost_estimate=pl.CostEstimate(
            flops=0, bytes_accessed=4 * rows * count * chunk, transcendentals=0
        ),
        name="column_chunks",
    )(order, *blocks)


def away_and_near(blocks, axis):
    count = lax.axis_size(axis)
    index = jnp.arange(count, dtype=jnp.int32).reshape(count // 2, 2)
    order = lax.axis_index(axis) ^ jnp.concatenate([index[:, 1], index[:, 0]])
    return column_chunks(blocks, order)


def halving_sum(part_of, columns, axis, dimension, parts):
    half = columns.shape[1] // 2
    away, near = columns[:, :half], columns[:, half:]
    count = lax.axis_size(axis)
    results = []
    for p in range(parts):
        arrived = swap(part_of(away, p).astype(BF16), axis, 0)
        near_sum = part_of(near, p) + arrived.astype(F32)
        steps = list(bits_of(axis))[1:]
        if p % 2:
            steps.reverse()
        held = dict(zip(range(0, count, 2), jnp.split(near_sum, count // 2, axis=dimension)))
        for bit in steps:
            leaving = [r for r in held if r >> bit & 1]
            staying = [r for r in held if not r >> bit & 1]
            sent = jnp.concatenate([held[r].astype(BF16) for r in leaving], axis=dimension)
            come = jnp.split(swap(sent, axis, bit), len(leaving), axis=dimension)
            for r, block in zip(leaving, come):
                held[r ^ (1 << bit)] = (
                    held[r ^ (1 << bit)].astype(BF16).astype(F32) + block.astype(F32)
                )
            held = {r: held[r] for r in staying}
        results.append(held[0])
    return results


def select_kernel(rank_ref, data_ref, out_ref):
    slots = out_ref.shape[2]
    tokens = data_ref.shape[1]
    slot = lax.broadcasted_iota(jnp.int32, (slots, tokens), 0)
    hot = jnp.where(slot == rank_ref[0], 1.0, 0.0).astype(BF16)
    out_ref[0, 0] = jnp.dot(hot, data_ref[0], preferred_element_type=F32).astype(BF16)


def select_rows(rank, data, slots):
    experts, blocks, tokens = rank.shape
    width = data.shape[-1]
    return pl.pallas_call(
        select_kernel,
        grid=(blocks, experts),
        in_specs=[
            pl.BlockSpec((1, 1, tokens), lambda s, e: (e * blocks + s, 0, 0)),
            pl.BlockSpec((1, tokens, width), lambda s, e: (s, 0, 0)),
        ],
        out_specs=pl.BlockSpec((1, 1, slots, width), lambda s, e: (e, s, 0, 0)),
        out_shape=jax.ShapeDtypeStruct((experts, blocks, slots, width), BF16),
        cost_estimate=pl.CostEstimate(
            flops=2 * experts * blocks * slots * tokens * width,
            bytes_accessed=2 * (experts * blocks * slots + blocks * tokens) * width,
            transcendentals=0,
        ),
        name="select_rows",
    )(rank.reshape(experts * blocks, 1, tokens), data.reshape(blocks, tokens, width))


def spread_kernel(rank_ref, weight_ref, rows_ref, out_ref):
    experts, _, slots, _ = rows_ref.shape
    tokens = out_ref.shape[1]
    slot = lax.broadcasted_iota(jnp.int32, (tokens, slots), 1)
    total = None
    for e in range(experts):
        hot = jnp.where(slot == rank_ref[e, 0], weight_ref[e, 0], 0.0).astype(BF16)
        part = jnp.dot(hot, rows_ref[e, 0], preferred_element_type=F32)
        total = part if total is None else total + part
    out_ref[0] = total


def spread_rows(rank, weight, rows):
    experts, blocks, tokens = rank.shape
    slots, width = rows.shape[2:]
    return pl.pallas_call(
        spread_kernel,
        grid=(blocks,),
        in_specs=[
            pl.BlockSpec((experts, 1, tokens, 1), lambda s: (0, s, 0, 0)),
            pl.BlockSpec((experts, 1, tokens, 1), lambda s: (0, s, 0, 0)),
            pl.BlockSpec((experts, 1, slots, width), lambda s: (0, s, 0, 0)),
        ],
        out_specs=pl.BlockSpec((1, tokens, width), lambda s: (s, 0, 0)),
        out_shape=jax.ShapeDtypeStruct((blocks, tokens, width), F32),
        cost_estimate=pl.CostEstimate(
            flops=2 * experts * blocks * slots * tokens * width,
            bytes_accessed=(2 * experts * blocks * slots + 4 * blocks * tokens) * width,
            transcendentals=0,
        ),
        name="spread_rows",
    )(rank.reshape(experts, blocks, tokens, 1), weight.reshape(experts, blocks, tokens, 1), rows)


def project_kernel(rows_ref, weight_ref, bias_ref, cosine_ref, sine_ref, held_ref, out_ref):
    head_size = cosine_ref.shape[1]
    sums = (
        jnp.dot(rows_ref[...], weight_ref[...], preferred_element_type=F32) + bias_ref[0:1, :]
    )
    for part in range(3):
        values = sums[:, part * head_size : (part + 1) * head_size]
        if part < 2:
            turned = pltpu.roll(values, head_size // 2, 1)
            values = values * cosine_ref[...] + turned * sine_ref[...]
        out_ref[:, part * head_size : (part + 1) * head_size] = values.astype(BF16)


def project(rows, weight, bias, cosine, sine, held, k):
    count, width = rows.shape
    head_size = cosine.shape[1]
    columns = 3 * head_size
    total = weight.shape[1]
    return pl.pallas_call(
        project_kernel,
        grid=(total // columns,),
        in_specs=[
            pl.BlockSpec((count, width), lambda h: (0, 0)),
            pl.BlockSpec((width, columns), lambda h: (0, h)),
            pl.BlockSpec((8, columns), lambda h: (0, h)),
            pl.BlockSpec((count, head_size), lambda h: (k, 0)),
            pl.BlockSpec((count, head_size), lambda h: (k, 0)),
            pl.BlockSpec(memory_space=pl.ANY),
        ],
        out_specs=pl.BlockSpec((count, columns), lambda h: (k, h)),
        out_shape=jax.ShapeDtypeStruct(held.shape, BF16),
        input_output_aliases={5: 0},
        cost_estimate=pl.CostEstimate(
            flops=2 * count * width * total,
            bytes_accessed=2 * (count * width + width * total + count * total),
            transcendentals=0,
        ),
        name="project",
    )(rows, weight, bias, cosine, sine, held)


def attend_kernel(q_ref, k_ref, v_ref, mask_ref, out_ref, *, score_scale):
    scores = (
        lax.dot_general(
            q_ref[...], k_ref[...], (((1,), (1,)), ((), ())), preferred_element_type=F32
        )
        * (score_scale * LOG2E)
        + mask_ref[...]
    )
    exponent = jnp.exp2(scores - jnp.max(scores, axis=1, keepdims=True))
    weights = exponent * (1.0 / jnp.sum(exponent, axis=1, keepdims=True))
    out_ref[...] = jnp.dot(
        weights.astype(BF16), v_ref[...], preferred_element_type=F32
    ).astype(BF16)


def attend(qkv, mask, count, head_size, k):
    length, total = qkv.shape
    heads = total // (3 * head_size)
    return pl.pallas_call(
        lambda *refs: attend_kernel(*refs, score_scale=1.0 / math.sqrt(head_size)),
        grid=(heads,),
        in_specs=[
            pl.BlockSpec((count, head_size), lambda h: (k, 3 * h)),
            pl.BlockSpec((length, head_size), lambda h: (0, 3 * h + 1)),
            pl.BlockSpec((length, head_size), lambda h: (0, 3 * h + 2)),
            pl.BlockSpec((count, length), lambda h: (k, 0)),
        ],
        out_specs=pl.BlockSpec((count, head_size), lambda h: (0, h)),
        out_shape=jax.ShapeDtypeStruct((count, heads * head_size), BF16),
        cost_estimate=pl.CostEstimate(
            flops=4 * count * length * heads * head_size,
            bytes_accessed=4 * (count + length) * heads * head_size,
            transcendentals=heads * count * length,
        ),
        name="attend",
    )(qkv, qkv, qkv, mask)


def attend_back_kernel(
    q_ref, k_ref, v_ref, grad_ref, mask_ref, cosine_ref, sine_ref, out_ref, gk_ref, gv_ref,
    *, score_scale
):
    step = pl.program_id(1)
    count, head_size = q_ref.shape
    scores = (
        lax.dot_general(
            k_ref[...], q_ref[...], (((1,), (1,)), ((), ())), preferred_element_type=F32
        )
        * (score_scale * LOG2E)
        + mask_ref[...]
    )
    exponent = jnp.exp2(scores - jnp.max(scores, axis=0, keepdims=True))
    probs = exponent * (1.0 / jnp.sum(exponent, axis=0, keepdims=True))
    grad_probs = lax.dot_general(
        v_ref[...], grad_ref[...], (((1,), (1,)), ((), ())), preferred_element_type=F32
    )
    centre = jnp.sum(probs * grad_probs, axis=0, keepdims=True)
    grad_scores = (probs * (grad_probs - centre)).astype(BF16)
    grad_keys = jnp.dot(grad_scores, q_ref[...], preferred_element_type=F32)
    grad_values = jnp.dot(probs.astype(BF16), grad_ref[...], preferred_element_type=F32)

    @pl.when(step == 0)
    def _():
        gk_ref[...] = grad_keys
        gv_ref[...] = grad_values

    @pl.when(step > 0)
    def _():
        gk_ref[...] += grad_keys
        gv_ref[...] += grad_values

    def turn_back(values, place):
        turned = pltpu.roll(values, head_size // 2, 1)
        return (values * cosine_ref[place, :] - turned * sine_ref[place, :]).astype(BF16)

    grad_queries = (
        lax.dot_general(
            grad_scores, k_ref[...], (((0,), (0,)), ((), ())), preferred_element_type=F32
        )
        * score_scale
    )
    place = pl.ds(pl.multiple_of(step * count, count), count)
    out_ref[place, 0:head_size] = turn_back(grad_queries, place)

    @pl.when(step == pl.num_programs(1) - 1)
    def _():
        out_ref[:, head_size : 2 * head_size] = turn_back(gk_ref[...] * score_scale, slice(None))
        out_ref[:, 2 * head_size :] = gv_ref[...].astype(BF16)


def attend_back(qkv, grad_out, mask, cosine, sine, count):
    length, total = qkv.shape
    head_size = cosine.shape[1]
    heads = total // (3 * head_size)
    return pl.pallas_call(
        lambda *refs: attend_back_kernel(*refs, score_scale=1.0 / math.sqrt(head_size)),
        grid=(heads, length // count),
        in_specs=[
            pl.BlockSpec((count, head_size), lambda h, i: (i, 3 * h)),
            pl.BlockSpec((length, head_size), lambda h, i: (0, 3 * h + 1)),
            pl.BlockSpec((length, head_size), lambda h, i: (0, 3 * h + 2)),
            pl.BlockSpec((count, head_size), lambda h, i: (i, h)),
            pl.BlockSpec((length, count), lambda h, i: (0, i)),
            pl.BlockSpec((length, head_size), lambda h, i: (0, 0)),
            pl.BlockSpec((length, head_size), lambda h, i: (0, 0)),
        ],
        out_specs=pl.BlockSpec((length, 3 * head_size), lambda h, i: (0, h)),
        out_shape=jax.ShapeDtypeStruct((length, total), BF16),
        scratch_shapes=[
            pltpu.VMEM((length, head_size), F32),
            pltpu.VMEM((length, head_size), F32),
        ],
        cost_estimate=pl.CostEstimate(
            flops=10 * length * length * heads * head_size,
            bytes_accessed=14 * length * heads * head_size,
            transcendentals=heads * length * length,
        ),
        name="attend_back",
    )(qkv, qkv, qkv, grad_out, mask, cosine, sine)


def scatter_sum(values, dimension):
    return lax.psum_scatter(
        values.astype(BF16), "grp", scatter_dimension=dimension, tiled=True
    ).astype(F32)


def per_device(
    tokens,
    attn_norm,
    query_weight,
    key_weight,
    value_weight,
    query_bias,
    key_bias,
    value_bias,
    out_weight,
    ffn_norm,
    router_weight,
    shared_switch,
    shared_gate,
    shared_up,
    shared_down,
    expert_gate,
    expert_up,
    expert_down,
    routes,
    pieces,
    documents,
    cotangent,
):
    ep_count = lax.axis_size("ep")
    grp_count = lax.axis_size("grp")
    place = lax.axis_index("ep")
    row_count, own_count, model_width = tokens.shape
    length = own_count * ep_count
    heads_here = query_bias.shape[0]
    head_size = query_bias.shape[1] * grp_count
    head_width = heads_here * head_size
    hidden_width = shared_gate.shape[1]
    experts_here = expert_gate.shape[0]
    experts_all = experts_here * ep_count
    top_count = routes.shape[2]
    capacity = (own_count * top_count // experts_all * 5 + 3) // 4
    order = (place - jnp.arange(ep_count, dtype=jnp.int32)) % ep_count

    w_qkv = lax.all_gather(
        by_head(query_weight, key_weight, value_weight, heads_here),
        "grp",
        axis=0,
        tiled=True,
    )
    small_sizes = [
        attn_norm.size,
        query_bias.size,
        key_bias.size,
        value_bias.size,
        ffn_norm.size,
        router_weight.size,
        shared_switch.size,
    ]
    small = gather_small(
        jnp.concatenate(
            [
                part.reshape(-1)
                for part in (
                    attn_norm,
                    query_bias,
                    key_bias,
                    value_bias,
                    ffn_norm,
                    router_weight,
                    shared_switch,
                )
            ]
        ),
        "grp",
    )
    pieces_of_small = []
    begin = 0
    for size in small_sizes:
        pieces_of_small.append(small[:, begin : begin + size])
        begin += size
    gain_first = pieces_of_small[0].reshape(-1).astype(F32)
    biases = [
        part.reshape(grp_count, heads_here, -1).transpose(1, 0, 2).reshape(1, -1)
        for part in pieces_of_small[1:4]
    ]
    bias_qkv = jnp.broadcast_to(
        by_head(*biases, heads_here).astype(F32), (8, 3 * head_width)
    )
    gain_second = pieces_of_small[4].reshape(-1).astype(F32)
    w_router = pieces_of_small[5].reshape(model_width, experts_all)
    w_switch = pieces_of_small[6].reshape(model_width)
    w_out = lax.all_gather(out_weight, "grp", axis=1, tiled=True)
    w_sgu = lax.all_gather(
        jnp.concatenate([shared_gate, shared_up], axis=1), "grp", axis=0, tiled=True
    )
    w_sdown = lax.all_gather(shared_down, "grp", axis=1, tiled=True)

    tokens_own = tokens.reshape(own_count, model_width)
    grad_own_low = cotangent.reshape(own_count, model_width)
    x_blocks = ring_gather(tokens_own, "ep")
    own_places = jnp.arange(own_count, dtype=jnp.int32)
    position = (order[:, None] * own_count + own_places[None, :]).reshape(length)
    piece = jnp.take(pieces.reshape(ep_count, own_count), order, axis=0).reshape(length)
    document = jnp.take(documents.reshape(ep_count, own_count), order, axis=0).reshape(length)
    allowed = (document[:, None] == document[None, :]) & (
        (position[:, None] >= position[None, :])
        | ((piece[:, None] == piece[None, :]) & (piece[:, None] > 0))
    )
    allowed_by_key = (document[:, None] == document[None, :]) & (
        (position[:, None] <= position[None, :])
        | ((piece[:, None] == piece[None, :]) & (piece[:, None] > 0))
    )
    mask = jnp.where(allowed, 0.0, NEG)
    mask_by_key = jnp.where(allowed_by_key, 0.0, NEG)
    cosine_table, sine_table = rotary_tables(position, head_size)
    qkv = jnp.zeros((length, 3 * head_width), BF16)
    h_parts = []
    for k, block in enumerate(x_blocks):
        wide = after(block, qkv).astype(F32)
        h_parts.append((wide * inverse_rms(wide) * gain_first).astype(BF16))
        qkv = project(h_parts[k], w_qkv, bias_qkv, cosine_table, sine_table, qkv, k)
    chosen = jnp.stack(
        ring_gather(after(routes.reshape(own_count, top_count).T, x_blocks[-1]), "ep")
    )
    o_parts = [None] * ep_count
    ready = qkv
    for step in range(ep_count):
        k = (step + 1) % ep_count
        o_parts[k] = attend(ready, mask, own_count, head_size, k)
        ready, o_parts[k] = lax.optimization_barrier((ready, o_parts[k]))
    o_low = jnp.concatenate(o_parts, axis=0)

    def block_of(values, k):
        return values[k * own_count : (k + 1) * own_count]

    attn_own = ring_reduce(lambda k: times(o_parts[k], w_out), "ep")
    x_own = tokens_own.astype(F32)
    x1_own = x_own + attn_own
    inverse_two = inverse_rms(x1_own)
    hat_two = x1_own * inverse_two
    columns_h_one = away_and_near(h_parts, "grp")
    h_own, columns_h_one, mask_by_key, chosen = lax.optimization_barrier(
        ((hat_two * gain_second).astype(BF16), columns_h_one, mask_by_key, chosen)
    )
    h_blocks = ring_gather(h_own, "ep")
    h_two = jnp.concatenate(h_blocks, axis=0)
    logits = times(h_two, jnp.concatenate([w_router, w_switch[:, None]], axis=1))
    route_probs = jax.nn.softmax(logits[:, :experts_all], axis=-1)
    switch = jax.nn.sigmoid(logits[:, experts_all])
    expert_ids = place * experts_here + jnp.arange(experts_here, dtype=jnp.int32)
    named = jnp.any(chosen[None] == expert_ids[:, None, None, None], axis=2)
    before = (own_places[:, None] < own_places[None, :]).astype(BF16)
    rank = jnp.einsum("est,tu->esu", named.astype(BF16), before, preferred_element_type=F32).astype(
        jnp.int32
    )
    rank = jnp.where(named & (rank < capacity), rank, -1)
    local_probs = lax.dynamic_slice_in_dim(route_probs, place * experts_here, experts_here, 1)
    local_probs = local_probs.reshape(ep_count, own_count, experts_here).transpose(2, 0, 1)
    hot = (
        rank[:, :, None, :] == jnp.arange(capacity, dtype=jnp.int32)[None, None, :, None]
    )
    gate_slot = jnp.sum(jnp.where(hot, local_probs[:, :, None, :], 0.0), axis=-1)
    slot_shape = (experts_here, ep_count * capacity, model_width)
    gate_rows = gate_slot.reshape(experts_here, ep_count * capacity, 1)

    ring = [(j, (j + 1) % ep_count) for j in range(ep_count)]
    grad_blocks = [grad_own_low]
    s_pre = times(h_two, w_sgu)
    s_gate = s_pre[:, :hidden_width]
    s_up = s_pre[:, hidden_width:]
    sig_shared = jax.nn.sigmoid(s_gate)
    silu_shared = s_gate * sig_shared
    s_hidden = (silu_shared * s_up).astype(BF16)
    s_part = times(s_hidden, w_sdown)
    columns_h_two = away_and_near(h_blocks, "grp")
    flat_rows = select_rows(rank, after(h_two, s_part, columns_h_two), capacity)
    gates = [h_blocks[-1], s_hidden, flat_rows]
    for k in range(1, ep_count):
        leaving = after(grad_blocks[-1], gates[min(k, len(gates)) - 1])
        grad_blocks.append(lax.ppermute(leaving, "ep", ring))
    flat_rows = flat_rows.reshape(slot_shape)
    grad_low = jnp.concatenate(grad_blocks, axis=0)
    grad_all = grad_low.astype(F32)
    grad_sout = (switch[:, None] * grad_all).astype(BF16)
    grad_shidden = times_trans(grad_sout, w_sdown)
    slope_shared = sig_shared * (1.0 + s_gate * (1.0 - sig_shared))
    grad_s = jnp.concatenate(
        [
            (grad_shidden * s_up * slope_shared).astype(BF16),
            (grad_shidden * silu_shared).astype(BF16),
        ],
        axis=1,
    )
    gate_pre = jnp.einsum("erd,edf->erf", flat_rows, expert_gate, preferred_element_type=F32)
    up_pre = jnp.einsum("erd,edf->erf", flat_rows, expert_up, preferred_element_type=F32)
    sig_expert = jax.nn.sigmoid(gate_pre)
    silu_gate = gate_pre * sig_expert
    hidden = (silu_gate * up_pre).astype(BF16)
    result = jnp.einsum("erf,efd->erd", hidden, expert_down, preferred_element_type=F32).astype(
        BF16
    )
    row_shape = (experts_here, ep_count, capacity, model_width)
    mixture = spread_rows(rank, local_probs, result.reshape(row_shape)).reshape(
        length, model_width
    )
    y_part = switch[:, None] * s_part + mixture
    y_first = block_of(y_part, 1 % ep_count).astype(BF16)
    grad_rows = select_rows(rank, after(grad_low, y_first), capacity).reshape(slot_shape)
    grad_plain = jnp.einsum("erd,efd->erf", grad_rows, expert_down, preferred_element_type=F32)
    grad_gate = jnp.sum(grad_plain * hidden.astype(F32), axis=-1)
    grad_hidden = gate_rows * grad_plain
    slope_expert = sig_expert * (1.0 + gate_pre * (1.0 - sig_expert))
    grad_gate_pre = (grad_hidden * up_pre * slope_expert).astype(BF16)
    grad_up_pre = (grad_hidden * silu_gate).astype(BF16)
    hidden_gated = (gate_rows * hidden.astype(F32)).astype(BF16)
    grad_inputs = (
        jnp.einsum("erf,edf->erd", grad_gate_pre, expert_gate, preferred_element_type=F32)
        + jnp.einsum("erf,edf->erd", grad_up_pre, expert_up, preferred_element_type=F32)
    ).astype(BF16)
    grad_moe = spread_rows(
        rank, jnp.ones_like(local_probs), grad_inputs.reshape(row_shape)
    ).reshape(length, model_width)

    layer_own = x1_own + ring_reduce(lambda k: block_of(y_part, k), "ep", y_first)

    shared_dot = jnp.sum(grad_all * s_part, axis=-1).reshape(1, ep_count, own_count)
    grad_probs_part = jnp.sum(
        jnp.where(
            hot, grad_gate.reshape(experts_here, ep_count, capacity)[:, :, :, None], 0.0
        ),
        axis=2,
    )
    scalars = jnp.concatenate([grad_probs_part, shared_dot], axis=0)
    home = [scalars[:, 0]]
    for k in range(1, ep_count):
        home.append(
            lax.ppermute(scalars[:, k], "ep", [(j, (j - k) % ep_count) for j in range(ep_count)])
        )
    home = jnp.stack(home)
    grad_probs = jnp.take(
        home[:, :experts_here],
        (jnp.arange(ep_count, dtype=jnp.int32) - place) % ep_count,
        axis=0,
    )
    grad_probs = grad_probs.reshape(experts_all, own_count).T
    probs_own = route_probs[:own_count]
    switch_own = switch[:own_count]
    grad_logit = (
        probs_own * (grad_probs - jnp.sum(probs_own * grad_probs, axis=-1, keepdims=True))
    ).astype(BF16)
    grad_switch = (
        jnp.sum(home[:, experts_here], axis=0) * switch_own * (1.0 - switch_own)
    ).astype(BF16)

    w_small = jnp.concatenate([w_router, w_switch[:, None]], axis=1)
    grad_small = jnp.concatenate([grad_logit, grad_switch[:, None]], axis=1)
    grad_s_ring, layer_own = lax.optimization_barrier((grad_s, layer_own))
    layer_out = layer_own.reshape(row_count, own_count, model_width).astype(BF16)

    def grad_h2_part(k):
        return times_trans(block_of(grad_s_ring, k), w_sgu) + block_of(grad_moe, k)

    grad_h2_first = grad_h2_part(1 % ep_count).astype(BF16)
    grad_h2 = ring_reduce(grad_h2_part, "ep", grad_h2_first) + times_trans(grad_small, w_small)
    late_rows, late_hidden, late_grad_gate, late_grad_up, late_grad_rows, _ = (
        lax.optimization_barrier(
            (flat_rows, hidden_gated, grad_gate_pre, grad_up_pre, grad_rows, grad_h2_first)
        )
    )
    part_edown, part_egate, part_eup = (
        jnp.einsum(form, left_side, right_side, preferred_element_type=F32).astype(BF16)
        for form, left_side, right_side in (
            ("erf,erd->efd", late_hidden, late_grad_rows),
            ("erd,erf->edf", late_rows, late_grad_gate),
            ("erd,erf->edf", late_rows, late_grad_up),
        )
    )
    weighted = grad_h2 * gain_second
    grad_x1 = grad_own_low.astype(F32) + inverse_two * (
        weighted - hat_two * jnp.mean(weighted * hat_two, axis=-1, keepdims=True)
    )
    grad_x1_low = after(grad_x1.astype(BF16), part_edown, part_egate, part_eup)
    late_grad_sout, late_columns, late_s_hidden, late_grad_s, _ = lax.optimization_barrier(
        (grad_sout, columns_h_two, s_hidden, grad_s, grad_x1_low)
    )
    sum_sdown = jnp.concatenate(
        halving_sum(
            lambda columns, p: inner_rows(
                late_s_hidden[:, p * hidden_width // 2 : (p + 1) * hidden_width // 2], columns
            ),
            away_and_near([late_grad_sout], "grp"),
            "grp",
            1,
            2,
        ),
        axis=0,
    )
    sum_sgate, sum_sup = halving_sum(
        lambda columns, p: inner_rows(
            columns, late_grad_s[:, p * hidden_width : (p + 1) * hidden_width]
        ),
        late_columns,
        "grp",
        0,
        2,
    )

    sum_edown = scatter_sum(part_edown, 2)
    sum_egate = scatter_sum(part_egate, 1)
    sum_eup = scatter_sum(part_eup, 1)
    grad_attn_blocks = ring_gather(grad_x1_low, "ep")
    sum_out = jnp.concatenate(
        halving_sum(
            lambda columns, p: inner_rows(
                o_low[:, p * head_width // 2 : (p + 1) * head_width // 2], columns
            ),
            away_and_near(grad_attn_blocks, "grp"),
            "grp",
            1,
            2,
        ),
        axis=0,
    )
    grad_o = jnp.concatenate(
        [times_trans(block, w_out).astype(BF16) for block in grad_attn_blocks], axis=0
    )
    grad_qkv = attend_back(qkv, grad_o, mask_by_key, cosine_table, sine_table, own_count)
    grad_qkv, sum_edown, sum_egate, sum_eup = lax.optimization_barrier(
        (grad_qkv, sum_edown, sum_egate, sum_eup)
    )
    gain_two_part = jnp.sum(grad_h2 * hat_two, axis=0)
    small_part = after(
        jnp.concatenate([inner_rows(grad_small, h_own), gain_two_part[None, :]], axis=0), grad_qkv
    )
    chunk_width = model_width // grp_count
    grp_place = lax.axis_index("grp")
    small_sum = sum_all(
        lax.dynamic_slice_in_dim(sum_all(small_part, "grp"), grp_place * chunk_width, chunk_width, 1),
        "ep",
    )

    qkv_half = 3 * head_width // 2
    sum_qkv = jnp.concatenate(
        halving_sum(
            lambda columns, p: inner_rows(
                columns, grad_qkv[:, p * qkv_half : (p + 1) * qkv_half]
            ),
            columns_h_one,
            "grp",
            0,
            2,
        ),
        axis=1,
    )
    bias_sum = jnp.sum(grad_qkv.astype(F32), axis=0).reshape(3 * heads_here, head_size)
    bias_width = head_size // grp_count
    sum_bias = lax.dynamic_slice_in_dim(
        sum_all(bias_sum, "grp"), grp_place * bias_width, bias_width, 1
    )
    grad_h1 = ring_reduce(lambda k: times_trans(block_of(grad_qkv, k), w_qkv), "ep")
    grad_tokens = grad_x1 + norm_back(x_own, gain_first, grad_h1)
    tokens_grad = grad_tokens.reshape(row_count, own_count, model_width)
    gain_one_part = jnp.sum(grad_h1 * (x_own * inverse_rms(x_own)), axis=0)[None, :]
    gain_one = sum_all(
        lax.dynamic_slice_in_dim(
            sum_all(gain_one_part, "grp"), grp_place * chunk_width, chunk_width, 1
        ),
        "ep",
    )[0]

    def of_heads(values, part):
        begins = range(part * head_size, 3 * head_width, 3 * head_size)
        return jnp.concatenate([values[:, b : b + head_size] for b in begins], axis=1)

    return (
        layer_out,
        tokens_grad,
        gain_one,
        of_heads(sum_qkv, 0),
        of_heads(sum_qkv, 1),
        of_heads(sum_qkv, 2),
        sum_bias[0::3],
        sum_bias[1::3],
        sum_bias[2::3],
        sum_out,
        small_sum[experts_all + 1],
        small_sum[:experts_all].T,
        small_sum[experts_all],
        sum_sgate,
        sum_sup,
        sum_sdown,
        sum_egate,
        sum_eup,
        sum_edown,
    )


def solution(mesh):
    return jax.shard_map(
        per_device,
        mesh=mesh,
        in_specs=(
            P("grp", "ep", None),
            P("grp"),
            P("grp", "ep"),
            P("grp", "ep"),
            P("grp", "ep"),
            P("ep", "grp"),
            P("ep", "grp"),
            P("ep", "grp"),
            P("ep", "grp"),
            P("grp"),
            P("grp", None),
            P("grp"),
            P("grp", "ep"),
            P("grp", "ep"),
            P("ep", "grp"),
            P("ep", None, None),
            P("ep", None, None),
            P("ep", None, None),
            P("grp", "ep", None),
            P("grp", None),
            P("grp", None),
            P("grp", "ep", None),
        ),
        out_specs=(
            P("grp", "ep", None),
            P("grp", "ep", None),
            P("grp"),
            P("grp", "ep"),
            P("grp", "ep"),
            P("grp", "ep"),
            P("ep", "grp"),
            P("ep", "grp"),
            P("ep", "grp"),
            P("ep", "grp"),
            P("grp"),
            P("grp", None),
            P("grp"),
            P("grp", "ep"),
            P("grp", "ep"),
            P("ep", "grp"),
            P("ep", "grp", None),
            P("ep", "grp", None),
            P("ep", None, "grp"),
        ),
        check_vma=False,
    )
```

```python
import math

import jax
import jax.numpy as jnp
from jax import lax
from jax.experimental import pallas as pl
from jax.experimental.pallas import tpu as pltpu
from jax.sharding import PartitionSpec as P

EPS = 1e-06
THETA = 1000000.0
NEG = -1e30
LOG2E = 1.4426950408889634
F32 = jnp.float32
BF16 = jnp.bfloat16


def inverse_rms(values):
    return lax.rsqrt(jnp.mean(values * values, axis=-1, keepdims=True) + EPS)


def norm_back(values, gain_vec, upstream):
    inverse = inverse_rms(values)
    scaled = values * inverse
    weighted = upstream * gain_vec
    return inverse * (weighted - scaled * jnp.mean(weighted * scaled, axis=-1, keepdims=True))


def rotary_tables(position, head_size):
    frequency = THETA ** (-(jnp.arange(head_size // 2, dtype=F32) * 2.0 / head_size))
    angle = position.astype(F32)[:, None] * frequency[None, :]
    cosine, sine = jnp.cos(angle), jnp.sin(angle)
    return (
        jnp.concatenate([cosine, cosine], axis=1),
        jnp.concatenate([-sine, sine], axis=1),
    )


def after(values, *others):
    return lax.optimization_barrier((values, *others))[0]


def by_head(queries, keys, values, heads):
    rows = queries.shape[0]
    parts = [part.reshape(rows, heads, -1) for part in (queries, keys, values)]
    return jnp.concatenate(parts, axis=2).reshape(rows, -1)


def inner_rows(left_side, right_side):
    return lax.dot_general(
        left_side, right_side, (((0,), (0,)), ((), ())), preferred_element_type=F32
    )


def times_trans(left_side, right_side):
    return lax.dot_general(
        left_side, right_side, (((1,), (1,)), ((), ())), preferred_element_type=F32
    )


def times(left_side, right_side):
    return jnp.dot(left_side, right_side, preferred_element_type=F32)


def ring_gather(own_block, axis):
    count = lax.axis_size(axis)
    pairs = [(j, (j + 1) % count) for j in range(count)]
    blocks = [own_block]
    for _ in range(count - 1):
        blocks.append(lax.ppermute(blocks[-1], axis, pairs))
    return blocks


def ring_reduce(part_of, axis, first=None, beside=None):
    count = lax.axis_size(axis)
    pairs = [(j, (j + 1) % count) for j in range(count)]
    running = part_of(1 % count).astype(BF16) if first is None else first
    parts = [lax.optimization_barrier(part_of((step + 1) % count)) for step in range(1, count)]
    for step in range(1, count):
        arrived = lax.ppermute(running, axis, pairs)
        held = parts[step : step + 1]
        if beside is not None:
            held = held + list(beside(step, running))
        part = after(parts[step - 1], *held) if held else parts[step - 1]
        running = arrived.astype(F32) + part
        if step < count - 1:
            running = running.astype(BF16)
    return running


def bits_of(axis):
    return range(lax.axis_size(axis).bit_length() - 1)


def swap(values, axis, bit):
    count = lax.axis_size(axis)
    return lax.ppermute(values, axis, [(j, j ^ (1 << bit)) for j in range(count)])


def sum_all(values, axis):
    for bit in bits_of(axis):
        values = values + swap(values, axis, bit)
    return values


def gather_small(values, axis):
    count = lax.axis_size(axis)
    blocks = values[None, :]
    for bit in bits_of(axis):
        blocks = jnp.concatenate([blocks, swap(blocks, axis, bit)], axis=0)
    index = jnp.arange(count, dtype=jnp.int32)
    apart = index[:, None] ^ lax.axis_index(axis)
    return times((apart == index[None, :]).astype(values.dtype), blocks).astype(values.dtype)


def column_kernel(order_ref, *refs):
    out_ref = refs[-1]
    begin = 0
    for data_ref in refs[:-1]:
        out_ref[begin : begin + data_ref.shape[0], :] = data_ref[...]
        begin += data_ref.shape[0]


def column_chunks(blocks, order):
    rows = sum(block.shape[0] for block in blocks)
    count = order.shape[0]
    chunk = blocks[0].shape[1] // count
    return pl.pallas_call(
        column_kernel,
        grid_spec=pltpu.PrefetchScalarGridSpec(
            num_scalar_prefetch=1,
            grid=(count,),
            in_specs=[
                pl.BlockSpec((block.shape[0], chunk), lambda r, order_ref: (0, order_ref[r]))
                for block in blocks
            ],
            out_specs=pl.BlockSpec((rows, chunk), lambda r, order_ref: (0, r)),
        ),
        out_shape=jax.ShapeDtypeStruct((rows, count * chunk), blocks[0].dtype),
        cost_estimate=pl.CostEstimate(
            flops=0, bytes_accessed=4 * rows * count * chunk, transcendentals=0
        ),
        name="column_chunks",
    )(order, *blocks)


def away_and_near(blocks, axis):
    count = lax.axis_size(axis)
    index = jnp.arange(count, dtype=jnp.int32).reshape(count // 2, 2)
    order = lax.axis_index(axis) ^ jnp.concatenate([index[:, 1], index[:, 0]])
    return column_chunks(blocks, order)


def halving_send(part_of, columns, axis, parts):
    half = columns.shape[1] // 2
    away, near = columns[:, :half], columns[:, half:]
    leaving = [part_of(away, p).astype(BF16) for p in range(parts)]
    return leaving, near, [swap(block, axis, 0) for block in leaving]


def halving_near(part_of, near, arrived, tie):
    near, *arrived = lax.optimization_barrier((near, *arrived, tie))[:-1]
    return [(part_of(near, p) + block.astype(F32)).astype(BF16) for p, block in enumerate(arrived)]


def halving_rest(sums, axis, dimension, tie=None):
    count = lax.axis_size(axis)
    results = []
    for p, near_sum in enumerate(sums):
        steps = list(bits_of(axis))[1:]
        if p % 2:
            steps.reverse()
        held = dict(zip(range(0, count, 2), jnp.split(near_sum, count // 2, axis=dimension)))
        for turn, bit in enumerate(steps):
            leaving = [r for r in held if r >> bit & 1]
            staying = [r for r in held if not r >> bit & 1]
            sent = jnp.concatenate([held[r].astype(BF16) for r in leaving], axis=dimension)
            come = swap(sent, axis, bit)
            if turn == 0 and tie is not None:
                come = after(come, tie)
            for r, block in zip(leaving, jnp.split(come, len(leaving), axis=dimension)):
                held[r ^ (1 << bit)] = (
                    held[r ^ (1 << bit)].astype(BF16).astype(F32) + block.astype(F32)
                )
            held = {r: held[r] for r in staying}
        results.append(held[0])
    return results


def select_kernel(rank_ref, data_ref, out_ref):
    experts, _, slots, _ = out_ref.shape
    tokens = data_ref.shape[1]
    slot = lax.broadcasted_iota(jnp.int32, (slots, tokens), 0)
    hot = jnp.concatenate(
        [jnp.where(slot == rank_ref[e, 0], 1.0, 0.0).astype(BF16) for e in range(experts)], axis=0
    )
    rows = jnp.dot(hot, data_ref[0], preferred_element_type=F32).astype(BF16)
    for e in range(experts):
        out_ref[e, 0] = rows[e * slots : (e + 1) * slots]


def select_rows(rank, data, slots):
    experts, blocks, tokens = rank.shape
    width = data.shape[-1]
    return pl.pallas_call(
        select_kernel,
        grid=(blocks,),
        in_specs=[
            pl.BlockSpec((experts, 1, 1, tokens), lambda s: (0, s, 0, 0)),
            pl.BlockSpec((1, tokens, width), lambda s: (s, 0, 0)),
        ],
        out_specs=pl.BlockSpec((experts, 1, slots, width), lambda s: (0, s, 0, 0)),
        out_shape=jax.ShapeDtypeStruct((experts, blocks, slots, width), BF16),
        cost_estimate=pl.CostEstimate(
            flops=2 * experts * blocks * slots * tokens * width,
            bytes_accessed=2 * (experts * blocks * slots + blocks * tokens) * width,
            transcendentals=0,
        ),
        name="select_rows",
    )(rank.reshape(experts, blocks, 1, tokens), data.reshape(blocks, tokens, width))


def spread_kernel(rank_ref, weight_ref, rows_ref, *refs):
    out_ref = refs[-1]
    experts, _, slots, _ = rows_ref.shape
    tokens = out_ref.shape[1]
    slot = lax.broadcasted_iota(jnp.int32, (tokens, slots), 1)
    total = None
    for e in range(experts):
        hot = jnp.where(slot == rank_ref[e, 0], weight_ref[e, 0], 0.0).astype(BF16)
        part = jnp.dot(hot, rows_ref[e, 0], preferred_element_type=F32)
        total = part if total is None else total + part
    if len(refs) == 3:
        total = total + refs[0][0] * refs[1][0].astype(F32)
    out_ref[0] = total.astype(BF16)


def spread_rows(rank, weight, rows, scale=None, addend=None):
    experts, blocks, tokens = rank.shape
    slots, width = rows.shape[2:]
    column = pl.BlockSpec((experts, 1, tokens, 1), lambda s: (0, s, 0, 0))
    in_specs = [
        column,
        column,
        pl.BlockSpec((experts, 1, slots, width), lambda s: (0, s, 0, 0)),
    ]
    operands = [
        rank.reshape(experts, blocks, tokens, 1),
        weight.reshape(experts, blocks, tokens, 1),
        rows,
    ]
    if addend is not None:
        in_specs += [
            pl.BlockSpec((1, tokens, 1), lambda s: (s, 0, 0)),
            pl.BlockSpec((1, tokens, width), lambda s: (s, 0, 0)),
        ]
        operands += [scale.reshape(blocks, tokens, 1), addend.reshape(blocks, tokens, width)]
    return pl.pallas_call(
        spread_kernel,
        grid=(blocks,),
        in_specs=in_specs,
        out_specs=pl.BlockSpec((1, tokens, width), lambda s: (s, 0, 0)),
        out_shape=jax.ShapeDtypeStruct((blocks, tokens, width), BF16),
        cost_estimate=pl.CostEstimate(
            flops=2 * experts * blocks * slots * tokens * width,
            bytes_accessed=(2 * experts * blocks * slots + 4 * blocks * tokens) * width,
            transcendentals=0,
        ),
        name="spread_rows",
    )(*operands).reshape(blocks * tokens, width)


def project_kernel(rows_ref, weight_ref, bias_ref, cosine_ref, sine_ref, held_ref, out_ref):
    head_size = cosine_ref.shape[1]
    sums = (
        jnp.dot(rows_ref[...], weight_ref[...], preferred_element_type=F32) + bias_ref[0:1, :]
    )
    for part in range(3):
        values = sums[:, part * head_size : (part + 1) * head_size]
        if part < 2:
            turned = pltpu.roll(values, head_size // 2, 1)
            values = values * cosine_ref[...] + turned * sine_ref[...]
        out_ref[:, part * head_size : (part + 1) * head_size] = values.astype(BF16)


def project(rows, weight, bias, cosine, sine, held, k):
    count, width = rows.shape
    head_size = cosine.shape[1]
    columns = 3 * head_size
    total = weight.shape[1]
    return pl.pallas_call(
        project_kernel,
        grid=(total // columns,),
        in_specs=[
            pl.BlockSpec((count, width), lambda h: (0, 0)),
            pl.BlockSpec((width, columns), lambda h: (0, h)),
            pl.BlockSpec((8, columns), lambda h: (0, h)),
            pl.BlockSpec((count, head_size), lambda h: (k, 0)),
            pl.BlockSpec((count, head_size), lambda h: (k, 0)),
            pl.BlockSpec(memory_space=pl.ANY),
        ],
        out_specs=pl.BlockSpec((count, columns), lambda h: (k, h)),
        out_shape=jax.ShapeDtypeStruct(held.shape, BF16),
        input_output_aliases={5: 0},
        cost_estimate=pl.CostEstimate(
            flops=2 * count * width * total,
            bytes_accessed=2 * (count * width + width * total + count * total),
            transcendentals=0,
        ),
        name="project",
    )(rows, weight, bias, cosine, sine, held)


def attend_kernel(q_ref, k_ref, v_ref, mask_ref, out_ref, *, score_scale):
    scores = (
        lax.dot_general(
            q_ref[...], k_ref[...], (((1,), (1,)), ((), ())), preferred_element_type=F32
        )
        * (score_scale * LOG2E)
        + mask_ref[...]
    )
    exponent = jnp.exp2(scores - jnp.max(scores, axis=1, keepdims=True))
    weights = exponent * (1.0 / jnp.sum(exponent, axis=1, keepdims=True))
    out_ref[...] = jnp.dot(
        weights.astype(BF16), v_ref[...], preferred_element_type=F32
    ).astype(BF16)


def attend(qkv, mask, count, head_size, k):
    length, total = qkv.shape
    heads = total // (3 * head_size)
    return pl.pallas_call(
        lambda *refs: attend_kernel(*refs, score_scale=1.0 / math.sqrt(head_size)),
        grid=(heads,),
        in_specs=[
            pl.BlockSpec((count, head_size), lambda h: (k, 3 * h)),
            pl.BlockSpec((length, head_size), lambda h: (0, 3 * h + 1)),
            pl.BlockSpec((length, head_size), lambda h: (0, 3 * h + 2)),
            pl.BlockSpec((count, length), lambda h: (k, 0)),
        ],
        out_specs=pl.BlockSpec((count, head_size), lambda h: (0, h)),
        out_shape=jax.ShapeDtypeStruct((count, heads * head_size), BF16),
        cost_estimate=pl.CostEstimate(
            flops=4 * count * length * heads * head_size,
            bytes_accessed=4 * (count + length) * heads * head_size,
            transcendentals=heads * count * length,
        ),
        name="attend",
    )(qkv, qkv, qkv, mask)


def attend_back_block(q_ref, k_ref, v_ref, grad_ref, mask_ref, cosine_ref, sine_ref):
    score_scale = 1.0 / math.sqrt(q_ref.shape[1])
    scores = (
        lax.dot_general(
            k_ref[...], q_ref[...], (((1,), (1,)), ((), ())), preferred_element_type=F32
        )
        * (score_scale * LOG2E)
        + mask_ref[...]
    )
    exponent = jnp.exp2(scores - jnp.max(scores, axis=0, keepdims=True))
    probs = exponent * (1.0 / jnp.sum(exponent, axis=0, keepdims=True))
    grad_probs = lax.dot_general(
        v_ref[...], grad_ref[...], (((1,), (1,)), ((), ())), preferred_element_type=F32
    )
    centre = jnp.sum(probs * grad_probs, axis=0, keepdims=True)
    grad_scores = (probs * (grad_probs - centre)).astype(BF16)
    grad_keys = jnp.dot(grad_scores, q_ref[...], preferred_element_type=F32) * score_scale
    grad_values = jnp.dot(probs.astype(BF16), grad_ref[...], preferred_element_type=F32)
    grad_queries = lax.dot_general(
        grad_scores, k_ref[...], (((0,), (0,)), ((), ())), preferred_element_type=F32
    )
    return turn_back(grad_queries * score_scale, cosine_ref, sine_ref), grad_keys, grad_values


def turn_back(values, cosine_ref, sine_ref):
    turned = pltpu.roll(values, values.shape[1] // 2, 1)
    return (values * cosine_ref[...] - turned * sine_ref[...]).astype(BF16)


def attend_back_some_kernel(
    q_ref, k_ref, v_ref, grad_ref, mask_ref, cosine_ref, sine_ref, gq_ref, gk_ref, gv_ref
):
    gq_ref[...], grad_keys, grad_values = attend_back_block(
        q_ref, k_ref, v_ref, grad_ref, mask_ref, cosine_ref, sine_ref
    )

    @pl.when(pl.program_id(1) == 0)
    def _():
        gk_ref[...] = grad_keys
        gv_ref[...] = grad_values

    @pl.when(pl.program_id(1) > 0)
    def _():
        gk_ref[...] += grad_keys
        gv_ref[...] += grad_values


def attend_back_last_kernel(
    q_ref, k_ref, v_ref, grad_ref, mask_ref, cosine_ref, sine_ref,
    all_cosine_ref, all_sine_ref, some_gq_ref, some_gk_ref, some_gv_ref, out_ref
):
    head_size = q_ref.shape[1]
    before = some_gq_ref.shape[0]
    grad_queries, grad_keys, grad_values = attend_back_block(
        q_ref, k_ref, v_ref, grad_ref, mask_ref, cosine_ref, sine_ref
    )
    out_ref[:before, :head_size] = some_gq_ref[...]
    out_ref[before:, :head_size] = grad_queries
    out_ref[:, head_size : 2 * head_size] = turn_back(
        some_gk_ref[...] + grad_keys, all_cosine_ref, all_sine_ref
    )
    out_ref[:, 2 * head_size :] = (some_gv_ref[...] + grad_values).astype(BF16)


def attend_back(qkv, grad_out, mask, cosine, sine, count, some=None):
    length, total = qkv.shape
    head_size = cosine.shape[1]
    heads = total // (3 * head_size)
    blocks = grad_out.shape[0] // count
    first = 0 if some is None else length // count - 1
    in_specs = [
        pl.BlockSpec((count, head_size), lambda h, i: (i + first, 3 * h)),
        pl.BlockSpec((length, head_size), lambda h, i: (0, 3 * h + 1)),
        pl.BlockSpec((length, head_size), lambda h, i: (0, 3 * h + 2)),
        pl.BlockSpec((count, head_size), lambda h, i: (i, h)),
        pl.BlockSpec((length, count), lambda h, i: (0, i + first)),
        pl.BlockSpec((count, head_size), lambda h, i: (i + first, 0)),
        pl.BlockSpec((count, head_size), lambda h, i: (i + first, 0)),
    ]
    cost = pl.CostEstimate(
        flops=10 * blocks * count * length * heads * head_size,
        bytes_accessed=20 * length * heads * head_size,
        transcendentals=heads * blocks * count * length,
    )
    whole = pl.BlockSpec((length, head_size), lambda h, i: (0, h))
    operands = [qkv, qkv, qkv, grad_out, mask, cosine, sine]
    if some is None:
        wide = jax.ShapeDtypeStruct((length, heads * head_size), F32)
        return pl.pallas_call(
            attend_back_some_kernel,
            grid=(heads, blocks),
            in_specs=in_specs,
            out_specs=[
                pl.BlockSpec((count, head_size), lambda h, i: (i, h)),
                whole,
                whole,
            ],
            out_shape=[
                jax.ShapeDtypeStruct((blocks * count, heads * head_size), BF16),
                wide,
                wide,
            ],
            cost_estimate=cost,
            name="attend_back_some",
        )(*operands)
    everywhere = pl.BlockSpec((length, head_size), lambda h, i: (0, 0))
    return pl.pallas_call(
        attend_back_last_kernel,
        grid=(heads, 1),
        in_specs=in_specs
        + [
            everywhere,
            everywhere,
            pl.BlockSpec((some[0].shape[0], head_size), lambda h, i: (0, h)),
            whole,
            whole,
        ],
        out_specs=pl.BlockSpec((length, 3 * head_size), lambda h, i: (0, h)),
        out_shape=jax.ShapeDtypeStruct((length, total), BF16),
        cost_estimate=cost,
        name="attend_back_last",
    )(*operands, cosine, sine, *some)


def scatter_raw(values, dimension):
    return lax.psum_scatter(values.astype(BF16), "grp", scatter_dimension=dimension, tiled=True)


def per_device(
    tokens,
    attn_norm,
    query_weight,
    key_weight,
    value_weight,
    query_bias,
    key_bias,
    value_bias,
    out_weight,
    ffn_norm,
    router_weight,
    shared_switch,
    shared_gate,
    shared_up,
    shared_down,
    expert_gate,
    expert_up,
    expert_down,
    routes,
    pieces,
    documents,
    cotangent,
):
    ep_count = lax.axis_size("ep")
    grp_count = lax.axis_size("grp")
    place = lax.axis_index("ep")
    row_count, own_count, model_width = tokens.shape
    length = own_count * ep_count
    heads_here = query_bias.shape[0]
    head_size = query_bias.shape[1] * grp_count
    head_width = heads_here * head_size
    hidden_width = shared_gate.shape[1]
    experts_here = expert_gate.shape[0]
    experts_all = experts_here * ep_count
    top_count = routes.shape[2]
    capacity = (own_count * top_count // experts_all * 5 + 3) // 4
    order = (place - jnp.arange(ep_count, dtype=jnp.int32)) % ep_count

    w_qkv = lax.all_gather(
        by_head(query_weight, key_weight, value_weight, heads_here),
        "grp",
        axis=0,
        tiled=True,
    )
    small_sizes = [
        attn_norm.size,
        query_bias.size,
        key_bias.size,
        value_bias.size,
        ffn_norm.size,
        router_weight.size,
        shared_switch.size,
    ]
    small = gather_small(
        jnp.concatenate(
            [
                part.reshape(-1)
                for part in (
                    attn_norm,
                    query_bias,
                    key_bias,
                    value_bias,
                    ffn_norm,
                    router_weight,
                    shared_switch,
                )
            ]
        ),
        "grp",
    )
    pieces_of_small = []
    begin = 0
    for size in small_sizes:
        pieces_of_small.append(small[:, begin : begin + size])
        begin += size
    gain_first = pieces_of_small[0].reshape(-1).astype(F32)
    biases = [
        part.reshape(grp_count, heads_here, -1).transpose(1, 0, 2).reshape(1, -1)
        for part in pieces_of_small[1:4]
    ]
    bias_qkv = jnp.broadcast_to(
        by_head(*biases, heads_here).astype(F32), (8, 3 * head_width)
    )
    gain_second = pieces_of_small[4].reshape(-1).astype(F32)
    w_router = pieces_of_small[5].reshape(model_width, experts_all)
    w_switch = pieces_of_small[6].reshape(model_width)
    w_out = lax.all_gather(out_weight, "grp", axis=1, tiled=True)
    w_sgu = lax.all_gather(
        jnp.concatenate([shared_gate, shared_up], axis=1), "grp", axis=0, tiled=True
    )
    w_sdown = lax.all_gather(shared_down, "grp", axis=1, tiled=True)

    tokens_own = tokens.reshape(own_count, model_width)
    grad_own_low = cotangent.reshape(own_count, model_width)
    x_blocks = ring_gather(tokens_own, "ep")
    routes_own = routes.reshape(own_count, top_count).T
    chosen = jnp.stack(
        [routes_own]
        + [
            lax.ppermute(routes_own, "ep", [(j, (j + k) % ep_count) for j in range(ep_count)])
            for k in range(1, ep_count)
        ]
    )
    own_places = jnp.arange(own_count, dtype=jnp.int32)
    position = (order[:, None] * own_count + own_places[None, :]).reshape(length)
    piece = jnp.take(pieces.reshape(ep_count, own_count), order, axis=0).reshape(length)
    document = jnp.take(documents.reshape(ep_count, own_count), order, axis=0).reshape(length)
    allowed = (document[:, None] == document[None, :]) & (
        (position[:, None] >= position[None, :])
        | ((piece[:, None] == piece[None, :]) & (piece[:, None] > 0))
    )
    allowed_by_key = (document[:, None] == document[None, :]) & (
        (position[:, None] <= position[None, :])
        | ((piece[:, None] == piece[None, :]) & (piece[:, None] > 0))
    )
    mask = jnp.where(allowed, 0.0, NEG)
    mask_by_key = jnp.where(allowed_by_key, 0.0, NEG)
    cosine_table, sine_table = rotary_tables(position, head_size)
    qkv = jnp.zeros((length, 3 * head_width), BF16)
    h_parts = []
    for k, block in enumerate(x_blocks):
        wide = after(block, qkv).astype(F32)
        h_parts.append((wide * inverse_rms(wide) * gain_first).astype(BF16))
        qkv = project(h_parts[k], w_qkv, bias_qkv, cosine_table, sine_table, qkv, k)
    qkv, chosen = lax.optimization_barrier((qkv, chosen))
    columns_h_one = away_and_near(h_parts, "grp")
    o_parts = [None] * ep_count
    ready = qkv
    for step in range(ep_count):
        k = (step + 1) % ep_count
        o_parts[k] = attend(ready, mask, own_count, head_size, k)
        if step == 1:
            ready = after(ready, columns_h_one, mask_by_key)
        ready, o_parts[k] = lax.optimization_barrier((ready, o_parts[k]))
    o_low = jnp.concatenate(o_parts, axis=0)

    def block_of(values, k):
        return values[k * own_count : (k + 1) * own_count]

    attn_own = ring_reduce(lambda k: times(o_parts[k], w_out), "ep")
    x_own = tokens_own.astype(F32)
    x1_own = x_own + attn_own
    inverse_two = inverse_rms(x1_own)
    hat_two = x1_own * inverse_two
    h_own = (hat_two * gain_second).astype(BF16)
    h_blocks = ring_gather(h_own, "ep")
    h_two = jnp.concatenate(h_blocks, axis=0)
    logits = times(h_two, jnp.concatenate([w_router, w_switch[:, None]], axis=1))
    route_probs = jax.nn.softmax(logits[:, :experts_all], axis=-1)
    switch = jax.nn.sigmoid(logits[:, experts_all])
    expert_ids = place * experts_here + jnp.arange(experts_here, dtype=jnp.int32)
    named = jnp.any(chosen[None] == expert_ids[:, None, None, None], axis=2)
    before = (own_places[:, None] < own_places[None, :]).astype(BF16)
    rank = jnp.einsum("est,tu->esu", named.astype(BF16), before, preferred_element_type=F32).astype(
        jnp.int32
    )
    rank = jnp.where(named & (rank < capacity), rank, -1)
    local_probs = lax.dynamic_slice_in_dim(route_probs, place * experts_here, experts_here, 1)
    local_probs = local_probs.reshape(ep_count, own_count, experts_here).transpose(2, 0, 1)
    hot = (
        rank[:, :, None, :] == jnp.arange(capacity, dtype=jnp.int32)[None, None, :, None]
    )
    gate_slot = jnp.sum(jnp.where(hot, local_probs[:, :, None, :], 0.0), axis=-1)
    slot_shape = (experts_here, ep_count * capacity, model_width)
    gate_rows = gate_slot.reshape(experts_here, ep_count * capacity, 1)

    s_pre = times(h_two, w_sgu)
    s_gate = s_pre[:, :hidden_width]
    s_up = s_pre[:, hidden_width:]
    sig_shared = jax.nn.sigmoid(s_gate)
    silu_shared = s_gate * sig_shared
    s_hidden = (silu_shared * s_up).astype(BF16)
    ring = [(j, (j + 1) % ep_count) for j in range(ep_count)]
    grad_blocks = [
        grad_own_low,
        lax.ppermute(after(grad_own_low, h_blocks[-1]), "ep", ring),
    ]
    s_part = times(after(s_hidden, grad_blocks[1]), w_sdown).astype(BF16)
    grad_blocks.append(lax.ppermute(after(grad_blocks[1], s_hidden), "ep", ring))
    for k in range(3, ep_count):
        grad_blocks.append(lax.ppermute(after(grad_blocks[-1], s_part), "ep", ring))
    flat_rows = select_rows(rank, after(h_two, s_part, *grad_blocks[:3]), capacity)
    flat_rows = flat_rows.reshape(slot_shape)
    grad_low = jnp.concatenate(grad_blocks, axis=0)
    grad_all = grad_low.astype(F32)
    grad_sout = (switch[:, None] * grad_all).astype(BF16)
    grad_shidden = times_trans(grad_sout, w_sdown)
    slope_shared = sig_shared * (1.0 + s_gate * (1.0 - sig_shared))
    grad_s = jnp.concatenate(
        [
            (grad_shidden * s_up * slope_shared).astype(BF16),
            (grad_shidden * silu_shared).astype(BF16),
        ],
        axis=1,
    )
    gate_pre = jnp.einsum("erd,edf->erf", flat_rows, expert_gate, preferred_element_type=F32)
    up_pre = jnp.einsum("erd,edf->erf", flat_rows, expert_up, preferred_element_type=F32)
    sig_expert = jax.nn.sigmoid(gate_pre)
    silu_gate = gate_pre * sig_expert
    hidden = (silu_gate * up_pre).astype(BF16)
    result = jnp.einsum(
        "erf,efd->erd",
        after(hidden, *grad_blocks),
        expert_down,
        preferred_element_type=F32,
    ).astype(BF16)
    row_shape = (experts_here, ep_count, capacity, model_width)
    y_part = spread_rows(rank, local_probs, result.reshape(row_shape), switch, s_part)
    y_first = block_of(y_part, 1 % ep_count)
    part_sdown = inner_rows(s_hidden, after(grad_sout, grad_s)).astype(BF16)
    part_sgu = inner_rows(after(h_two, part_sdown), grad_s).astype(BF16)
    raw_sdown = scatter_raw(part_sdown, 1)
    raw_sgu = scatter_raw(part_sgu, 0)
    grad_rows = select_rows(
        rank, after(grad_low, y_first, part_sdown, part_sgu), capacity
    ).reshape(slot_shape)
    grad_plain = jnp.einsum("erd,efd->erf", grad_rows, expert_down, preferred_element_type=F32)
    grad_gate = jnp.sum(grad_plain * hidden.astype(F32), axis=-1)
    grad_hidden = gate_rows * grad_plain
    slope_expert = sig_expert * (1.0 + gate_pre * (1.0 - sig_expert))
    grad_gate_pre = (grad_hidden * up_pre * slope_expert).astype(BF16)
    grad_up_pre = (grad_hidden * silu_gate).astype(BF16)
    hidden_gated = (gate_rows * hidden.astype(F32)).astype(BF16)
    part_edown = jnp.einsum(
        "erf,erd->efd", hidden_gated, grad_rows, preferred_element_type=F32
    ).astype(BF16)
    raw_edown = scatter_raw(part_edown, 2)
    grad_inputs = (
        jnp.einsum(
            "erf,edf->erd",
            after(grad_gate_pre, part_edown),
            expert_gate,
            preferred_element_type=F32,
        )
        + jnp.einsum("erf,edf->erd", grad_up_pre, expert_up, preferred_element_type=F32)
    ).astype(BF16)
    grad_moe = spread_rows(rank, jnp.ones_like(local_probs), grad_inputs.reshape(row_shape))

    layer_own = x1_own + ring_reduce(
        lambda k: block_of(y_part, k),
        "ep",
        y_first,
        lambda step, sent: [grad_moe] if step == ep_count - 1 else [],
    )

    shared_dot = jnp.sum(grad_all * s_part.astype(F32), axis=-1).reshape(1, ep_count, own_count)
    grad_probs_part = jnp.sum(
        jnp.where(
            hot, grad_gate.reshape(experts_here, ep_count, capacity)[:, :, :, None], 0.0
        ),
        axis=2,
    )
    scalars = jnp.concatenate([grad_probs_part, shared_dot], axis=0)
    home = [scalars[:, 0]]
    for k in range(1, ep_count):
        home.append(
            lax.ppermute(scalars[:, k], "ep", [(j, (j - k) % ep_count) for j in range(ep_count)])
        )
    home = jnp.stack(home)
    grad_probs = jnp.take(
        home[:, :experts_here],
        (jnp.arange(ep_count, dtype=jnp.int32) - place) % ep_count,
        axis=0,
    )
    grad_probs = grad_probs.reshape(experts_all, own_count).T
    probs_own = route_probs[:own_count]
    switch_own = switch[:own_count]
    grad_logit = (
        probs_own * (grad_probs - jnp.sum(probs_own * grad_probs, axis=-1, keepdims=True))
    ).astype(BF16)
    grad_switch = (
        jnp.sum(home[:, experts_here], axis=0) * switch_own * (1.0 - switch_own)
    ).astype(BF16)

    w_small = jnp.concatenate([w_router, w_switch[:, None]], axis=1)
    grad_small = jnp.concatenate([grad_logit, grad_switch[:, None]], axis=1)
    grad_s_ring, layer_own = lax.optimization_barrier((grad_s, layer_own))
    layer_out = layer_own.reshape(row_count, own_count, model_width).astype(BF16)

    def grad_h2_part(k):
        return times_trans(block_of(grad_s_ring, k), w_sgu) + block_of(grad_moe, k)

    grad_h2_first = grad_h2_part(1 % ep_count).astype(BF16)
    forms = (
        ("erd,erf->edf", flat_rows, grad_gate_pre),
        ("erd,erf->edf", flat_rows, grad_up_pre),
    )
    expert_raw = []

    def expert_part(sent):
        form, left_side, right_side = forms[len(expert_raw)]
        left_side, right_side, _ = lax.optimization_barrier((left_side, right_side, sent))
        part = jnp.einsum(form, left_side, right_side, preferred_element_type=F32).astype(BF16)
        expert_raw.append(scatter_raw(part, 1))
        return part

    def beside_h2(step, sent):
        return {1: [raw_sdown], 2: [expert_part, raw_sgu], 3: [expert_part]}.get(step, [])

    grad_h2 = ring_reduce(
        grad_h2_part,
        "ep",
        grad_h2_first,
        lambda step, sent: [
            item(sent) if callable(item) else item for item in beside_h2(step, sent)
        ],
    ) + times_trans(grad_small, w_small)
    weighted = grad_h2 * gain_second
    grad_x1 = grad_own_low.astype(F32) + inverse_two * (
        weighted - hat_two * jnp.mean(weighted * hat_two, axis=-1, keepdims=True)
    )
    grad_x1_low = grad_x1.astype(BF16)
    while len(expert_raw) < len(forms):
        expert_part(grad_x1_low)
    grad_attn_blocks = ring_gather(grad_x1_low, "ep")

    back_tables = (mask_by_key, cosine_table, sine_table, own_count)
    grad_o = [times_trans(block, w_out).astype(BF16) for block in grad_attn_blocks[:-1]]
    some_back = attend_back(qkv, jnp.concatenate(grad_o, axis=0), *back_tables)
    last_block = after(grad_attn_blocks[-1], *some_back)
    grad_qkv = attend_back(
        qkv, times_trans(last_block, w_out).astype(BF16), *back_tables, some_back
    )
    gain_two_part = jnp.sum(grad_h2 * hat_two, axis=0)
    small_part = jnp.concatenate([inner_rows(grad_small, h_own), gain_two_part[None, :]], axis=0)
    chunk_width = model_width // grp_count
    grp_place = lax.axis_index("grp")
    qkv_half = 3 * head_width // 2
    grad_h1_first = times_trans(block_of(grad_qkv, 1 % ep_count), w_qkv).astype(BF16)

    def qkv_part(columns, p):
        return inner_rows(columns, grad_qkv[:, p * qkv_half : (p + 1) * qkv_half])

    def out_part(columns, p):
        return inner_rows(o_low[:, p * head_width // 2 : (p + 1) * head_width // 2], columns)

    qkv_left, qkv_columns, qkv_come = halving_send(
        qkv_part, after(columns_h_one, grad_h1_first), "grp", 2
    )
    columns_grad_attn = away_and_near(
        [after(block, *qkv_left) for block in grad_attn_blocks], "grp"
    )
    out_left, out_columns, out_come = halving_send(out_part, columns_grad_attn, "grp", 2)
    near_sums = []

    def beside_h1(step, sent):
        if step == 1:
            return qkv_left
        if step == 2:
            return out_left
        if step == 3:
            near_sums.append(halving_near(qkv_part, qkv_columns, qkv_come, sent))
            near_sums.append(halving_near(out_part, out_columns, out_come, near_sums[0][0]))
            return near_sums[0] + near_sums[1]
        return []

    grad_h1 = ring_reduce(
        lambda k: times_trans(block_of(grad_qkv, k), w_qkv), "ep", grad_h1_first, beside_h1
    )
    qkv_near, out_near = near_sums
    sum_qkv = jnp.concatenate(halving_rest(qkv_near, "grp", 0, grad_h1), axis=1)
    sum_out = jnp.concatenate(halving_rest(out_near, "grp", 1, grad_h1), axis=0)
    small_sum = sum_all(
        lax.dynamic_slice_in_dim(sum_all(after(small_part, *out_near), "grp"), grp_place * chunk_width, chunk_width, 1),
        "ep",
    )

    bias_sum = jnp.sum(grad_qkv.astype(F32), axis=0).reshape(3 * heads_here, head_size)
    bias_width = head_size // grp_count
    sum_bias = lax.dynamic_slice_in_dim(
        sum_all(after(bias_sum, *out_near), "grp"), grp_place * bias_width, bias_width, 1
    )
    grad_tokens = grad_x1 + norm_back(x_own, gain_first, grad_h1)
    tokens_grad = grad_tokens.reshape(row_count, own_count, model_width)
    gain_one_part = jnp.sum(grad_h1 * (x_own * inverse_rms(x_own)), axis=0)[None, :]
    sum_sdown, sum_sgu, sum_edown, sum_egate, sum_eup = (
        raw.astype(F32) for raw in (raw_sdown, raw_sgu, raw_edown, *expert_raw)
    )
    gain_one_part = after(gain_one_part, sum_sdown, sum_sgu, sum_edown)
    gain_one = sum_all(
        lax.dynamic_slice_in_dim(
            sum_all(gain_one_part, "grp"), grp_place * chunk_width, chunk_width, 1
        ),
        "ep",
    )[0]

    def of_heads(values, part):
        begins = range(part * head_size, 3 * head_width, 3 * head_size)
        return jnp.concatenate([values[:, b : b + head_size] for b in begins], axis=1)

    return (
        layer_out,
        tokens_grad,
        gain_one,
        of_heads(sum_qkv, 0),
        of_heads(sum_qkv, 1),
        of_heads(sum_qkv, 2),
        sum_bias[0::3],
        sum_bias[1::3],
        sum_bias[2::3],
        sum_out,
        small_sum[experts_all + 1],
        small_sum[:experts_all].T,
        small_sum[experts_all],
        sum_sgu[:, :hidden_width],
        sum_sgu[:, hidden_width:],
        sum_sdown,
        sum_egate,
        sum_eup,
        sum_edown,
    )


def solution(mesh):
    return jax.shard_map(
        per_device,
        mesh=mesh,
        in_specs=(
            P("grp", "ep", None),
            P("grp"),
            P("grp", "ep"),
            P("grp", "ep"),
            P("grp", "ep"),
            P("ep", "grp"),
            P("ep", "grp"),
            P("ep", "grp"),
            P("ep", "grp"),
            P("grp"),
            P("grp", None),
            P("grp"),
            P("grp", "ep"),
            P("grp", "ep"),
            P("ep", "grp"),
            P("ep", None, None),
            P("ep", None, None),
            P("ep", None, None),
            P("grp", "ep", None),
            P("grp", None),
            P("grp", None),
            P("grp", "ep", None),
        ),
        out_specs=(
            P("grp", "ep", None),
            P("grp", "ep", None),
            P("grp"),
            P("grp", "ep"),
            P("grp", "ep"),
            P("grp", "ep"),
            P("ep", "grp"),
            P("ep", "grp"),
            P("ep", "grp"),
            P("ep", "grp"),
            P("grp"),
            P("grp", None),
            P("grp"),
            P("grp", "ep"),
            P("grp", "ep"),
            P("ep", "grp"),
            P("ep", "grp", None),
            P("ep", "grp", None),
            P("ep", None, "grp"),
        ),
        check_vma=False,
    )
```

```python
import math

import jax
import jax.numpy as jnp
from jax import lax
from jax.experimental import pallas as pl
from jax.experimental.pallas import tpu as pltpu
from jax.sharding import PartitionSpec as P

EPS = 1e-06
THETA = 1000000.0
NEG = -1e30
LOG2E = 1.4426950408889634
WIDE = 512
F32 = jnp.float32
BF16 = jnp.bfloat16


def inverse_rms(values):
    return lax.rsqrt(jnp.mean(values * values, axis=-1, keepdims=True) + EPS)


def norm_back(values, gain_vec, upstream):
    inverse = inverse_rms(values)
    scaled = values * inverse
    weighted = upstream * gain_vec
    return inverse * (weighted - scaled * jnp.mean(weighted * scaled, axis=-1, keepdims=True))


def rotary_tables(position, head_size):
    frequency = THETA ** (-(jnp.arange(head_size // 2, dtype=F32) * 2.0 / head_size))
    angle = position.astype(F32)[:, None] * frequency[None, :]
    cosine, sine = jnp.cos(angle), jnp.sin(angle)
    return (
        jnp.concatenate([cosine, cosine], axis=1),
        jnp.concatenate([-sine, sine], axis=1),
    )


def after(values, *others):
    return lax.optimization_barrier((values, *others))[0]


def by_head(queries, keys, values, heads):
    rows = queries.shape[0]
    parts = [part.reshape(rows, heads, -1) for part in (queries, keys, values)]
    return jnp.concatenate(parts, axis=2).reshape(rows, -1)


def inner_rows(left_side, right_side):
    return lax.dot_general(
        left_side, right_side, (((0,), (0,)), ((), ())), preferred_element_type=F32
    )


def times_trans(left_side, right_side):
    return lax.dot_general(
        left_side, right_side, (((1,), (1,)), ((), ())), preferred_element_type=F32
    )


def times(left_side, right_side):
    return jnp.dot(left_side, right_side, preferred_element_type=F32)


def ring_gather(own_block, axis):
    count = lax.axis_size(axis)
    pairs = [(j, (j + 1) % count) for j in range(count)]
    blocks = [own_block]
    for _ in range(count - 1):
        blocks.append(lax.ppermute(blocks[-1], axis, pairs))
    return blocks


def ring_reduce(part_of, axis, first=None, beside=None, middle=None):
    count = lax.axis_size(axis)
    pairs = [(j, (j + 1) % count) for j in range(count)]
    running = part_of(1 % count).astype(BF16) if first is None else first
    if middle is None:
        parts = [part_of((step + 1) % count) for step in range(1, count)]
    else:
        parts = [*jnp.split(middle, count - 2, axis=0), part_of(0)]
    parts = [lax.optimization_barrier(part) for part in parts]
    for step in range(1, count):
        arrived = lax.ppermute(running, axis, pairs)
        held = parts[step:] if middle is not None else parts[step : step + 1]
        if beside is not None:
            held = held + list(beside(step, running))
        part = after(parts[step - 1], *held) if held else parts[step - 1]
        running = arrived.astype(F32) + part
        if step < count - 1:
            running = running.astype(BF16)
    return running


def bits_of(axis):
    return range(lax.axis_size(axis).bit_length() - 1)


def swap(values, axis, bit):
    count = lax.axis_size(axis)
    return lax.ppermute(values, axis, [(j, j ^ (1 << bit)) for j in range(count)])


def sum_all(values, axis):
    for bit in bits_of(axis):
        values = values + swap(values, axis, bit)
    return values


def gather_small(values, axis):
    count = lax.axis_size(axis)
    blocks = values[None, :]
    for bit in bits_of(axis):
        blocks = jnp.concatenate([blocks, swap(blocks, axis, bit)], axis=0)
    index = jnp.arange(count, dtype=jnp.int32)
    apart = index[:, None] ^ lax.axis_index(axis)
    return times((apart == index[None, :]).astype(values.dtype), blocks).astype(values.dtype)


def column_kernel(order_ref, *refs):
    out_ref = refs[-1]
    begin = 0
    for data_ref in refs[:-1]:
        out_ref[begin : begin + data_ref.shape[0], :] = data_ref[...]
        begin += data_ref.shape[0]


def column_chunks(blocks, order):
    rows = sum(block.shape[0] for block in blocks)
    count = order.shape[0]
    chunk = blocks[0].shape[1] // count
    return pl.pallas_call(
        column_kernel,
        grid_spec=pltpu.PrefetchScalarGridSpec(
            num_scalar_prefetch=1,
            grid=(count,),
            in_specs=[
                pl.BlockSpec((block.shape[0], chunk), lambda r, order_ref: (0, order_ref[r]))
                for block in blocks
            ],
            out_specs=pl.BlockSpec((rows, chunk), lambda r, order_ref: (0, r)),
        ),
        out_shape=jax.ShapeDtypeStruct((rows, count * chunk), blocks[0].dtype),
        cost_estimate=pl.CostEstimate(
            flops=0, bytes_accessed=4 * rows * count * chunk, transcendentals=0
        ),
        name="column_chunks",
    )(order, *blocks)


def away_and_near(blocks, axis):
    count = lax.axis_size(axis)
    index = jnp.arange(count, dtype=jnp.int32).reshape(count // 2, 2)
    order = lax.axis_index(axis) ^ jnp.concatenate([index[:, 1], index[:, 0]])
    return column_chunks(blocks, order)


def halving_send(part_of, columns, axis, parts):
    half = columns.shape[1] // 2
    away, near = columns[:, :half], columns[:, half:]
    leaving = [part_of(away, p).astype(BF16) for p in range(parts)]
    return leaving, near, [swap(block, axis, 0) for block in leaving]


def halving_near(part_of, near, arrived, tie):
    near, *arrived = lax.optimization_barrier((near, *arrived, tie))[:-1]
    return [(part_of(near, p) + block.astype(F32)).astype(BF16) for p, block in enumerate(arrived)]


def halving_rest(sums, axis, dimension, tie=None):
    count = lax.axis_size(axis)
    results = []
    for p, near_sum in enumerate(sums):
        steps = list(bits_of(axis))[1:]
        if p % 2:
            steps.reverse()
        held = dict(zip(range(0, count, 2), jnp.split(near_sum, count // 2, axis=dimension)))
        for turn, bit in enumerate(steps):
            leaving = [r for r in held if r >> bit & 1]
            staying = [r for r in held if not r >> bit & 1]
            sent = jnp.concatenate([held[r].astype(BF16) for r in leaving], axis=dimension)
            come = swap(sent, axis, bit)
            if turn == 0 and tie is not None:
                come = after(come, tie)
            for r, block in zip(leaving, jnp.split(come, len(leaving), axis=dimension)):
                held[r ^ (1 << bit)] = (
                    held[r ^ (1 << bit)].astype(BF16).astype(F32) + block.astype(F32)
                )
            held = {r: held[r] for r in staying}
        results.append(held[0])
    return results


def select_kernel(rank_ref, data_ref, out_ref):
    experts, _, slots, _ = out_ref.shape
    tokens = data_ref.shape[1]
    slot = lax.broadcasted_iota(jnp.int32, (slots, tokens), 0)
    hot = jnp.concatenate(
        [jnp.where(slot == rank_ref[e, 0], 1.0, 0.0).astype(BF16) for e in range(experts)], axis=0
    )
    rows = jnp.dot(hot, data_ref[0], preferred_element_type=F32).astype(BF16)
    for e in range(experts):
        out_ref[e, 0] = rows[e * slots : (e + 1) * slots]


def select_rows(rank, data, slots):
    experts, blocks, tokens = rank.shape
    width = data.shape[-1]
    return pl.pallas_call(
        select_kernel,
        grid=(blocks,),
        in_specs=[
            pl.BlockSpec((experts, 1, 1, tokens), lambda s: (0, s, 0, 0)),
            pl.BlockSpec((1, tokens, width), lambda s: (s, 0, 0)),
        ],
        out_specs=pl.BlockSpec((experts, 1, slots, width), lambda s: (0, s, 0, 0)),
        out_shape=jax.ShapeDtypeStruct((experts, blocks, slots, width), BF16),
        cost_estimate=pl.CostEstimate(
            flops=2 * experts * blocks * slots * tokens * width,
            bytes_accessed=2 * (experts * blocks * slots + blocks * tokens) * width,
            transcendentals=0,
        ),
        name="select_rows",
    )(rank.reshape(experts, blocks, 1, tokens), data.reshape(blocks, tokens, width))


def spread_kernel(rank_ref, weight_ref, rows_ref, *refs):
    out_ref = refs[-1]
    experts, _, slots, _ = rows_ref.shape
    tokens = out_ref.shape[1]
    slot = lax.broadcasted_iota(jnp.int32, (tokens, slots), 1)
    total = None
    for e in range(experts):
        hot = jnp.where(slot == rank_ref[e, 0], weight_ref[e, 0], 0.0).astype(BF16)
        part = jnp.dot(hot, rows_ref[e, 0], preferred_element_type=F32)
        total = part if total is None else total + part
    if len(refs) == 3:
        total = total + refs[0][0] * refs[1][0].astype(F32)
    out_ref[0] = total.astype(BF16)


def spread_rows(rank, weight, rows, scale=None, addend=None):
    experts, blocks, tokens = rank.shape
    slots, width = rows.shape[2:]
    column = pl.BlockSpec((experts, 1, tokens, 1), lambda s: (0, s, 0, 0))
    in_specs = [
        column,
        column,
        pl.BlockSpec((experts, 1, slots, width), lambda s: (0, s, 0, 0)),
    ]
    operands = [
        rank.reshape(experts, blocks, tokens, 1),
        weight.reshape(experts, blocks, tokens, 1),
        rows,
    ]
    if addend is not None:
        in_specs += [
            pl.BlockSpec((1, tokens, 1), lambda s: (s, 0, 0)),
            pl.BlockSpec((1, tokens, width), lambda s: (s, 0, 0)),
        ]
        operands += [scale.reshape(blocks, tokens, 1), addend.reshape(blocks, tokens, width)]
    return pl.pallas_call(
        spread_kernel,
        grid=(blocks,),
        in_specs=in_specs,
        out_specs=pl.BlockSpec((1, tokens, width), lambda s: (s, 0, 0)),
        out_shape=jax.ShapeDtypeStruct((blocks, tokens, width), BF16),
        cost_estimate=pl.CostEstimate(
            flops=2 * experts * blocks * slots * tokens * width,
            bytes_accessed=(2 * experts * blocks * slots + 4 * blocks * tokens) * width,
            transcendentals=0,
        ),
        name="spread_rows",
    )(*operands).reshape(blocks * tokens, width)


def expert_up_kernel(rows_ref, gate_ref, up_ref, gate_out, up_out, hidden_out):
    gate = jnp.dot(rows_ref[0], gate_ref[0], preferred_element_type=F32)
    up = jnp.dot(rows_ref[0], up_ref[0], preferred_element_type=F32)
    gate_out[0] = gate.astype(BF16)
    up_out[0] = up.astype(BF16)
    hidden_out[0] = (gate * jax.nn.sigmoid(gate) * up).astype(BF16)


def expert_specs(experts, rows, inner):
    return (
        pl.BlockSpec((1, rows, WIDE), lambda e, k: (e, 0, k)),
        pl.BlockSpec((1, rows, inner), lambda e, k: (e, 0, 0)),
        pl.BlockSpec((1, WIDE, inner), lambda e, k: (e, k, 0)),
        pl.BlockSpec((1, inner, WIDE), lambda e, k: (e, 0, k)),
    )


def expert_cost(experts, rows, width, inner, weights):
    return pl.CostEstimate(
        flops=2 * weights * experts * rows * width * inner,
        bytes_accessed=2 * experts * (weights * width * inner + rows * (width + 3 * inner)),
        transcendentals=0,
    )


def expert_up_all(rows, gate_weight, up_weight):
    experts, count, width = rows.shape
    inner = gate_weight.shape[2]
    half = count // 2
    weight = pl.BlockSpec((1, width, inner), lambda e, i: (e, 0, 0))
    out = pl.BlockSpec((1, half, inner), lambda e, i: (e, i, 0))
    return pl.pallas_call(
        expert_up_kernel,
        grid=(experts, 2),
        in_specs=[pl.BlockSpec((1, half, width), lambda e, i: (e, i, 0)), weight, weight],
        out_specs=[out] * 3,
        out_shape=[jax.ShapeDtypeStruct((experts, count, inner), BF16)] * 3,
        cost_estimate=expert_cost(experts, count, width, inner, 2),
        name="expert_up",
    )(rows, gate_weight, up_weight)


def expert_down_kernel(hidden_ref, down_ref, out_ref):
    out_ref[0] = jnp.dot(hidden_ref[0], down_ref[0], preferred_element_type=F32).astype(BF16)


def expert_down_all(hidden, down_weight):
    experts, count, inner = hidden.shape
    width = down_weight.shape[2]
    by_width, by_inner, _, weight = expert_specs(experts, count, inner)
    return pl.pallas_call(
        expert_down_kernel,
        grid=(experts, width // WIDE),
        in_specs=[by_inner, weight],
        out_specs=by_width,
        out_shape=jax.ShapeDtypeStruct((experts, count, width), BF16),
        cost_estimate=expert_cost(experts, count, width, inner, 1),
        name="expert_down",
    )(hidden, down_weight)


def expert_back_kernel(
    grad_ref, down_ref, gate_ref, up_ref, hidden_ref, share_ref,
    gate_out, up_out, gated_out, dot_out
):
    plain = times_trans(grad_ref[0], down_ref[0])
    hidden = hidden_ref[0].astype(F32)
    share = share_ref[0]
    dot_out[0] = jnp.sum(plain * hidden, axis=1, keepdims=True)
    gated_out[0] = (share * hidden).astype(BF16)
    grad_hidden = share * plain
    gate = gate_ref[0].astype(F32)
    sig = jax.nn.sigmoid(gate)
    up_out[0] = (grad_hidden * gate * sig).astype(BF16)
    slope = sig * (1.0 + gate * (1.0 - sig))
    gate_out[0] = (grad_hidden * up_ref[0].astype(F32) * slope).astype(BF16)


def expert_back_all(grad_rows, down_weight, gate, up, hidden, share):
    experts, count, width = grad_rows.shape
    inner = down_weight.shape[1]
    half = count // 2
    own = pl.BlockSpec((1, half, inner), lambda e, i: (e, i, 0))
    one = pl.BlockSpec((1, half, 1), lambda e, i: (e, i, 0))
    return pl.pallas_call(
        expert_back_kernel,
        grid=(experts, 2),
        in_specs=[
            pl.BlockSpec((1, half, width), lambda e, i: (e, i, 0)),
            pl.BlockSpec((1, inner, width), lambda e, i: (e, 0, 0)),
            own,
            own,
            own,
            one,
        ],
        out_specs=[own, own, own, one],
        out_shape=[jax.ShapeDtypeStruct((experts, count, inner), BF16)] * 3
        + [jax.ShapeDtypeStruct((experts, count, 1), F32)],
        cost_estimate=expert_cost(experts, count, width, inner, 1),
        name="expert_back",
    )(grad_rows, down_weight, gate, up, hidden, share)


def expert_in_kernel(grad_gate_ref, grad_up_ref, gate_ref, up_ref, out_ref):
    out_ref[0] = (
        times_trans(grad_gate_ref[0], gate_ref[0]) + times_trans(grad_up_ref[0], up_ref[0])
    ).astype(BF16)


def expert_in_all(grad_gate, grad_up, gate_weight, up_weight):
    experts, count, inner = grad_gate.shape
    width = gate_weight.shape[1]
    by_width, by_inner, weight, _ = expert_specs(experts, count, inner)
    return pl.pallas_call(
        expert_in_kernel,
        grid=(experts, width // WIDE),
        in_specs=[by_inner, by_inner, weight, weight],
        out_specs=by_width,
        out_shape=jax.ShapeDtypeStruct((experts, count, width), BF16),
        cost_estimate=expert_cost(experts, count, width, inner, 2),
        name="expert_in",
    )(grad_gate, grad_up, gate_weight, up_weight)


def project_kernel(rows_ref, weight_ref, bias_ref, cosine_ref, sine_ref, held_ref, out_ref):
    head_size = cosine_ref.shape[1]
    sums = (
        jnp.dot(rows_ref[...], weight_ref[...], preferred_element_type=F32) + bias_ref[0:1, :]
    )
    for part in range(3):
        values = sums[:, part * head_size : (part + 1) * head_size]
        if part < 2:
            turned = pltpu.roll(values, head_size // 2, 1)
            values = values * cosine_ref[...] + turned * sine_ref[...]
        out_ref[:, part * head_size : (part + 1) * head_size] = values.astype(BF16)


def project(rows, weight, bias, cosine, sine, held, k):
    count, width = rows.shape
    head_size = cosine.shape[1]
    columns = 3 * head_size
    total = weight.shape[1]
    return pl.pallas_call(
        project_kernel,
        grid=(total // columns,),
        in_specs=[
            pl.BlockSpec((count, width), lambda h: (0, 0)),
            pl.BlockSpec((width, columns), lambda h: (0, h)),
            pl.BlockSpec((8, columns), lambda h: (0, h)),
            pl.BlockSpec((count, head_size), lambda h: (k, 0)),
            pl.BlockSpec((count, head_size), lambda h: (k, 0)),
            pl.BlockSpec(memory_space=pl.ANY),
        ],
        out_specs=pl.BlockSpec((count, columns), lambda h: (k, h)),
        out_shape=jax.ShapeDtypeStruct(held.shape, BF16),
        input_output_aliases={5: 0},
        cost_estimate=pl.CostEstimate(
            flops=2 * count * width * total,
            bytes_accessed=2 * (count * width + width * total + count * total),
            transcendentals=0,
        ),
        name="project",
    )(rows, weight, bias, cosine, sine, held)


def attend_kernel(q_ref, k_ref, v_ref, mask_ref, out_ref, *, score_scale):
    scores = (
        lax.dot_general(
            q_ref[...], k_ref[...], (((1,), (1,)), ((), ())), preferred_element_type=F32
        )
        * (score_scale * LOG2E)
        + mask_ref[...]
    )
    exponent = jnp.exp2(scores - jnp.max(scores, axis=1, keepdims=True))
    weights = exponent * (1.0 / jnp.sum(exponent, axis=1, keepdims=True))
    out_ref[...] = jnp.dot(
        weights.astype(BF16), v_ref[...], preferred_element_type=F32
    ).astype(BF16)


def attend(qkv, mask, count, head_size, k):
    length, total = qkv.shape
    heads = total // (3 * head_size)
    return pl.pallas_call(
        lambda *refs: attend_kernel(*refs, score_scale=1.0 / math.sqrt(head_size)),
        grid=(heads,),
        in_specs=[
            pl.BlockSpec((count, head_size), lambda h: (k, 3 * h)),
            pl.BlockSpec((length, head_size), lambda h: (0, 3 * h + 1)),
            pl.BlockSpec((length, head_size), lambda h: (0, 3 * h + 2)),
            pl.BlockSpec((count, length), lambda h: (k, 0)),
        ],
        out_specs=pl.BlockSpec((count, head_size), lambda h: (0, h)),
        out_shape=jax.ShapeDtypeStruct((count, heads * head_size), BF16),
        cost_estimate=pl.CostEstimate(
            flops=4 * count * length * heads * head_size,
            bytes_accessed=4 * (count + length) * heads * head_size,
            transcendentals=heads * count * length,
        ),
        name="attend",
    )(qkv, qkv, qkv, mask)


def attend_back_block(q_ref, k_ref, v_ref, grad_ref, mask_ref, cosine_ref, sine_ref):
    score_scale = 1.0 / math.sqrt(q_ref.shape[1])
    scores = (
        lax.dot_general(
            k_ref[...], q_ref[...], (((1,), (1,)), ((), ())), preferred_element_type=F32
        )
        * (score_scale * LOG2E)
        + mask_ref[...]
    )
    exponent = jnp.exp2(scores - jnp.max(scores, axis=0, keepdims=True))
    probs = exponent * (1.0 / jnp.sum(exponent, axis=0, keepdims=True))
    grad_probs = lax.dot_general(
        v_ref[...], grad_ref[...], (((1,), (1,)), ((), ())), preferred_element_type=F32
    )
    centre = jnp.sum(probs * grad_probs, axis=0, keepdims=True)
    grad_scores = (probs * (grad_probs - centre)).astype(BF16)
    grad_keys = jnp.dot(grad_scores, q_ref[...], preferred_element_type=F32) * score_scale
    grad_values = jnp.dot(probs.astype(BF16), grad_ref[...], preferred_element_type=F32)
    grad_queries = lax.dot_general(
        grad_scores, k_ref[...], (((0,), (0,)), ((), ())), preferred_element_type=F32
    )
    return turn_back(grad_queries * score_scale, cosine_ref, sine_ref), grad_keys, grad_values


def turn_back(values, cosine_ref, sine_ref):
    turned = pltpu.roll(values, values.shape[1] // 2, 1)
    return (values * cosine_ref[...] - turned * sine_ref[...]).astype(BF16)


def attend_back_some_kernel(
    q_ref, k_ref, v_ref, grad_ref, mask_ref, cosine_ref, sine_ref, gq_ref, gk_ref, gv_ref
):
    gq_ref[...], grad_keys, grad_values = attend_back_block(
        q_ref, k_ref, v_ref, grad_ref, mask_ref, cosine_ref, sine_ref
    )

    @pl.when(pl.program_id(1) == 0)
    def _():
        gk_ref[...] = grad_keys
        gv_ref[...] = grad_values

    @pl.when(pl.program_id(1) > 0)
    def _():
        gk_ref[...] += grad_keys
        gv_ref[...] += grad_values


def attend_back_last_kernel(
    q_ref, k_ref, v_ref, grad_ref, mask_ref, cosine_ref, sine_ref,
    all_cosine_ref, all_sine_ref, some_gq_ref, some_gk_ref, some_gv_ref, out_ref
):
    head_size = q_ref.shape[1]
    before = some_gq_ref.shape[0]
    grad_queries, grad_keys, grad_values = attend_back_block(
        q_ref, k_ref, v_ref, grad_ref, mask_ref, cosine_ref, sine_ref
    )
    out_ref[:before, :head_size] = some_gq_ref[...]
    out_ref[before:, :head_size] = grad_queries
    out_ref[:, head_size : 2 * head_size] = turn_back(
        some_gk_ref[...] + grad_keys, all_cosine_ref, all_sine_ref
    )
    out_ref[:, 2 * head_size :] = (some_gv_ref[...] + grad_values).astype(BF16)


def attend_back(qkv, grad_out, mask, cosine, sine, count, some=None):
    length, total = qkv.shape
    head_size = cosine.shape[1]
    heads = total // (3 * head_size)
    blocks = grad_out.shape[0] // count
    first = 0 if some is None else length // count - 1
    in_specs = [
        pl.BlockSpec((count, head_size), lambda h, i: (i + first, 3 * h)),
        pl.BlockSpec((length, head_size), lambda h, i: (0, 3 * h + 1)),
        pl.BlockSpec((length, head_size), lambda h, i: (0, 3 * h + 2)),
        pl.BlockSpec((count, head_size), lambda h, i: (i, h)),
        pl.BlockSpec((length, count), lambda h, i: (0, i + first)),
        pl.BlockSpec((count, head_size), lambda h, i: (i + first, 0)),
        pl.BlockSpec((count, head_size), lambda h, i: (i + first, 0)),
    ]
    cost = pl.CostEstimate(
        flops=10 * blocks * count * length * heads * head_size,
        bytes_accessed=20 * length * heads * head_size,
        transcendentals=heads * blocks * count * length,
    )
    whole = pl.BlockSpec((length, head_size), lambda h, i: (0, h))
    operands = [qkv, qkv, qkv, grad_out, mask, cosine, sine]
    if some is None:
        wide = jax.ShapeDtypeStruct((length, heads * head_size), F32)
        return pl.pallas_call(
            attend_back_some_kernel,
            grid=(heads, blocks),
            in_specs=in_specs,
            out_specs=[
                pl.BlockSpec((count, head_size), lambda h, i: (i, h)),
                whole,
                whole,
            ],
            out_shape=[
                jax.ShapeDtypeStruct((blocks * count, heads * head_size), BF16),
                wide,
                wide,
            ],
            cost_estimate=cost,
            name="attend_back_some",
        )(*operands)
    everywhere = pl.BlockSpec((length, head_size), lambda h, i: (0, 0))
    return pl.pallas_call(
        attend_back_last_kernel,
        grid=(heads, 1),
        in_specs=in_specs
        + [
            everywhere,
            everywhere,
            pl.BlockSpec((some[0].shape[0], head_size), lambda h, i: (0, h)),
            whole,
            whole,
        ],
        out_specs=pl.BlockSpec((length, 3 * head_size), lambda h, i: (0, h)),
        out_shape=jax.ShapeDtypeStruct((length, total), BF16),
        cost_estimate=cost,
        name="attend_back_last",
    )(*operands, cosine, sine, *some)


def scatter_raw(values, dimension):
    return lax.psum_scatter(values.astype(BF16), "grp", scatter_dimension=dimension, tiled=True)


def per_device(
    tokens,
    attn_norm,
    query_weight,
    key_weight,
    value_weight,
    query_bias,
    key_bias,
    value_bias,
    out_weight,
    ffn_norm,
    router_weight,
    shared_switch,
    shared_gate,
    shared_up,
    shared_down,
    expert_gate,
    expert_up,
    expert_down,
    routes,
    pieces,
    documents,
    cotangent,
):
    ep_count = lax.axis_size("ep")
    grp_count = lax.axis_size("grp")
    place = lax.axis_index("ep")
    row_count, own_count, model_width = tokens.shape
    length = own_count * ep_count
    heads_here = query_bias.shape[0]
    head_size = query_bias.shape[1] * grp_count
    head_width = heads_here * head_size
    hidden_width = shared_gate.shape[1]
    experts_here = expert_gate.shape[0]
    experts_all = experts_here * ep_count
    top_count = routes.shape[2]
    capacity = (own_count * top_count // experts_all * 5 + 3) // 4
    order = (place - jnp.arange(ep_count, dtype=jnp.int32)) % ep_count

    w_qkv = lax.all_gather(
        by_head(query_weight, key_weight, value_weight, heads_here),
        "grp",
        axis=0,
        tiled=True,
    )
    small_sizes = [
        attn_norm.size,
        query_bias.size,
        key_bias.size,
        value_bias.size,
        ffn_norm.size,
        router_weight.size,
        shared_switch.size,
    ]
    small = gather_small(
        jnp.concatenate(
            [
                part.reshape(-1)
                for part in (
                    attn_norm,
                    query_bias,
                    key_bias,
                    value_bias,
                    ffn_norm,
                    router_weight,
                    shared_switch,
                )
            ]
        ),
        "grp",
    )
    pieces_of_small = []
    begin = 0
    for size in small_sizes:
        pieces_of_small.append(small[:, begin : begin + size])
        begin += size
    gain_first = pieces_of_small[0].reshape(-1).astype(F32)
    biases = [
        part.reshape(grp_count, heads_here, -1).transpose(1, 0, 2).reshape(1, -1)
        for part in pieces_of_small[1:4]
    ]
    bias_qkv = jnp.broadcast_to(
        by_head(*biases, heads_here).astype(F32), (8, 3 * head_width)
    )
    gain_second = pieces_of_small[4].reshape(-1).astype(F32)
    w_router = pieces_of_small[5].reshape(model_width, experts_all)
    w_switch = pieces_of_small[6].reshape(model_width)
    w_out = lax.all_gather(out_weight, "grp", axis=1, tiled=True)
    w_sgu = lax.all_gather(
        jnp.concatenate([shared_gate, shared_up], axis=1), "grp", axis=0, tiled=True
    )
    w_sdown = lax.all_gather(shared_down, "grp", axis=1, tiled=True)

    tokens_own = tokens.reshape(own_count, model_width)
    grad_own_low = cotangent.reshape(own_count, model_width)
    x_blocks = ring_gather(tokens_own, "ep")
    routes_own = routes.reshape(own_count, top_count).T
    chosen = jnp.stack(
        [routes_own]
        + [
            lax.ppermute(routes_own, "ep", [(j, (j + k) % ep_count) for j in range(ep_count)])
            for k in range(1, ep_count)
        ]
    )
    own_places = jnp.arange(own_count, dtype=jnp.int32)
    position = (order[:, None] * own_count + own_places[None, :]).reshape(length)
    piece = jnp.take(pieces.reshape(ep_count, own_count), order, axis=0).reshape(length)
    document = jnp.take(documents.reshape(ep_count, own_count), order, axis=0).reshape(length)
    allowed = (document[:, None] == document[None, :]) & (
        (position[:, None] >= position[None, :])
        | ((piece[:, None] == piece[None, :]) & (piece[:, None] > 0))
    )
    allowed_by_key = (document[:, None] == document[None, :]) & (
        (position[:, None] <= position[None, :])
        | ((piece[:, None] == piece[None, :]) & (piece[:, None] > 0))
    )
    mask = jnp.where(allowed, 0.0, NEG)
    mask_by_key = jnp.where(allowed_by_key, 0.0, NEG)
    cosine_table, sine_table = rotary_tables(position, head_size)
    qkv = jnp.zeros((length, 3 * head_width), BF16)
    h_parts = []
    for k, block in enumerate(x_blocks):
        wide = after(block, qkv).astype(F32)
        h_parts.append((wide * inverse_rms(wide) * gain_first).astype(BF16))
        qkv = project(h_parts[k], w_qkv, bias_qkv, cosine_table, sine_table, qkv, k)
    qkv, chosen = lax.optimization_barrier((qkv, chosen))
    columns_h_one = away_and_near(h_parts, "grp")
    o_parts = [None] * ep_count
    ready = qkv
    for step in range(ep_count):
        k = (step + 1) % ep_count
        o_parts[k] = attend(ready, mask, own_count, head_size, k)
        if step == 1:
            ready = after(ready, columns_h_one, mask_by_key)
        ready, o_parts[k] = lax.optimization_barrier((ready, o_parts[k]))
    o_low = jnp.concatenate(o_parts, axis=0)

    def block_of(values, k):
        return values[k * own_count : (k + 1) * own_count]

    attn_own = ring_reduce(lambda k: times(o_parts[k], w_out), "ep")
    x_own = tokens_own.astype(F32)
    x1_own = x_own + attn_own
    inverse_two = inverse_rms(x1_own)
    hat_two = x1_own * inverse_two
    h_own = (hat_two * gain_second).astype(BF16)
    h_blocks = ring_gather(h_own, "ep")
    h_two = jnp.concatenate(h_blocks, axis=0)
    logits = times(h_two, jnp.concatenate([w_router, w_switch[:, None]], axis=1))
    route_probs = jax.nn.softmax(logits[:, :experts_all], axis=-1)
    switch = jax.nn.sigmoid(logits[:, experts_all])
    expert_ids = place * experts_here + jnp.arange(experts_here, dtype=jnp.int32)
    named = jnp.any(chosen[None] == expert_ids[:, None, None, None], axis=2)
    before = (own_places[:, None] < own_places[None, :]).astype(BF16)
    rank = jnp.einsum("est,tu->esu", named.astype(BF16), before, preferred_element_type=F32).astype(
        jnp.int32
    )
    rank = jnp.where(named & (rank < capacity), rank, -1)
    local_probs = lax.dynamic_slice_in_dim(route_probs, place * experts_here, experts_here, 1)
    local_probs = local_probs.reshape(ep_count, own_count, experts_here).transpose(2, 0, 1)
    hot = (
        rank[:, :, None, :] == jnp.arange(capacity, dtype=jnp.int32)[None, None, :, None]
    )
    gate_slot = jnp.sum(jnp.where(hot, local_probs[:, :, None, :], 0.0), axis=-1)
    slot_shape = (experts_here, ep_count * capacity, model_width)
    gate_rows = gate_slot.reshape(experts_here, ep_count * capacity, 1)

    s_pre = times(h_two, w_sgu)
    s_gate = s_pre[:, :hidden_width]
    s_up = s_pre[:, hidden_width:]
    sig_shared = jax.nn.sigmoid(s_gate)
    silu_shared = s_gate * sig_shared
    s_hidden = (silu_shared * s_up).astype(BF16)
    s_part = times(s_hidden, w_sdown).astype(BF16)
    grad_blocks = lax.all_gather(after(grad_own_low, h_blocks[-1]), "ep", axis=0)
    flat_rows = select_rows(rank, after(h_two, s_part), capacity)
    flat_rows = flat_rows.reshape(slot_shape)
    gate_pre, up_pre, hidden = expert_up_all(flat_rows, expert_gate, expert_up)
    result = expert_down_all(hidden, expert_down)
    grad_blocks = after(grad_blocks, result)
    grad_low = jnp.take(grad_blocks, order, axis=0).reshape(length, model_width)
    grad_all = grad_low.astype(F32)
    grad_sout = (switch[:, None] * grad_all).astype(BF16)
    grad_shidden = times_trans(grad_sout, w_sdown)
    slope_shared = sig_shared * (1.0 + s_gate * (1.0 - sig_shared))
    grad_s = jnp.concatenate(
        [
            (grad_shidden * s_up * slope_shared).astype(BF16),
            (grad_shidden * silu_shared).astype(BF16),
        ],
        axis=1,
    )
    row_shape = (experts_here, ep_count, capacity, model_width)
    y_part = spread_rows(rank, local_probs, result.reshape(row_shape), switch, s_part)
    y_first = block_of(y_part, 1 % ep_count)
    part_sdown = inner_rows(s_hidden, after(grad_sout, grad_s)).astype(BF16)
    part_sgu = inner_rows(after(h_two, part_sdown), grad_s).astype(BF16)
    raw_sdown = scatter_raw(part_sdown, 1)
    raw_sgu = scatter_raw(part_sgu, 0)
    grad_rows = select_rows(
        rank, after(grad_low, y_first, part_sdown, part_sgu), capacity
    ).reshape(slot_shape)
    grad_gate_pre, grad_up_pre, hidden_gated, grad_gate = expert_back_all(
        grad_rows, expert_down, gate_pre, up_pre, hidden, gate_rows
    )

    routed = []

    def beside_y(step, sent):
        if step == 1:
            return [grad_gate_pre]
        if step == 2:
            part = jnp.einsum(
                "erf,erd->efd", after(hidden_gated, sent), grad_rows, preferred_element_type=F32
            )
            routed.append(part.astype(BF16))
            return routed[:]
        if step == 3:
            routed.append(
                expert_in_all(
                    after(grad_gate_pre, routed[0], sent), grad_up_pre, expert_gate, expert_up
                )
            )
            return routed[1:]
        return []

    layer_own = x1_own + ring_reduce(lambda k: block_of(y_part, k), "ep", y_first, beside_y)
    part_edown, grad_inputs = routed
    raw_edown = scatter_raw(part_edown, 2)
    shared_dot = jnp.sum(grad_all * s_part.astype(F32), axis=-1).reshape(1, ep_count, own_count)
    grad_probs_part = jnp.sum(
        jnp.where(
            hot, grad_gate.reshape(experts_here, ep_count, capacity)[:, :, :, None], 0.0
        ),
        axis=2,
    )
    scalars = jnp.concatenate([grad_probs_part, shared_dot], axis=0)
    home = [scalars[:, 0]]
    for k in range(1, ep_count):
        home.append(
            lax.ppermute(scalars[:, k], "ep", [(j, (j - k) % ep_count) for j in range(ep_count)])
        )
    grad_inputs, layer_own, *home = lax.optimization_barrier((grad_inputs, layer_own, *home))
    home = jnp.stack(home)
    grad_moe = spread_rows(rank, jnp.ones_like(local_probs), grad_inputs.reshape(row_shape))

    grad_probs = jnp.take(
        home[:, :experts_here],
        (jnp.arange(ep_count, dtype=jnp.int32) - place) % ep_count,
        axis=0,
    )
    grad_probs = grad_probs.reshape(experts_all, own_count).T
    probs_own = route_probs[:own_count]
    switch_own = switch[:own_count]
    grad_logit = (
        probs_own * (grad_probs - jnp.sum(probs_own * grad_probs, axis=-1, keepdims=True))
    ).astype(BF16)
    grad_switch = (
        jnp.sum(home[:, experts_here], axis=0) * switch_own * (1.0 - switch_own)
    ).astype(BF16)

    w_small = jnp.concatenate([w_router, w_switch[:, None]], axis=1)
    grad_small = jnp.concatenate([grad_logit, grad_switch[:, None]], axis=1)
    layer_out = layer_own.reshape(row_count, own_count, model_width).astype(BF16)

    def grad_h2_part(k):
        return times_trans(block_of(grad_s, k), w_sgu) + block_of(grad_moe, k)

    grad_h2_first = grad_h2_part(1 % ep_count).astype(BF16)
    forms = (
        ("erd,erf->edf", flat_rows, grad_gate_pre),
        ("erd,erf->edf", flat_rows, grad_up_pre),
    )
    expert_raw = []

    def expert_part(sent):
        form, left_side, right_side = forms[len(expert_raw)]
        left_side, right_side, _ = lax.optimization_barrier((left_side, right_side, sent))
        part = jnp.einsum(form, left_side, right_side, preferred_element_type=F32).astype(BF16)
        expert_raw.append(scatter_raw(part, 1))
        return part

    def beside_h2(step, sent):
        return {1: [raw_sdown], 2: [expert_part, raw_sgu], 3: [expert_part]}.get(step, [])

    grad_h2 = ring_reduce(
        grad_h2_part,
        "ep",
        grad_h2_first,
        lambda step, sent: [
            item(sent) if callable(item) else item for item in beside_h2(step, sent)
        ],
        times_trans(grad_s[2 * own_count :], w_sgu) + grad_moe[2 * own_count :],
    ) + times_trans(grad_small, w_small)
    weighted = grad_h2 * gain_second
    grad_x1 = grad_own_low.astype(F32) + inverse_two * (
        weighted - hat_two * jnp.mean(weighted * hat_two, axis=-1, keepdims=True)
    )
    grad_x1_low = grad_x1.astype(BF16)
    while len(expert_raw) < len(forms):
        expert_part(grad_x1_low)
    grad_attn_blocks = ring_gather(grad_x1_low, "ep")

    gain_two_part = jnp.sum(grad_h2 * hat_two, axis=0)
    small_part = jnp.concatenate([inner_rows(grad_small, h_own), gain_two_part[None, :]], axis=0)
    small_grp = sum_all(small_part, "grp")
    back_tables = (mask_by_key, cosine_table, sine_table, own_count)
    grad_o = [times_trans(block, w_out).astype(BF16) for block in grad_attn_blocks[:-1]]
    some_back = attend_back(after(qkv, small_grp), jnp.concatenate(grad_o, axis=0), *back_tables)
    last_block = after(grad_attn_blocks[-1], *some_back)
    grad_qkv = attend_back(
        qkv, times_trans(last_block, w_out).astype(BF16), *back_tables, some_back
    )
    chunk_width = model_width // grp_count
    grp_place = lax.axis_index("grp")
    qkv_half = 3 * head_width // 2
    grad_h1_first = times_trans(block_of(grad_qkv, 1 % ep_count), w_qkv).astype(BF16)

    def qkv_part(columns, p):
        return inner_rows(columns, grad_qkv[:, p * qkv_half : (p + 1) * qkv_half])

    def out_part(columns, p):
        return inner_rows(o_low[:, p * head_width // 2 : (p + 1) * head_width // 2], columns)

    qkv_left, qkv_columns, qkv_come = halving_send(
        qkv_part, after(columns_h_one, grad_h1_first), "grp", 2
    )
    near_sums = []
    out_sent = []

    def beside_h1(step, sent):
        if step == 1:
            return qkv_left
        if step == 2:
            columns_grad_attn = away_and_near(
                [after(block, sent) for block in grad_attn_blocks], "grp"
            )
            out_sent.extend(halving_send(out_part, columns_grad_attn, "grp", 2))
            return out_sent[0]
        if step == 3:
            near_sums.append(halving_near(qkv_part, qkv_columns, qkv_come, sent))
            near_sums.append(halving_near(out_part, out_sent[1], out_sent[2], near_sums[0][0]))
            return near_sums[0] + near_sums[1]
        return []

    grad_h1 = ring_reduce(
        lambda k: times_trans(block_of(grad_qkv, k), w_qkv),
        "ep",
        grad_h1_first,
        beside_h1,
        times_trans(grad_qkv[2 * own_count :], w_qkv),
    )
    qkv_near, out_near = near_sums
    grad_tokens = grad_x1 + norm_back(x_own, gain_first, grad_h1)
    tokens_grad = grad_tokens.reshape(row_count, own_count, model_width)
    gain_one_part = jnp.sum(grad_h1 * (x_own * inverse_rms(x_own)), axis=0)
    sum_sdown, sum_sgu, sum_edown, sum_egate, sum_eup = (
        raw.astype(F32) for raw in (raw_sdown, raw_sgu, raw_edown, *expert_raw)
    )
    gain_one_part = after(gain_one_part, sum_sdown, sum_sgu, sum_edown)
    last_part = jnp.concatenate([gain_one_part, jnp.sum(grad_qkv.astype(F32), axis=0)])[None, :]
    sum_qkv = jnp.concatenate(halving_rest(qkv_near, "grp", 0, last_part), axis=1)
    sum_out = jnp.concatenate(halving_rest(out_near, "grp", 1, last_part), axis=0)
    last_grp = sum_all(last_part, "grp")
    bias_width = head_size // grp_count
    sum_bias = lax.dynamic_slice_in_dim(
        last_grp[:, model_width:].reshape(3 * heads_here, head_size),
        grp_place * bias_width,
        bias_width,
        1,
    )
    small_sum = sum_all(
        lax.dynamic_slice_in_dim(
            jnp.concatenate([small_grp, last_grp[:, :model_width]], axis=0),
            grp_place * chunk_width,
            chunk_width,
            1,
        ),
        "ep",
    )

    def of_heads(values, part):
        begins = range(part * head_size, 3 * head_width, 3 * head_size)
        return jnp.concatenate([values[:, b : b + head_size] for b in begins], axis=1)

    return (
        layer_out,
        tokens_grad,
        small_sum[experts_all + 2],
        of_heads(sum_qkv, 0),
        of_heads(sum_qkv, 1),
        of_heads(sum_qkv, 2),
        sum_bias[0::3],
        sum_bias[1::3],
        sum_bias[2::3],
        sum_out,
        small_sum[experts_all + 1],
        small_sum[:experts_all].T,
        small_sum[experts_all],
        sum_sgu[:, :hidden_width],
        sum_sgu[:, hidden_width:],
        sum_sdown,
        sum_egate,
        sum_eup,
        sum_edown,
    )


def solution(mesh):
    return jax.shard_map(
        per_device,
        mesh=mesh,
        in_specs=(
            P("grp", "ep", None),
            P("grp"),
            P("grp", "ep"),
            P("grp", "ep"),
            P("grp", "ep"),
            P("ep", "grp"),
            P("ep", "grp"),
            P("ep", "grp"),
            P("ep", "grp"),
            P("grp"),
            P("grp", None),
            P("grp"),
            P("grp", "ep"),
            P("grp", "ep"),
            P("ep", "grp"),
            P("ep", None, None),
            P("ep", None, None),
            P("ep", None, None),
            P("grp", "ep", None),
            P("grp", None),
            P("grp", None),
            P("grp", "ep", None),
        ),
        out_specs=(
            P("grp", "ep", None),
            P("grp", "ep", None),
            P("grp"),
            P("grp", "ep"),
            P("grp", "ep"),
            P("grp", "ep"),
            P("ep", "grp"),
            P("ep", "grp"),
            P("ep", "grp"),
            P("ep", "grp"),
            P("grp"),
            P("grp", None),
            P("grp"),
            P("grp", "ep"),
            P("grp", "ep"),
            P("ep", "grp"),
            P("ep", "grp", None),
            P("ep", "grp", None),
            P("ep", None, "grp"),
        ),
        check_vma=False,
    )
```

```python
import math

import jax
import jax.numpy as jnp
from jax import lax
from jax.experimental import pallas as pl
from jax.experimental.pallas import tpu as pltpu
from jax.sharding import PartitionSpec as P

EPS = 1e-06
THETA = 1000000.0
NEG = -1e30
LOG2E = 1.4426950408889634
WIDE = 512
F32 = jnp.float32
BF16 = jnp.bfloat16


def inverse_rms(values):
    return lax.rsqrt(jnp.mean(values * values, axis=-1, keepdims=True) + EPS)


def norm_back(values, gain_vec, upstream):
    inverse = inverse_rms(values)
    scaled = values * inverse
    weighted = upstream * gain_vec
    return inverse * (weighted - scaled * jnp.mean(weighted * scaled, axis=-1, keepdims=True))


def rotary_tables(position, head_size):
    frequency = THETA ** (-(jnp.arange(head_size // 2, dtype=F32) * 2.0 / head_size))
    angle = position.astype(F32)[:, None] * frequency[None, :]
    cosine, sine = jnp.cos(angle), jnp.sin(angle)
    return (
        jnp.concatenate([cosine, cosine], axis=1),
        jnp.concatenate([-sine, sine], axis=1),
    )


def after(values, *others):
    return lax.optimization_barrier((values, *others))[0]


def by_head(queries, keys, values, heads):
    rows = queries.shape[0]
    parts = [part.reshape(rows, heads, -1) for part in (queries, keys, values)]
    return jnp.concatenate(parts, axis=2).reshape(rows, -1)


def inner_rows(left_side, right_side):
    return lax.dot_general(
        left_side, right_side, (((0,), (0,)), ((), ())), preferred_element_type=F32
    )


def times_trans(left_side, right_side):
    return lax.dot_general(
        left_side, right_side, (((1,), (1,)), ((), ())), preferred_element_type=F32
    )


def times(left_side, right_side):
    return jnp.dot(left_side, right_side, preferred_element_type=F32)


def ring_gather(own_block, axis):
    count = lax.axis_size(axis)
    pairs = [(j, (j + 1) % count) for j in range(count)]
    blocks = [own_block]
    for _ in range(count - 1):
        blocks.append(lax.ppermute(blocks[-1], axis, pairs))
    return blocks


def ring_reduce(part_of, axis, first=None, beside=None, middle=None):
    count = lax.axis_size(axis)
    pairs = [(j, (j + 1) % count) for j in range(count)]
    running = part_of(1 % count).astype(BF16) if first is None else first
    if middle is None:
        parts = [part_of((step + 1) % count) for step in range(1, count)]
    else:
        parts = [*jnp.split(middle, count - 2, axis=0), part_of(0)]
    parts = [lax.optimization_barrier(part) for part in parts]
    for step in range(1, count):
        arrived = lax.ppermute(running, axis, pairs)
        held = parts[step:] if middle is not None else parts[step : step + 1]
        if beside is not None:
            held = held + list(beside(step, running))
        part = after(parts[step - 1], *held) if held else parts[step - 1]
        running = arrived.astype(F32) + part
        if step < count - 1:
            running = running.astype(BF16)
    return running


def bits_of(axis):
    return range(lax.axis_size(axis).bit_length() - 1)


def swap(values, axis, bit):
    count = lax.axis_size(axis)
    return lax.ppermute(values, axis, [(j, j ^ (1 << bit)) for j in range(count)])


def sum_all(values, axis):
    for bit in bits_of(axis):
        values = values + swap(values, axis, bit)
    return values


def gather_small(values, axis):
    count = lax.axis_size(axis)
    blocks = values[None, :]
    for bit in bits_of(axis):
        blocks = jnp.concatenate([blocks, swap(blocks, axis, bit)], axis=0)
    index = jnp.arange(count, dtype=jnp.int32)
    apart = index[:, None] ^ lax.axis_index(axis)
    return times((apart == index[None, :]).astype(values.dtype), blocks).astype(values.dtype)


def column_kernel(order_ref, *refs):
    out_ref = refs[-1]
    begin = 0
    for data_ref in refs[:-1]:
        out_ref[begin : begin + data_ref.shape[0], :] = data_ref[...]
        begin += data_ref.shape[0]


def column_chunks(blocks, order):
    rows = sum(block.shape[0] for block in blocks)
    count = order.shape[0]
    chunk = blocks[0].shape[1] // count
    return pl.pallas_call(
        column_kernel,
        grid_spec=pltpu.PrefetchScalarGridSpec(
            num_scalar_prefetch=1,
            grid=(count,),
            in_specs=[
                pl.BlockSpec((block.shape[0], chunk), lambda r, order_ref: (0, order_ref[r]))
                for block in blocks
            ],
            out_specs=pl.BlockSpec((rows, chunk), lambda r, order_ref: (0, r)),
        ),
        out_shape=jax.ShapeDtypeStruct((rows, count * chunk), blocks[0].dtype),
        cost_estimate=pl.CostEstimate(
            flops=0, bytes_accessed=4 * rows * count * chunk, transcendentals=0
        ),
        name="column_chunks",
    )(order, *blocks)


def away_and_near(blocks, axis):
    count = lax.axis_size(axis)
    index = jnp.arange(count, dtype=jnp.int32).reshape(count // 2, 2)
    order = lax.axis_index(axis) ^ jnp.concatenate([index[:, 1], index[:, 0]])
    return column_chunks(blocks, order)


def halving_send(part_of, columns, axis, parts):
    half = columns.shape[1] // 2
    away, near = columns[:, :half], columns[:, half:]
    leaving = [part_of(away, p).astype(BF16) for p in range(parts)]
    return leaving, near, [swap(block, axis, 0) for block in leaving]


def halving_near(part_of, near, arrived, tie):
    near, *arrived = lax.optimization_barrier((near, *arrived, tie))[:-1]
    return [(part_of(near, p) + block.astype(F32)).astype(BF16) for p, block in enumerate(arrived)]


def halving_rest(sums, axis, dimension, tie=None):
    count = lax.axis_size(axis)
    results = []
    for p, near_sum in enumerate(sums):
        steps = list(bits_of(axis))[1:]
        if p % 2:
            steps.reverse()
        held = dict(zip(range(0, count, 2), jnp.split(near_sum, count // 2, axis=dimension)))
        for turn, bit in enumerate(steps):
            leaving = [r for r in held if r >> bit & 1]
            staying = [r for r in held if not r >> bit & 1]
            sent = jnp.concatenate([held[r].astype(BF16) for r in leaving], axis=dimension)
            come = swap(sent, axis, bit)
            if turn == 0 and tie is not None:
                come = after(come, tie)
            for r, block in zip(leaving, jnp.split(come, len(leaving), axis=dimension)):
                held[r ^ (1 << bit)] = (
                    held[r ^ (1 << bit)].astype(BF16).astype(F32) + block.astype(F32)
                )
            held = {r: held[r] for r in staying}
        results.append(held[0])
    return results


def select_kernel(rank_ref, data_ref, out_ref):
    experts, _, slots, _ = out_ref.shape
    tokens = data_ref.shape[1]
    slot = lax.broadcasted_iota(jnp.int32, (slots, tokens), 0)
    hot = jnp.concatenate(
        [jnp.where(slot == rank_ref[e, 0], 1.0, 0.0).astype(BF16) for e in range(experts)], axis=0
    )
    rows = jnp.dot(hot, data_ref[0], preferred_element_type=F32).astype(BF16)
    for e in range(experts):
        out_ref[e, 0] = rows[e * slots : (e + 1) * slots]


def select_rows(rank, data, slots):
    experts, blocks, tokens = rank.shape
    width = data.shape[-1]
    return pl.pallas_call(
        select_kernel,
        grid=(blocks,),
        in_specs=[
            pl.BlockSpec((experts, 1, 1, tokens), lambda s: (0, s, 0, 0)),
            pl.BlockSpec((1, tokens, width), lambda s: (s, 0, 0)),
        ],
        out_specs=pl.BlockSpec((experts, 1, slots, width), lambda s: (0, s, 0, 0)),
        out_shape=jax.ShapeDtypeStruct((experts, blocks, slots, width), BF16),
        cost_estimate=pl.CostEstimate(
            flops=2 * experts * blocks * slots * tokens * width,
            bytes_accessed=2 * (experts * blocks * slots + blocks * tokens) * width,
            transcendentals=0,
        ),
        name="select_rows",
    )(rank.reshape(experts, blocks, 1, tokens), data.reshape(blocks, tokens, width))


def spread_kernel(rank_ref, weight_ref, rows_ref, *refs):
    out_ref = refs[-1]
    experts, _, slots, _ = rows_ref.shape
    tokens = out_ref.shape[1]
    slot = lax.broadcasted_iota(jnp.int32, (tokens, slots), 1)
    total = None
    for e in range(experts):
        hot = jnp.where(slot == rank_ref[e, 0], weight_ref[e, 0], 0.0).astype(BF16)
        part = jnp.dot(hot, rows_ref[e, 0], preferred_element_type=F32)
        total = part if total is None else total + part
    if len(refs) == 3:
        total = total + refs[0][0] * refs[1][0].astype(F32)
    out_ref[0] = total.astype(BF16)


def spread_rows(rank, weight, rows, scale=None, addend=None):
    experts, blocks, tokens = rank.shape
    slots, width = rows.shape[2:]
    column = pl.BlockSpec((experts, 1, tokens, 1), lambda s: (0, s, 0, 0))
    in_specs = [
        column,
        column,
        pl.BlockSpec((experts, 1, slots, width), lambda s: (0, s, 0, 0)),
    ]
    operands = [
        rank.reshape(experts, blocks, tokens, 1),
        weight.reshape(experts, blocks, tokens, 1),
        rows,
    ]
    if addend is not None:
        in_specs += [
            pl.BlockSpec((1, tokens, 1), lambda s: (s, 0, 0)),
            pl.BlockSpec((1, tokens, width), lambda s: (s, 0, 0)),
        ]
        operands += [scale.reshape(blocks, tokens, 1), addend.reshape(blocks, tokens, width)]
    return pl.pallas_call(
        spread_kernel,
        grid=(blocks,),
        in_specs=in_specs,
        out_specs=pl.BlockSpec((1, tokens, width), lambda s: (s, 0, 0)),
        out_shape=jax.ShapeDtypeStruct((blocks, tokens, width), BF16),
        cost_estimate=pl.CostEstimate(
            flops=2 * experts * blocks * slots * tokens * width,
            bytes_accessed=(2 * experts * blocks * slots + 4 * blocks * tokens) * width,
            transcendentals=0,
        ),
        name="spread_rows",
    )(*operands).reshape(blocks * tokens, width)


def expert_up_kernel(rows_ref, gate_ref, up_ref, gate_out, up_out, hidden_out):
    gate = jnp.dot(rows_ref[0], gate_ref[0], preferred_element_type=F32)
    up = jnp.dot(rows_ref[0], up_ref[0], preferred_element_type=F32)
    gate_out[0] = gate.astype(BF16)
    up_out[0] = up.astype(BF16)
    hidden_out[0] = (gate * jax.nn.sigmoid(gate) * up).astype(BF16)


def expert_specs(experts, rows, inner):
    return (
        pl.BlockSpec((1, rows, WIDE), lambda e, k: (e, 0, k)),
        pl.BlockSpec((1, rows, inner), lambda e, k: (e, 0, 0)),
        pl.BlockSpec((1, WIDE, inner), lambda e, k: (e, k, 0)),
        pl.BlockSpec((1, inner, WIDE), lambda e, k: (e, 0, k)),
    )


def expert_cost(experts, rows, width, inner, weights):
    return pl.CostEstimate(
        flops=2 * weights * experts * rows * width * inner,
        bytes_accessed=2 * experts * (weights * width * inner + rows * (width + 3 * inner)),
        transcendentals=0,
    )


def expert_up_all(rows, gate_weight, up_weight):
    experts, count, width = rows.shape
    inner = gate_weight.shape[2]
    half = count // 2
    weight = pl.BlockSpec((1, width, inner), lambda e, i: (e, 0, 0))
    out = pl.BlockSpec((1, half, inner), lambda e, i: (e, i, 0))
    return pl.pallas_call(
        expert_up_kernel,
        grid=(experts, 2),
        in_specs=[pl.BlockSpec((1, half, width), lambda e, i: (e, i, 0)), weight, weight],
        out_specs=[out] * 3,
        out_shape=[jax.ShapeDtypeStruct((experts, count, inner), BF16)] * 3,
        cost_estimate=expert_cost(experts, count, width, inner, 2),
        name="expert_up",
    )(rows, gate_weight, up_weight)


def expert_down_kernel(hidden_ref, down_ref, out_ref):
    out_ref[0] = jnp.dot(hidden_ref[0], down_ref[0], preferred_element_type=F32).astype(BF16)


def expert_down_all(hidden, down_weight):
    experts, count, inner = hidden.shape
    width = down_weight.shape[2]
    by_width, by_inner, _, weight = expert_specs(experts, count, inner)
    return pl.pallas_call(
        expert_down_kernel,
        grid=(experts, width // WIDE),
        in_specs=[by_inner, weight],
        out_specs=by_width,
        out_shape=jax.ShapeDtypeStruct((experts, count, width), BF16),
        cost_estimate=expert_cost(experts, count, width, inner, 1),
        name="expert_down",
    )(hidden, down_weight)


def expert_back_kernel(
    grad_ref, down_ref, gate_ref, up_ref, hidden_ref, share_ref,
    gate_out, up_out, gated_out, dot_out
):
    plain = times_trans(grad_ref[0], down_ref[0])
    hidden = hidden_ref[0].astype(F32)
    share = share_ref[0]
    dot_out[0] = jnp.sum(plain * hidden, axis=1, keepdims=True)
    gated_out[0] = (share * hidden).astype(BF16)
    grad_hidden = share * plain
    gate = gate_ref[0].astype(F32)
    sig = jax.nn.sigmoid(gate)
    up_out[0] = (grad_hidden * gate * sig).astype(BF16)
    slope = sig * (1.0 + gate * (1.0 - sig))
    gate_out[0] = (grad_hidden * up_ref[0].astype(F32) * slope).astype(BF16)


def expert_back_all(grad_rows, down_weight, gate, up, hidden, share):
    experts, count, width = grad_rows.shape
    inner = down_weight.shape[1]
    half = count // 2
    own = pl.BlockSpec((1, half, inner), lambda e, i: (e, i, 0))
    one = pl.BlockSpec((1, half, 1), lambda e, i: (e, i, 0))
    return pl.pallas_call(
        expert_back_kernel,
        grid=(experts, 2),
        in_specs=[
            pl.BlockSpec((1, half, width), lambda e, i: (e, i, 0)),
            pl.BlockSpec((1, inner, width), lambda e, i: (e, 0, 0)),
            own,
            own,
            own,
            one,
        ],
        out_specs=[own, own, own, one],
        out_shape=[jax.ShapeDtypeStruct((experts, count, inner), BF16)] * 3
        + [jax.ShapeDtypeStruct((experts, count, 1), F32)],
        cost_estimate=expert_cost(experts, count, width, inner, 1),
        name="expert_back",
    )(grad_rows, down_weight, gate, up, hidden, share)


def expert_in_kernel(grad_gate_ref, grad_up_ref, gate_ref, up_ref, out_ref):
    out_ref[0] = (
        times_trans(grad_gate_ref[0], gate_ref[0]) + times_trans(grad_up_ref[0], up_ref[0])
    ).astype(BF16)


def expert_in_all(grad_gate, grad_up, gate_weight, up_weight):
    experts, count, inner = grad_gate.shape
    width = gate_weight.shape[1]
    by_width, by_inner, weight, _ = expert_specs(experts, count, inner)
    return pl.pallas_call(
        expert_in_kernel,
        grid=(experts, width // WIDE),
        in_specs=[by_inner, by_inner, weight, weight],
        out_specs=by_width,
        out_shape=jax.ShapeDtypeStruct((experts, count, width), BF16),
        cost_estimate=expert_cost(experts, count, width, inner, 2),
        name="expert_in",
    )(grad_gate, grad_up, gate_weight, up_weight)


def project_kernel(rows_ref, weight_ref, bias_ref, cosine_ref, sine_ref, held_ref, out_ref):
    head_size = cosine_ref.shape[1]
    sums = (
        jnp.dot(rows_ref[...], weight_ref[...], preferred_element_type=F32) + bias_ref[0:1, :]
    )
    for part in range(3):
        values = sums[:, part * head_size : (part + 1) * head_size]
        if part < 2:
            turned = pltpu.roll(values, head_size // 2, 1)
            values = values * cosine_ref[...] + turned * sine_ref[...]
        out_ref[:, part * head_size : (part + 1) * head_size] = values.astype(BF16)


def project(rows, weight, bias, cosine, sine, held, k):
    count, width = rows.shape
    head_size = cosine.shape[1]
    columns = 3 * head_size
    total = weight.shape[1]
    return pl.pallas_call(
        project_kernel,
        grid=(total // columns,),
        in_specs=[
            pl.BlockSpec((count, width), lambda h: (0, 0)),
            pl.BlockSpec((width, columns), lambda h: (0, h)),
            pl.BlockSpec((8, columns), lambda h: (0, h)),
            pl.BlockSpec((count, head_size), lambda h: (k, 0)),
            pl.BlockSpec((count, head_size), lambda h: (k, 0)),
            pl.BlockSpec(memory_space=pl.ANY),
        ],
        out_specs=pl.BlockSpec((count, columns), lambda h: (k, h)),
        out_shape=jax.ShapeDtypeStruct(held.shape, BF16),
        input_output_aliases={5: 0},
        cost_estimate=pl.CostEstimate(
            flops=2 * count * width * total,
            bytes_accessed=2 * (count * width + width * total + count * total),
            transcendentals=0,
        ),
        name="project",
    )(rows, weight, bias, cosine, sine, held)


def attend_kernel(q_ref, k_ref, v_ref, mask_ref, out_ref, *, score_scale):
    scores = (
        lax.dot_general(
            q_ref[...], k_ref[...], (((1,), (1,)), ((), ())), preferred_element_type=F32
        )
        * (score_scale * LOG2E)
        + mask_ref[...]
    )
    exponent = jnp.exp2(scores - jnp.max(scores, axis=1, keepdims=True))
    weights = exponent * (1.0 / jnp.sum(exponent, axis=1, keepdims=True))
    out_ref[...] = jnp.dot(
        weights.astype(BF16), v_ref[...], preferred_element_type=F32
    ).astype(BF16)


def attend(qkv, mask, count, head_size, k):
    length, total = qkv.shape
    heads = total // (3 * head_size)
    return pl.pallas_call(
        lambda *refs: attend_kernel(*refs, score_scale=1.0 / math.sqrt(head_size)),
        grid=(heads,),
        in_specs=[
            pl.BlockSpec((count, head_size), lambda h: (k, 3 * h)),
            pl.BlockSpec((length, head_size), lambda h: (0, 3 * h + 1)),
            pl.BlockSpec((length, head_size), lambda h: (0, 3 * h + 2)),
            pl.BlockSpec((count, length), lambda h: (k, 0)),
        ],
        out_specs=pl.BlockSpec((count, head_size), lambda h: (0, h)),
        out_shape=jax.ShapeDtypeStruct((count, heads * head_size), BF16),
        cost_estimate=pl.CostEstimate(
            flops=4 * count * length * heads * head_size,
            bytes_accessed=4 * (count + length) * heads * head_size,
            transcendentals=heads * count * length,
        ),
        name="attend",
    )(qkv, qkv, qkv, mask)


def attend_back_block(q_ref, k_ref, v_ref, grad_ref, mask_ref, cosine_ref, sine_ref):
    score_scale = 1.0 / math.sqrt(q_ref.shape[1])
    scores = (
        lax.dot_general(
            k_ref[...], q_ref[...], (((1,), (1,)), ((), ())), preferred_element_type=F32
        )
        * (score_scale * LOG2E)
        + mask_ref[...]
    )
    exponent = jnp.exp2(scores - jnp.max(scores, axis=0, keepdims=True))
    probs = exponent * (1.0 / jnp.sum(exponent, axis=0, keepdims=True))
    grad_probs = lax.dot_general(
        v_ref[...], grad_ref[...], (((1,), (1,)), ((), ())), preferred_element_type=F32
    )
    centre = jnp.sum(probs * grad_probs, axis=0, keepdims=True)
    grad_scores = (probs * (grad_probs - centre)).astype(BF16)
    grad_keys = jnp.dot(grad_scores, q_ref[...], preferred_element_type=F32) * score_scale
    grad_values = jnp.dot(probs.astype(BF16), grad_ref[...], preferred_element_type=F32)
    grad_queries = lax.dot_general(
        grad_scores, k_ref[...], (((0,), (0,)), ((), ())), preferred_element_type=F32
    )
    return turn_back(grad_queries * score_scale, cosine_ref, sine_ref), grad_keys, grad_values


def turn_back(values, cosine_ref, sine_ref):
    turned = pltpu.roll(values, values.shape[1] // 2, 1)
    return (values * cosine_ref[...] - turned * sine_ref[...]).astype(BF16)


def attend_back_some_kernel(
    q_ref, k_ref, v_ref, grad_ref, mask_ref, cosine_ref, sine_ref, gq_ref, gk_ref, gv_ref
):
    gq_ref[...], grad_keys, grad_values = attend_back_block(
        q_ref, k_ref, v_ref, grad_ref, mask_ref, cosine_ref, sine_ref
    )

    @pl.when(pl.program_id(1) == 0)
    def _():
        gk_ref[...] = grad_keys
        gv_ref[...] = grad_values

    @pl.when(pl.program_id(1) > 0)
    def _():
        gk_ref[...] += grad_keys
        gv_ref[...] += grad_values


def attend_back_last_kernel(
    q_ref, k_ref, v_ref, grad_ref, mask_ref, cosine_ref, sine_ref,
    all_cosine_ref, all_sine_ref, some_gq_ref, some_gk_ref, some_gv_ref, out_ref
):
    head_size = q_ref.shape[1]
    before = some_gq_ref.shape[0]
    grad_queries, grad_keys, grad_values = attend_back_block(
        q_ref, k_ref, v_ref, grad_ref, mask_ref, cosine_ref, sine_ref
    )
    out_ref[:before, :head_size] = some_gq_ref[...]
    out_ref[before:, :head_size] = grad_queries
    out_ref[:, head_size : 2 * head_size] = turn_back(
        some_gk_ref[...] + grad_keys, all_cosine_ref, all_sine_ref
    )
    out_ref[:, 2 * head_size :] = (some_gv_ref[...] + grad_values).astype(BF16)


def attend_back(qkv, grad_out, mask, cosine, sine, count, some=None):
    length, total = qkv.shape
    head_size = cosine.shape[1]
    heads = total // (3 * head_size)
    blocks = grad_out.shape[0] // count
    first = 0 if some is None else length // count - 1
    in_specs = [
        pl.BlockSpec((count, head_size), lambda h, i: (i + first, 3 * h)),
        pl.BlockSpec((length, head_size), lambda h, i: (0, 3 * h + 1)),
        pl.BlockSpec((length, head_size), lambda h, i: (0, 3 * h + 2)),
        pl.BlockSpec((count, head_size), lambda h, i: (i, h)),
        pl.BlockSpec((length, count), lambda h, i: (0, i + first)),
        pl.BlockSpec((count, head_size), lambda h, i: (i + first, 0)),
        pl.BlockSpec((count, head_size), lambda h, i: (i + first, 0)),
    ]
    cost = pl.CostEstimate(
        flops=10 * blocks * count * length * heads * head_size,
        bytes_accessed=20 * length * heads * head_size,
        transcendentals=heads * blocks * count * length,
    )
    whole = pl.BlockSpec((length, head_size), lambda h, i: (0, h))
    operands = [qkv, qkv, qkv, grad_out, mask, cosine, sine]
    if some is None:
        wide = jax.ShapeDtypeStruct((length, heads * head_size), F32)
        return pl.pallas_call(
            attend_back_some_kernel,
            grid=(heads, blocks),
            in_specs=in_specs,
            out_specs=[
                pl.BlockSpec((count, head_size), lambda h, i: (i, h)),
                whole,
                whole,
            ],
            out_shape=[
                jax.ShapeDtypeStruct((blocks * count, heads * head_size), BF16),
                wide,
                wide,
            ],
            cost_estimate=cost,
            name="attend_back_some",
        )(*operands)
    everywhere = pl.BlockSpec((length, head_size), lambda h, i: (0, 0))
    return pl.pallas_call(
        attend_back_last_kernel,
        grid=(heads, 1),
        in_specs=in_specs
        + [
            everywhere,
            everywhere,
            pl.BlockSpec((some[0].shape[0], head_size), lambda h, i: (0, h)),
            whole,
            whole,
        ],
        out_specs=pl.BlockSpec((length, 3 * head_size), lambda h, i: (0, h)),
        out_shape=jax.ShapeDtypeStruct((length, total), BF16),
        cost_estimate=cost,
        name="attend_back_last",
    )(*operands, cosine, sine, *some)


def scatter_raw(values, dimension):
    return lax.psum_scatter(values.astype(BF16), "grp", scatter_dimension=dimension, tiled=True)


def per_device(
    tokens,
    attn_norm,
    query_weight,
    key_weight,
    value_weight,
    query_bias,
    key_bias,
    value_bias,
    out_weight,
    ffn_norm,
    router_weight,
    shared_switch,
    shared_gate,
    shared_up,
    shared_down,
    expert_gate,
    expert_up,
    expert_down,
    routes,
    pieces,
    documents,
    cotangent,
):
    ep_count = lax.axis_size("ep")
    grp_count = lax.axis_size("grp")
    place = lax.axis_index("ep")
    row_count, own_count, model_width = tokens.shape
    length = own_count * ep_count
    heads_here = query_bias.shape[0]
    head_size = query_bias.shape[1] * grp_count
    head_width = heads_here * head_size
    hidden_width = shared_gate.shape[1]
    experts_here = expert_gate.shape[0]
    experts_all = experts_here * ep_count
    top_count = routes.shape[2]
    capacity = (own_count * top_count // experts_all * 5 + 3) // 4
    order = (place - jnp.arange(ep_count, dtype=jnp.int32)) % ep_count

    w_qkv = lax.all_gather(
        by_head(query_weight, key_weight, value_weight, heads_here),
        "grp",
        axis=0,
        tiled=True,
    )
    small_sizes = [
        attn_norm.size,
        query_bias.size,
        key_bias.size,
        value_bias.size,
        ffn_norm.size,
        router_weight.size,
        shared_switch.size,
    ]
    small = gather_small(
        jnp.concatenate(
            [
                part.reshape(-1)
                for part in (
                    attn_norm,
                    query_bias,
                    key_bias,
                    value_bias,
                    ffn_norm,
                    router_weight,
                    shared_switch,
                )
            ]
        ),
        "grp",
    )
    pieces_of_small = []
    begin = 0
    for size in small_sizes:
        pieces_of_small.append(small[:, begin : begin + size])
        begin += size
    gain_first = pieces_of_small[0].reshape(-1).astype(F32)
    biases = [
        part.reshape(grp_count, heads_here, -1).transpose(1, 0, 2).reshape(1, -1)
        for part in pieces_of_small[1:4]
    ]
    bias_qkv = jnp.broadcast_to(
        by_head(*biases, heads_here).astype(F32), (8, 3 * head_width)
    )
    gain_second = pieces_of_small[4].reshape(-1).astype(F32)
    w_router = pieces_of_small[5].reshape(model_width, experts_all)
    w_switch = pieces_of_small[6].reshape(model_width)
    w_out = lax.all_gather(out_weight, "grp", axis=1, tiled=True)
    w_sgu = lax.all_gather(
        jnp.concatenate([shared_gate, shared_up], axis=1), "grp", axis=0, tiled=True
    )
    w_sdown = lax.all_gather(shared_down, "grp", axis=1, tiled=True)

    tokens_own = tokens.reshape(own_count, model_width)
    grad_own_low = cotangent.reshape(own_count, model_width)
    x_blocks = ring_gather(tokens_own, "ep")
    routes_own = routes.reshape(own_count, top_count).T
    chosen = jnp.stack(
        [routes_own]
        + [
            lax.ppermute(routes_own, "ep", [(j, (j + k) % ep_count) for j in range(ep_count)])
            for k in range(1, ep_count)
        ]
    )
    own_places = jnp.arange(own_count, dtype=jnp.int32)
    position = (order[:, None] * own_count + own_places[None, :]).reshape(length)
    piece = jnp.take(pieces.reshape(ep_count, own_count), order, axis=0).reshape(length)
    document = jnp.take(documents.reshape(ep_count, own_count), order, axis=0).reshape(length)
    allowed = (document[:, None] == document[None, :]) & (
        (position[:, None] >= position[None, :])
        | ((piece[:, None] == piece[None, :]) & (piece[:, None] > 0))
    )
    allowed_by_key = (document[:, None] == document[None, :]) & (
        (position[:, None] <= position[None, :])
        | ((piece[:, None] == piece[None, :]) & (piece[:, None] > 0))
    )
    mask = jnp.where(allowed, 0.0, NEG)
    mask_by_key = jnp.where(allowed_by_key, 0.0, NEG)
    cosine_table, sine_table = rotary_tables(position, head_size)
    qkv = jnp.zeros((length, 3 * head_width), BF16)
    h_parts = []
    for k, block in enumerate(x_blocks):
        wide = after(block, qkv).astype(F32)
        h_parts.append((wide * inverse_rms(wide) * gain_first).astype(BF16))
        qkv = project(h_parts[k], w_qkv, bias_qkv, cosine_table, sine_table, qkv, k)
    qkv, chosen = lax.optimization_barrier((qkv, chosen))
    columns_h_one = away_and_near(h_parts, "grp")
    o_parts = [None] * ep_count
    ready = qkv
    for step in range(ep_count):
        k = (step + 1) % ep_count
        o_parts[k] = attend(ready, mask, own_count, head_size, k)
        if step == 1:
            ready = after(ready, columns_h_one, mask_by_key)
        ready, o_parts[k] = lax.optimization_barrier((ready, o_parts[k]))
    o_low = jnp.concatenate(o_parts, axis=0)

    def block_of(values, k):
        return values[k * own_count : (k + 1) * own_count]

    attn_own = ring_reduce(lambda k: times(o_parts[k], w_out), "ep")
    x_own = tokens_own.astype(F32)
    x1_own = x_own + attn_own
    inverse_two = inverse_rms(x1_own)
    hat_two = x1_own * inverse_two
    h_own = (hat_two * gain_second).astype(BF16)
    h_blocks = ring_gather(h_own, "ep")
    h_two = jnp.concatenate(h_blocks, axis=0)
    logits = times(h_two, jnp.concatenate([w_router, w_switch[:, None]], axis=1))
    route_probs = jax.nn.softmax(logits[:, :experts_all], axis=-1)
    switch = jax.nn.sigmoid(logits[:, experts_all])
    expert_ids = place * experts_here + jnp.arange(experts_here, dtype=jnp.int32)
    named = jnp.any(chosen[None] == expert_ids[:, None, None, None], axis=2)
    before = (own_places[:, None] < own_places[None, :]).astype(BF16)
    rank = jnp.einsum("est,tu->esu", named.astype(BF16), before, preferred_element_type=F32).astype(
        jnp.int32
    )
    rank = jnp.where(named & (rank < capacity), rank, -1)
    local_probs = lax.dynamic_slice_in_dim(route_probs, place * experts_here, experts_here, 1)
    local_probs = local_probs.reshape(ep_count, own_count, experts_here).transpose(2, 0, 1)
    hot = (
        rank[:, :, None, :] == jnp.arange(capacity, dtype=jnp.int32)[None, None, :, None]
    )
    gate_slot = jnp.sum(jnp.where(hot, local_probs[:, :, None, :], 0.0), axis=-1)
    slot_shape = (experts_here, ep_count * capacity, model_width)
    gate_rows = gate_slot.reshape(experts_here, ep_count * capacity, 1)

    s_pre = times(h_two, w_sgu)
    s_gate = s_pre[:, :hidden_width]
    s_up = s_pre[:, hidden_width:]
    sig_shared = jax.nn.sigmoid(s_gate)
    silu_shared = s_gate * sig_shared
    s_hidden = (silu_shared * s_up).astype(BF16)
    s_part = times(s_hidden, w_sdown).astype(BF16)
    grad_blocks = lax.all_gather(after(grad_own_low, h_blocks[-1]), "ep", axis=0)
    flat_rows = select_rows(rank, after(h_two, s_part), capacity)
    flat_rows = flat_rows.reshape(slot_shape)
    gate_pre, up_pre, hidden = expert_up_all(flat_rows, expert_gate, expert_up)
    result = expert_down_all(hidden, expert_down)
    grad_blocks = after(grad_blocks, result)
    grad_low = jnp.take(grad_blocks, order, axis=0).reshape(length, model_width)
    grad_all = grad_low.astype(F32)
    grad_sout = (switch[:, None] * grad_all).astype(BF16)
    grad_shidden = times_trans(grad_sout, w_sdown)
    slope_shared = sig_shared * (1.0 + s_gate * (1.0 - sig_shared))
    grad_s = jnp.concatenate(
        [
            (grad_shidden * s_up * slope_shared).astype(BF16),
            (grad_shidden * silu_shared).astype(BF16),
        ],
        axis=1,
    )
    row_shape = (experts_here, ep_count, capacity, model_width)
    y_part = spread_rows(rank, local_probs, result.reshape(row_shape), switch, s_part)
    y_first = block_of(y_part, 1 % ep_count)
    part_sdown = inner_rows(s_hidden, after(grad_sout, grad_s)).astype(BF16)
    part_sgu = inner_rows(after(h_two, part_sdown), grad_s).astype(BF16)
    raw_sdown = scatter_raw(part_sdown, 1)
    raw_sgu = scatter_raw(part_sgu, 0)
    grad_rows = select_rows(
        rank, after(grad_low, y_first, part_sdown, part_sgu), capacity
    ).reshape(slot_shape)
    grad_gate_pre, grad_up_pre, hidden_gated, grad_gate = expert_back_all(
        grad_rows, expert_down, gate_pre, up_pre, hidden, gate_rows
    )

    routed = []

    def beside_y(step, sent):
        if step == 1:
            return [grad_gate_pre]
        if step == 2:
            part = jnp.einsum(
                "erf,erd->efd", after(hidden_gated, sent), grad_rows, preferred_element_type=F32
            )
            routed.append(part.astype(BF16))
            return routed[:]
        if step == 3:
            routed.append(
                expert_in_all(
                    after(grad_gate_pre, routed[0], sent), grad_up_pre, expert_gate, expert_up
                )
            )
            return routed[1:]
        return []

    layer_own = x1_own + ring_reduce(lambda k: block_of(y_part, k), "ep", y_first, beside_y)
    part_edown, grad_inputs = routed
    raw_edown = scatter_raw(part_edown, 2)
    shared_dot = jnp.sum(grad_all * s_part.astype(F32), axis=-1).reshape(1, ep_count, own_count)
    grad_probs_part = jnp.sum(
        jnp.where(
            hot, grad_gate.reshape(experts_here, ep_count, capacity)[:, :, :, None], 0.0
        ),
        axis=2,
    )
    scalars = jnp.concatenate([grad_probs_part, shared_dot], axis=0)
    home = [scalars[:, 0]]
    for k in range(1, ep_count):
        home.append(
            lax.ppermute(scalars[:, k], "ep", [(j, (j - k) % ep_count) for j in range(ep_count)])
        )
    grad_inputs, layer_own, *home = lax.optimization_barrier((grad_inputs, layer_own, *home))
    home = jnp.stack(home)
    grad_moe = spread_rows(rank, jnp.ones_like(local_probs), grad_inputs.reshape(row_shape))

    grad_probs = jnp.take(
        home[:, :experts_here],
        (jnp.arange(ep_count, dtype=jnp.int32) - place) % ep_count,
        axis=0,
    )
    grad_probs = grad_probs.reshape(experts_all, own_count).T
    probs_own = route_probs[:own_count]
    switch_own = switch[:own_count]
    grad_logit = (
        probs_own * (grad_probs - jnp.sum(probs_own * grad_probs, axis=-1, keepdims=True))
    ).astype(BF16)
    grad_switch = (
        jnp.sum(home[:, experts_here], axis=0) * switch_own * (1.0 - switch_own)
    ).astype(BF16)

    w_small = jnp.concatenate([w_router, w_switch[:, None]], axis=1)
    grad_small = jnp.concatenate([grad_logit, grad_switch[:, None]], axis=1)
    layer_out = layer_own.reshape(row_count, own_count, model_width).astype(BF16)

    def grad_h2_part(k):
        return times_trans(block_of(grad_s, k), w_sgu) + block_of(grad_moe, k)

    grad_h2_first = grad_h2_part(1 % ep_count).astype(BF16)
    forms = (
        ("erd,erf->edf", flat_rows, grad_gate_pre),
        ("erd,erf->edf", flat_rows, grad_up_pre),
    )
    expert_raw = []

    def expert_part(sent):
        form, left_side, right_side = forms[len(expert_raw)]
        left_side, right_side, _ = lax.optimization_barrier((left_side, right_side, sent))
        part = jnp.einsum(form, left_side, right_side, preferred_element_type=F32).astype(BF16)
        expert_raw.append(scatter_raw(part, 1))
        return part

    def beside_h2(step, sent):
        return {1: [raw_sdown], 2: [expert_part, raw_sgu], 3: [expert_part]}.get(step, [])

    grad_h2 = ring_reduce(
        grad_h2_part,
        "ep",
        grad_h2_first,
        lambda step, sent: [
            item(sent) if callable(item) else item for item in beside_h2(step, sent)
        ],
        times_trans(grad_s[2 * own_count :], w_sgu) + grad_moe[2 * own_count :],
    ) + times_trans(grad_small, w_small)
    weighted = grad_h2 * gain_second
    grad_x1 = grad_own_low.astype(F32) + inverse_two * (
        weighted - hat_two * jnp.mean(weighted * hat_two, axis=-1, keepdims=True)
    )
    grad_x1_low = grad_x1.astype(BF16)
    while len(expert_raw) < len(forms):
        expert_part(grad_x1_low)
    grad_attn_blocks = ring_gather(grad_x1_low, "ep")

    gain_two_part = jnp.sum(grad_h2 * hat_two, axis=0)
    small_part = jnp.concatenate([inner_rows(grad_small, h_own), gain_two_part[None, :]], axis=0)
    small_grp = sum_all(small_part, "grp")
    back_tables = (mask_by_key, cosine_table, sine_table, own_count)
    grad_o = [times_trans(block, w_out).astype(BF16) for block in grad_attn_blocks[:-1]]
    some_back = attend_back(after(qkv, small_grp), jnp.concatenate(grad_o, axis=0), *back_tables)
    last_block = after(grad_attn_blocks[-1], *some_back)
    grad_qkv = attend_back(
        qkv, times_trans(last_block, w_out).astype(BF16), *back_tables, some_back
    )
    chunk_width = model_width // grp_count
    grp_place = lax.axis_index("grp")
    qkv_half = 3 * head_width // 2
    grad_h1_first = times_trans(block_of(grad_qkv, 1 % ep_count), w_qkv).astype(BF16)

    def qkv_part(columns, p):
        return inner_rows(columns, grad_qkv[:, p * qkv_half : (p + 1) * qkv_half])

    def out_part(columns, p):
        return inner_rows(o_low[:, p * head_width // 2 : (p + 1) * head_width // 2], columns)

    qkv_left, qkv_columns, qkv_come = halving_send(
        qkv_part, after(columns_h_one, grad_h1_first), "grp", 2
    )
    near_sums = []
    out_sent = []

    def beside_h1(step, sent):
        if step == 1:
            return qkv_left
        if step == 2:
            near_sums.append(halving_near(qkv_part, qkv_columns, qkv_come, sent))
            columns_grad_attn = away_and_near(
                [after(block, *near_sums[0]) for block in grad_attn_blocks], "grp"
            )
            out_sent.extend(halving_send(out_part, columns_grad_attn, "grp", 2))
            return near_sums[0]
        if step == 3:
            near_sums.append(halving_near(out_part, out_sent[1], out_sent[2], sent))
            return near_sums[1]
        return []

    grad_h1 = ring_reduce(
        lambda k: times_trans(block_of(grad_qkv, k), w_qkv),
        "ep",
        grad_h1_first,
        beside_h1,
        times_trans(grad_qkv[2 * own_count :], w_qkv),
    )
    qkv_near, out_near = near_sums
    grad_tokens = grad_x1 + norm_back(x_own, gain_first, grad_h1)
    tokens_grad = grad_tokens.reshape(row_count, own_count, model_width)
    gain_one_part = jnp.sum(grad_h1 * (x_own * inverse_rms(x_own)), axis=0)
    sum_sdown, sum_sgu, sum_edown, sum_egate, sum_eup = (
        raw.astype(F32) for raw in (raw_sdown, raw_sgu, raw_edown, *expert_raw)
    )
    gain_one_part = after(gain_one_part, sum_sdown, sum_sgu, sum_edown)
    last_part = jnp.concatenate([gain_one_part, jnp.sum(grad_qkv.astype(F32), axis=0)])[None, :]
    last_tie = after(last_part, sum_egate, sum_eup)
    sum_qkv = jnp.concatenate(halving_rest(qkv_near, "grp", 0, last_tie), axis=1)
    sum_out = jnp.concatenate(halving_rest(out_near, "grp", 1, last_tie), axis=0)
    last_grp = sum_all(last_part, "grp")
    bias_width = head_size // grp_count
    sum_bias = lax.dynamic_slice_in_dim(
        last_grp[:, model_width:].reshape(3 * heads_here, head_size),
        grp_place * bias_width,
        bias_width,
        1,
    )
    small_sum = sum_all(
        lax.dynamic_slice_in_dim(
            jnp.concatenate([small_grp, last_grp[:, :model_width]], axis=0),
            grp_place * chunk_width,
            chunk_width,
            1,
        ),
        "ep",
    )

    def of_heads(values, part):
        begins = range(part * head_size, 3 * head_width, 3 * head_size)
        return jnp.concatenate([values[:, b : b + head_size] for b in begins], axis=1)

    return (
        layer_out,
        tokens_grad,
        small_sum[experts_all + 2],
        of_heads(sum_qkv, 0),
        of_heads(sum_qkv, 1),
        of_heads(sum_qkv, 2),
        sum_bias[0::3],
        sum_bias[1::3],
        sum_bias[2::3],
        sum_out,
        small_sum[experts_all + 1],
        small_sum[:experts_all].T,
        small_sum[experts_all],
        sum_sgu[:, :hidden_width],
        sum_sgu[:, hidden_width:],
        sum_sdown,
        sum_egate,
        sum_eup,
        sum_edown,
    )


def solution(mesh):
    return jax.shard_map(
        per_device,
        mesh=mesh,
        in_specs=(
            P("grp", "ep", None),
            P("grp"),
            P("grp", "ep"),
            P("grp", "ep"),
            P("grp", "ep"),
            P("ep", "grp"),
            P("ep", "grp"),
            P("ep", "grp"),
            P("ep", "grp"),
            P("grp"),
            P("grp", None),
            P("grp"),
            P("grp", "ep"),
            P("grp", "ep"),
            P("ep", "grp"),
            P("ep", None, None),
            P("ep", None, None),
            P("ep", None, None),
            P("grp", "ep", None),
            P("grp", None),
            P("grp", None),
            P("grp", "ep", None),
        ),
        out_specs=(
            P("grp", "ep", None),
            P("grp", "ep", None),
            P("grp"),
            P("grp", "ep"),
            P("grp", "ep"),
            P("grp", "ep"),
            P("ep", "grp"),
            P("ep", "grp"),
            P("ep", "grp"),
            P("ep", "grp"),
            P("grp"),
            P("grp", None),
            P("grp"),
            P("grp", "ep"),
            P("grp", "ep"),
            P("ep", "grp"),
            P("ep", "grp", None),
            P("ep", "grp", None),
            P("ep", None, "grp"),
        ),
        check_vma=False,
    )
```

```python
import math

import jax
import jax.numpy as jnp
from jax import lax
from jax.experimental import pallas as pl
from jax.experimental.pallas import tpu as pltpu
from jax.sharding import PartitionSpec as P

EPS = 1e-06
THETA = 1000000.0
NEG = -1e30
LOG2E = 1.4426950408889634
WIDE = 512
F32 = jnp.float32
BF16 = jnp.bfloat16


def inverse_rms(values):
    return lax.rsqrt(jnp.mean(values * values, axis=-1, keepdims=True) + EPS)


def norm_back(values, gain_vec, upstream):
    inverse = inverse_rms(values)
    scaled = values * inverse
    weighted = upstream * gain_vec
    return inverse * (weighted - scaled * jnp.mean(weighted * scaled, axis=-1, keepdims=True))


def rotary_tables(position, head_size):
    frequency = THETA ** (-(jnp.arange(head_size // 2, dtype=F32) * 2.0 / head_size))
    angle = position.astype(F32)[:, None] * frequency[None, :]
    cosine, sine = jnp.cos(angle), jnp.sin(angle)
    return (
        jnp.concatenate([cosine, cosine], axis=1),
        jnp.concatenate([-sine, sine], axis=1),
    )


def after(values, *others):
    return lax.optimization_barrier((values, *others))[0]


def by_head(queries, keys, values, heads):
    rows = queries.shape[0]
    parts = [part.reshape(rows, heads, -1) for part in (queries, keys, values)]
    return jnp.concatenate(parts, axis=2).reshape(rows, -1)


def inner_rows(left_side, right_side):
    return lax.dot_general(
        left_side, right_side, (((0,), (0,)), ((), ())), preferred_element_type=F32
    )


def times_trans(left_side, right_side):
    return lax.dot_general(
        left_side, right_side, (((1,), (1,)), ((), ())), preferred_element_type=F32
    )


def times(left_side, right_side):
    return jnp.dot(left_side, right_side, preferred_element_type=F32)


def ring_gather(own_block, axis):
    count = lax.axis_size(axis)
    pairs = [(j, (j + 1) % count) for j in range(count)]
    blocks = [own_block]
    for _ in range(count - 1):
        blocks.append(lax.ppermute(blocks[-1], axis, pairs))
    return blocks


def ring_reduce(part_of, axis, first=None, beside=None, middle=None):
    count = lax.axis_size(axis)
    pairs = [(j, (j + 1) % count) for j in range(count)]
    running = part_of(1 % count).astype(BF16) if first is None else first
    if middle is None:
        parts = [part_of((step + 1) % count) for step in range(1, count)]
    else:
        parts = [*jnp.split(middle, count - 2, axis=0), part_of(0)]
    parts = [lax.optimization_barrier(part) for part in parts]
    for step in range(1, count):
        arrived = lax.ppermute(running, axis, pairs)
        held = parts[step:] if middle is not None else parts[step : step + 1]
        if beside is not None:
            held = held + list(beside(step, running))
        part = after(parts[step - 1], *held) if held else parts[step - 1]
        running = arrived.astype(F32) + part
        if step < count - 1:
            running = running.astype(BF16)
    return running


def bits_of(axis):
    return range(lax.axis_size(axis).bit_length() - 1)


def swap(values, axis, bit):
    count = lax.axis_size(axis)
    return lax.ppermute(values, axis, [(j, j ^ (1 << bit)) for j in range(count)])


def sum_all(values, axis):
    for bit in bits_of(axis):
        values = values + swap(values, axis, bit)
    return values


def gather_small(values, axis):
    count = lax.axis_size(axis)
    blocks = values[None, :]
    for bit in bits_of(axis):
        blocks = jnp.concatenate([blocks, swap(blocks, axis, bit)], axis=0)
    index = jnp.arange(count, dtype=jnp.int32)
    apart = index[:, None] ^ lax.axis_index(axis)
    return times((apart == index[None, :]).astype(values.dtype), blocks).astype(values.dtype)


def column_kernel(order_ref, *refs):
    out_ref = refs[-1]
    begin = 0
    for data_ref in refs[:-1]:
        out_ref[begin : begin + data_ref.shape[0], :] = data_ref[...]
        begin += data_ref.shape[0]


def column_chunks(blocks, order):
    rows = sum(block.shape[0] for block in blocks)
    count = order.shape[0]
    chunk = blocks[0].shape[1] // count
    return pl.pallas_call(
        column_kernel,
        grid_spec=pltpu.PrefetchScalarGridSpec(
            num_scalar_prefetch=1,
            grid=(count,),
            in_specs=[
                pl.BlockSpec((block.shape[0], chunk), lambda r, order_ref: (0, order_ref[r]))
                for block in blocks
            ],
            out_specs=pl.BlockSpec((rows, chunk), lambda r, order_ref: (0, r)),
        ),
        out_shape=jax.ShapeDtypeStruct((rows, count * chunk), blocks[0].dtype),
        cost_estimate=pl.CostEstimate(
            flops=0, bytes_accessed=4 * rows * count * chunk, transcendentals=0
        ),
        name="column_chunks",
    )(order, *blocks)


def away_and_near(blocks, axis):
    count = lax.axis_size(axis)
    index = jnp.arange(count, dtype=jnp.int32).reshape(count // 2, 2)
    order = lax.axis_index(axis) ^ jnp.concatenate([index[:, 1], index[:, 0]])
    return column_chunks(blocks, order)


def halving_send(part_of, columns, axis, parts):
    half = columns.shape[1] // 2
    away, near = columns[:, :half], columns[:, half:]
    leaving = [part_of(away, p).astype(BF16) for p in range(parts)]
    return leaving, near, [swap(block, axis, 0) for block in leaving]


def halving_near(part_of, near, arrived, tie):
    near, *arrived = lax.optimization_barrier((near, *arrived, tie))[:-1]
    return [(part_of(near, p) + block.astype(F32)).astype(BF16) for p, block in enumerate(arrived)]


def halving_rest(sums, axis, dimension, tie=None):
    count = lax.axis_size(axis)
    results = []
    for p, near_sum in enumerate(sums):
        steps = list(bits_of(axis))[1:]
        if p % 2:
            steps.reverse()
        held = dict(zip(range(0, count, 2), jnp.split(near_sum, count // 2, axis=dimension)))
        for turn, bit in enumerate(steps):
            leaving = [r for r in held if r >> bit & 1]
            staying = [r for r in held if not r >> bit & 1]
            sent = jnp.concatenate([held[r].astype(BF16) for r in leaving], axis=dimension)
            come = swap(sent, axis, bit)
            if turn == 0 and tie is not None:
                come = after(come, tie)
            for r, block in zip(leaving, jnp.split(come, len(leaving), axis=dimension)):
                held[r ^ (1 << bit)] = (
                    held[r ^ (1 << bit)].astype(BF16).astype(F32) + block.astype(F32)
                )
            held = {r: held[r] for r in staying}
        results.append(held[0])
    return results


def select_kernel(rank_ref, data_ref, out_ref):
    experts, _, slots, _ = out_ref.shape
    tokens = data_ref.shape[1]
    slot = lax.broadcasted_iota(jnp.int32, (slots, tokens), 0)
    hot = jnp.concatenate(
        [jnp.where(slot == rank_ref[e, 0], 1.0, 0.0).astype(BF16) for e in range(experts)], axis=0
    )
    rows = jnp.dot(hot, data_ref[0], preferred_element_type=F32).astype(BF16)
    for e in range(experts):
        out_ref[e, 0] = rows[e * slots : (e + 1) * slots]


def select_rows(rank, data, slots):
    experts, blocks, tokens = rank.shape
    width = data.shape[-1]
    return pl.pallas_call(
        select_kernel,
        grid=(blocks,),
        in_specs=[
            pl.BlockSpec((experts, 1, 1, tokens), lambda s: (0, s, 0, 0)),
            pl.BlockSpec((1, tokens, width), lambda s: (s, 0, 0)),
        ],
        out_specs=pl.BlockSpec((experts, 1, slots, width), lambda s: (0, s, 0, 0)),
        out_shape=jax.ShapeDtypeStruct((experts, blocks, slots, width), BF16),
        cost_estimate=pl.CostEstimate(
            flops=2 * experts * blocks * slots * tokens * width,
            bytes_accessed=2 * (experts * blocks * slots + blocks * tokens) * width,
            transcendentals=0,
        ),
        name="select_rows",
    )(rank.reshape(experts, blocks, 1, tokens), data.reshape(blocks, tokens, width))


def spread_kernel(rank_ref, weight_ref, rows_ref, *refs):
    out_ref = refs[-1]
    experts, _, slots, _ = rows_ref.shape
    tokens = out_ref.shape[1]
    slot = lax.broadcasted_iota(jnp.int32, (tokens, slots), 1)
    total = None
    for e in range(experts):
        hot = jnp.where(slot == rank_ref[e, 0], weight_ref[e, 0], 0.0).astype(BF16)
        part = jnp.dot(hot, rows_ref[e, 0], preferred_element_type=F32)
        total = part if total is None else total + part
    if len(refs) == 3:
        total = total + refs[0][0] * refs[1][0].astype(F32)
    out_ref[0] = total.astype(BF16)


def spread_rows(rank, weight, rows, scale=None, addend=None):
    experts, blocks, tokens = rank.shape
    slots, width = rows.shape[2:]
    column = pl.BlockSpec((experts, 1, tokens, 1), lambda s: (0, s, 0, 0))
    in_specs = [
        column,
        column,
        pl.BlockSpec((experts, 1, slots, width), lambda s: (0, s, 0, 0)),
    ]
    operands = [
        rank.reshape(experts, blocks, tokens, 1),
        weight.reshape(experts, blocks, tokens, 1),
        rows,
    ]
    if addend is not None:
        in_specs += [
            pl.BlockSpec((1, tokens, 1), lambda s: (s, 0, 0)),
            pl.BlockSpec((1, tokens, width), lambda s: (s, 0, 0)),
        ]
        operands += [scale.reshape(blocks, tokens, 1), addend.reshape(blocks, tokens, width)]
    return pl.pallas_call(
        spread_kernel,
        grid=(blocks,),
        in_specs=in_specs,
        out_specs=pl.BlockSpec((1, tokens, width), lambda s: (s, 0, 0)),
        out_shape=jax.ShapeDtypeStruct((blocks, tokens, width), BF16),
        cost_estimate=pl.CostEstimate(
            flops=2 * experts * blocks * slots * tokens * width,
            bytes_accessed=(2 * experts * blocks * slots + 4 * blocks * tokens) * width,
            transcendentals=0,
        ),
        name="spread_rows",
    )(*operands).reshape(blocks * tokens, width)


def expert_up_kernel(rows_ref, gate_ref, up_ref, gate_out, up_out, hidden_out):
    gate = jnp.dot(rows_ref[0], gate_ref[0], preferred_element_type=F32)
    up = jnp.dot(rows_ref[0], up_ref[0], preferred_element_type=F32)
    gate_out[0] = gate.astype(BF16)
    up_out[0] = up.astype(BF16)
    hidden_out[0] = (gate * jax.nn.sigmoid(gate) * up).astype(BF16)


def expert_specs(experts, rows, inner):
    return (
        pl.BlockSpec((1, rows, WIDE), lambda e, k: (e, 0, k)),
        pl.BlockSpec((1, rows, inner), lambda e, k: (e, 0, 0)),
        pl.BlockSpec((1, WIDE, inner), lambda e, k: (e, k, 0)),
        pl.BlockSpec((1, inner, WIDE), lambda e, k: (e, 0, k)),
    )


def expert_cost(experts, rows, width, inner, weights):
    return pl.CostEstimate(
        flops=2 * weights * experts * rows * width * inner,
        bytes_accessed=2 * experts * (weights * width * inner + rows * (width + 3 * inner)),
        transcendentals=0,
    )


def expert_up_all(rows, gate_weight, up_weight):
    experts, count, width = rows.shape
    inner = gate_weight.shape[2]
    half = count // 2
    weight = pl.BlockSpec((1, width, inner), lambda e, i: (e, 0, 0))
    out = pl.BlockSpec((1, half, inner), lambda e, i: (e, i, 0))
    return pl.pallas_call(
        expert_up_kernel,
        grid=(experts, 2),
        in_specs=[pl.BlockSpec((1, half, width), lambda e, i: (e, i, 0)), weight, weight],
        out_specs=[out] * 3,
        out_shape=[jax.ShapeDtypeStruct((experts, count, inner), BF16)] * 3,
        cost_estimate=expert_cost(experts, count, width, inner, 2),
        name="expert_up",
    )(rows, gate_weight, up_weight)


def expert_down_kernel(hidden_ref, down_ref, out_ref):
    out_ref[0] = jnp.dot(hidden_ref[0], down_ref[0], preferred_element_type=F32).astype(BF16)


def expert_down_all(hidden, down_weight):
    experts, count, inner = hidden.shape
    width = down_weight.shape[2]
    by_width, by_inner, _, weight = expert_specs(experts, count, inner)
    return pl.pallas_call(
        expert_down_kernel,
        grid=(experts, width // WIDE),
        in_specs=[by_inner, weight],
        out_specs=by_width,
        out_shape=jax.ShapeDtypeStruct((experts, count, width), BF16),
        cost_estimate=expert_cost(experts, count, width, inner, 1),
        name="expert_down",
    )(hidden, down_weight)


def expert_back_kernel(
    grad_ref, down_ref, gate_ref, up_ref, hidden_ref, share_ref,
    gate_out, up_out, gated_out, dot_out
):
    plain = times_trans(grad_ref[0], down_ref[0])
    hidden = hidden_ref[0].astype(F32)
    share = share_ref[0]
    dot_out[0] = jnp.sum(plain * hidden, axis=1, keepdims=True)
    gated_out[0] = (share * hidden).astype(BF16)
    grad_hidden = share * plain
    gate = gate_ref[0].astype(F32)
    sig = jax.nn.sigmoid(gate)
    up_out[0] = (grad_hidden * gate * sig).astype(BF16)
    slope = sig * (1.0 + gate * (1.0 - sig))
    gate_out[0] = (grad_hidden * up_ref[0].astype(F32) * slope).astype(BF16)


def expert_back_all(grad_rows, down_weight, gate, up, hidden, share):
    experts, count, width = grad_rows.shape
    inner = down_weight.shape[1]
    half = count // 2
    own = pl.BlockSpec((1, half, inner), lambda e, i: (e, i, 0))
    one = pl.BlockSpec((1, half, 1), lambda e, i: (e, i, 0))
    return pl.pallas_call(
        expert_back_kernel,
        grid=(experts, 2),
        in_specs=[
            pl.BlockSpec((1, half, width), lambda e, i: (e, i, 0)),
            pl.BlockSpec((1, inner, width), lambda e, i: (e, 0, 0)),
            own,
            own,
            own,
            one,
        ],
        out_specs=[own, own, own, one],
        out_shape=[jax.ShapeDtypeStruct((experts, count, inner), BF16)] * 3
        + [jax.ShapeDtypeStruct((experts, count, 1), F32)],
        cost_estimate=expert_cost(experts, count, width, inner, 1),
        name="expert_back",
    )(grad_rows, down_weight, gate, up, hidden, share)


def expert_in_kernel(grad_gate_ref, grad_up_ref, gate_ref, up_ref, out_ref):
    out_ref[0] = (
        times_trans(grad_gate_ref[0], gate_ref[0]) + times_trans(grad_up_ref[0], up_ref[0])
    ).astype(BF16)


def expert_in_all(grad_gate, grad_up, gate_weight, up_weight):
    experts, count, inner = grad_gate.shape
    width = gate_weight.shape[1]
    by_width, by_inner, weight, _ = expert_specs(experts, count, inner)
    return pl.pallas_call(
        expert_in_kernel,
        grid=(experts, width // WIDE),
        in_specs=[by_inner, by_inner, weight, weight],
        out_specs=by_width,
        out_shape=jax.ShapeDtypeStruct((experts, count, width), BF16),
        cost_estimate=expert_cost(experts, count, width, inner, 2),
        name="expert_in",
    )(grad_gate, grad_up, gate_weight, up_weight)


def project_kernel(rows_ref, weight_ref, bias_ref, cosine_ref, sine_ref, held_ref, out_ref):
    head_size = cosine_ref.shape[1]
    sums = (
        jnp.dot(rows_ref[...], weight_ref[...], preferred_element_type=F32) + bias_ref[0:1, :]
    )
    for part in range(3):
        values = sums[:, part * head_size : (part + 1) * head_size]
        if part < 2:
            turned = pltpu.roll(values, head_size // 2, 1)
            values = values * cosine_ref[...] + turned * sine_ref[...]
        out_ref[:, part * head_size : (part + 1) * head_size] = values.astype(BF16)


def project(rows, weight, bias, cosine, sine, held, k):
    count, width = rows.shape
    head_size = cosine.shape[1]
    columns = 3 * head_size
    total = weight.shape[1]
    return pl.pallas_call(
        project_kernel,
        grid=(total // columns,),
        in_specs=[
            pl.BlockSpec((count, width), lambda h: (0, 0)),
            pl.BlockSpec((width, columns), lambda h: (0, h)),
            pl.BlockSpec((8, columns), lambda h: (0, h)),
            pl.BlockSpec((count, head_size), lambda h: (k, 0)),
            pl.BlockSpec((count, head_size), lambda h: (k, 0)),
            pl.BlockSpec(memory_space=pl.ANY),
        ],
        out_specs=pl.BlockSpec((count, columns), lambda h: (k, h)),
        out_shape=jax.ShapeDtypeStruct(held.shape, BF16),
        input_output_aliases={5: 0},
        cost_estimate=pl.CostEstimate(
            flops=2 * count * width * total,
            bytes_accessed=2 * (count * width + width * total + count * total),
            transcendentals=0,
        ),
        name="project",
    )(rows, weight, bias, cosine, sine, held)


def attend_kernel(q_ref, k_ref, v_ref, mask_ref, out_ref, *, score_scale):
    scores = (
        lax.dot_general(
            q_ref[...], k_ref[...], (((1,), (1,)), ((), ())), preferred_element_type=F32
        )
        * (score_scale * LOG2E)
        + mask_ref[...]
    )
    exponent = jnp.exp2(scores - jnp.max(scores, axis=1, keepdims=True))
    weights = exponent * (1.0 / jnp.sum(exponent, axis=1, keepdims=True))
    out_ref[...] = jnp.dot(
        weights.astype(BF16), v_ref[...], preferred_element_type=F32
    ).astype(BF16)


def attend(qkv, mask, count, head_size, k):
    length, total = qkv.shape
    heads = total // (3 * head_size)
    return pl.pallas_call(
        lambda *refs: attend_kernel(*refs, score_scale=1.0 / math.sqrt(head_size)),
        grid=(heads,),
        in_specs=[
            pl.BlockSpec((count, head_size), lambda h: (k, 3 * h)),
            pl.BlockSpec((length, head_size), lambda h: (0, 3 * h + 1)),
            pl.BlockSpec((length, head_size), lambda h: (0, 3 * h + 2)),
            pl.BlockSpec((count, length), lambda h: (k, 0)),
        ],
        out_specs=pl.BlockSpec((count, head_size), lambda h: (0, h)),
        out_shape=jax.ShapeDtypeStruct((count, heads * head_size), BF16),
        cost_estimate=pl.CostEstimate(
            flops=4 * count * length * heads * head_size,
            bytes_accessed=4 * (count + length) * heads * head_size,
            transcendentals=heads * count * length,
        ),
        name="attend",
    )(qkv, qkv, qkv, mask)


def attend_back_block(q_ref, k_ref, v_ref, grad_ref, mask_ref, cosine_ref, sine_ref):
    score_scale = 1.0 / math.sqrt(q_ref.shape[1])
    scores = (
        lax.dot_general(
            k_ref[...], q_ref[...], (((1,), (1,)), ((), ())), preferred_element_type=F32
        )
        * (score_scale * LOG2E)
        + mask_ref[...]
    )
    exponent = jnp.exp2(scores - jnp.max(scores, axis=0, keepdims=True))
    probs = exponent * (1.0 / jnp.sum(exponent, axis=0, keepdims=True))
    grad_probs = lax.dot_general(
        v_ref[...], grad_ref[...], (((1,), (1,)), ((), ())), preferred_element_type=F32
    )
    centre = jnp.sum(probs * grad_probs, axis=0, keepdims=True)
    grad_scores = (probs * (grad_probs - centre)).astype(BF16)
    grad_keys = jnp.dot(grad_scores, q_ref[...], preferred_element_type=F32) * score_scale
    grad_values = jnp.dot(probs.astype(BF16), grad_ref[...], preferred_element_type=F32)
    grad_queries = lax.dot_general(
        grad_scores, k_ref[...], (((0,), (0,)), ((), ())), preferred_element_type=F32
    )
    return turn_back(grad_queries * score_scale, cosine_ref, sine_ref), grad_keys, grad_values


def turn_back(values, cosine_ref, sine_ref):
    turned = pltpu.roll(values, values.shape[1] // 2, 1)
    return (values * cosine_ref[...] - turned * sine_ref[...]).astype(BF16)


def attend_back_some_kernel(
    q_ref, k_ref, v_ref, grad_ref, mask_ref, cosine_ref, sine_ref, gq_ref, gk_ref, gv_ref
):
    gq_ref[...], grad_keys, grad_values = attend_back_block(
        q_ref, k_ref, v_ref, grad_ref, mask_ref, cosine_ref, sine_ref
    )

    @pl.when(pl.program_id(1) == 0)
    def _():
        gk_ref[...] = grad_keys
        gv_ref[...] = grad_values

    @pl.when(pl.program_id(1) > 0)
    def _():
        gk_ref[...] += grad_keys
        gv_ref[...] += grad_values


def attend_back_last_kernel(
    q_ref, k_ref, v_ref, grad_ref, mask_ref, cosine_ref, sine_ref,
    all_cosine_ref, all_sine_ref, some_gq_ref, some_gk_ref, some_gv_ref, out_ref
):
    head_size = q_ref.shape[1]
    before = some_gq_ref.shape[0]
    grad_queries, grad_keys, grad_values = attend_back_block(
        q_ref, k_ref, v_ref, grad_ref, mask_ref, cosine_ref, sine_ref
    )
    out_ref[:before, :head_size] = some_gq_ref[...]
    out_ref[before:, :head_size] = grad_queries
    out_ref[:, head_size : 2 * head_size] = turn_back(
        some_gk_ref[...] + grad_keys, all_cosine_ref, all_sine_ref
    )
    out_ref[:, 2 * head_size :] = (some_gv_ref[...] + grad_values).astype(BF16)


def attend_back(qkv, grad_out, mask, cosine, sine, count, some=None):
    length, total = qkv.shape
    head_size = cosine.shape[1]
    heads = total // (3 * head_size)
    blocks = grad_out.shape[0] // count
    first = 0 if some is None else length // count - 1
    in_specs = [
        pl.BlockSpec((count, head_size), lambda h, i: (i + first, 3 * h)),
        pl.BlockSpec((length, head_size), lambda h, i: (0, 3 * h + 1)),
        pl.BlockSpec((length, head_size), lambda h, i: (0, 3 * h + 2)),
        pl.BlockSpec((count, head_size), lambda h, i: (i, h)),
        pl.BlockSpec((length, count), lambda h, i: (0, i + first)),
        pl.BlockSpec((count, head_size), lambda h, i: (i + first, 0)),
        pl.BlockSpec((count, head_size), lambda h, i: (i + first, 0)),
    ]
    cost = pl.CostEstimate(
        flops=10 * blocks * count * length * heads * head_size,
        bytes_accessed=20 * length * heads * head_size,
        transcendentals=heads * blocks * count * length,
    )
    whole = pl.BlockSpec((length, head_size), lambda h, i: (0, h))
    operands = [qkv, qkv, qkv, grad_out, mask, cosine, sine]
    if some is None:
        wide = jax.ShapeDtypeStruct((length, heads * head_size), F32)
        return pl.pallas_call(
            attend_back_some_kernel,
            grid=(heads, blocks),
            in_specs=in_specs,
            out_specs=[
                pl.BlockSpec((count, head_size), lambda h, i: (i, h)),
                whole,
                whole,
            ],
            out_shape=[
                jax.ShapeDtypeStruct((blocks * count, heads * head_size), BF16),
                wide,
                wide,
            ],
            cost_estimate=cost,
            name="attend_back_some",
        )(*operands)
    everywhere = pl.BlockSpec((length, head_size), lambda h, i: (0, 0))
    return pl.pallas_call(
        attend_back_last_kernel,
        grid=(heads, 1),
        in_specs=in_specs
        + [
            everywhere,
            everywhere,
            pl.BlockSpec((some[0].shape[0], head_size), lambda h, i: (0, h)),
            whole,
            whole,
        ],
        out_specs=pl.BlockSpec((length, 3 * head_size), lambda h, i: (0, h)),
        out_shape=jax.ShapeDtypeStruct((length, total), BF16),
        cost_estimate=cost,
        name="attend_back_last",
    )(*operands, cosine, sine, *some)


def scatter_raw(values, dimension):
    return lax.psum_scatter(values.astype(BF16), "grp", scatter_dimension=dimension, tiled=True)


def per_device(
    tokens,
    attn_norm,
    query_weight,
    key_weight,
    value_weight,
    query_bias,
    key_bias,
    value_bias,
    out_weight,
    ffn_norm,
    router_weight,
    shared_switch,
    shared_gate,
    shared_up,
    shared_down,
    expert_gate,
    expert_up,
    expert_down,
    routes,
    pieces,
    documents,
    cotangent,
):
    ep_count = lax.axis_size("ep")
    grp_count = lax.axis_size("grp")
    place = lax.axis_index("ep")
    row_count, own_count, model_width = tokens.shape
    length = own_count * ep_count
    heads_here = query_bias.shape[0]
    head_size = query_bias.shape[1] * grp_count
    head_width = heads_here * head_size
    hidden_width = shared_gate.shape[1]
    experts_here = expert_gate.shape[0]
    experts_all = experts_here * ep_count
    top_count = routes.shape[2]
    capacity = (own_count * top_count // experts_all * 5 + 3) // 4
    order = (place - jnp.arange(ep_count, dtype=jnp.int32)) % ep_count

    w_qkv = lax.all_gather(
        by_head(query_weight, key_weight, value_weight, heads_here),
        "grp",
        axis=0,
        tiled=True,
    )
    small_sizes = [
        attn_norm.size,
        query_bias.size,
        key_bias.size,
        value_bias.size,
        ffn_norm.size,
        router_weight.size,
        shared_switch.size,
    ]
    small = gather_small(
        jnp.concatenate(
            [
                part.reshape(-1)
                for part in (
                    attn_norm,
                    query_bias,
                    key_bias,
                    value_bias,
                    ffn_norm,
                    router_weight,
                    shared_switch,
                )
            ]
        ),
        "grp",
    )
    pieces_of_small = []
    begin = 0
    for size in small_sizes:
        pieces_of_small.append(small[:, begin : begin + size])
        begin += size
    gain_first = pieces_of_small[0].reshape(-1).astype(F32)
    biases = [
        part.reshape(grp_count, heads_here, -1).transpose(1, 0, 2).reshape(1, -1)
        for part in pieces_of_small[1:4]
    ]
    bias_qkv = jnp.broadcast_to(
        by_head(*biases, heads_here).astype(F32), (8, 3 * head_width)
    )
    gain_second = pieces_of_small[4].reshape(-1).astype(F32)
    w_router = pieces_of_small[5].reshape(model_width, experts_all)
    w_switch = pieces_of_small[6].reshape(model_width)
    w_out = lax.all_gather(out_weight, "grp", axis=1, tiled=True)
    w_sgu = lax.all_gather(
        jnp.concatenate([shared_gate, shared_up], axis=1), "grp", axis=0, tiled=True
    )
    w_sdown = lax.all_gather(shared_down, "grp", axis=1, tiled=True)

    tokens_own = tokens.reshape(own_count, model_width)
    grad_own_low = cotangent.reshape(own_count, model_width)
    x_blocks = ring_gather(tokens_own, "ep")
    routes_own = routes.reshape(own_count, top_count).T
    chosen = jnp.stack(
        [routes_own]
        + [
            lax.ppermute(routes_own, "ep", [(j, (j + k) % ep_count) for j in range(ep_count)])
            for k in range(1, ep_count)
        ]
    )
    own_places = jnp.arange(own_count, dtype=jnp.int32)
    position = (order[:, None] * own_count + own_places[None, :]).reshape(length)
    piece = jnp.take(pieces.reshape(ep_count, own_count), order, axis=0).reshape(length)
    document = jnp.take(documents.reshape(ep_count, own_count), order, axis=0).reshape(length)
    allowed = (document[:, None] == document[None, :]) & (
        (position[:, None] >= position[None, :])
        | ((piece[:, None] == piece[None, :]) & (piece[:, None] > 0))
    )
    allowed_by_key = (document[:, None] == document[None, :]) & (
        (position[:, None] <= position[None, :])
        | ((piece[:, None] == piece[None, :]) & (piece[:, None] > 0))
    )
    mask = jnp.where(allowed, 0.0, NEG)
    mask_by_key = jnp.where(allowed_by_key, 0.0, NEG)
    cosine_table, sine_table = rotary_tables(position, head_size)
    qkv = jnp.zeros((length, 3 * head_width), BF16)
    h_parts = []
    for k, block in enumerate(x_blocks):
        wide = after(block, qkv).astype(F32)
        h_parts.append((wide * inverse_rms(wide) * gain_first).astype(BF16))
        qkv = project(h_parts[k], w_qkv, bias_qkv, cosine_table, sine_table, qkv, k)
    qkv, chosen = lax.optimization_barrier((qkv, chosen))
    columns_h_one = away_and_near(h_parts, "grp")
    o_parts = [None] * ep_count
    ready = qkv
    for step in range(ep_count):
        k = (step + 1) % ep_count
        o_parts[k] = attend(ready, mask, own_count, head_size, k)
        if step == 1:
            ready = after(ready, columns_h_one, mask_by_key)
        ready, o_parts[k] = lax.optimization_barrier((ready, o_parts[k]))
    o_low = jnp.concatenate(o_parts, axis=0)

    def block_of(values, k):
        return values[k * own_count : (k + 1) * own_count]

    attn_own = ring_reduce(lambda k: times(o_parts[k], w_out), "ep")
    x_own = tokens_own.astype(F32)
    x1_own = x_own + attn_own
    inverse_two = inverse_rms(x1_own)
    hat_two = x1_own * inverse_two
    h_own = (hat_two * gain_second).astype(BF16)
    h_blocks = ring_gather(h_own, "ep")
    h_two = jnp.concatenate(h_blocks, axis=0)
    logits = times(h_two, jnp.concatenate([w_router, w_switch[:, None]], axis=1))
    route_probs = jax.nn.softmax(logits[:, :experts_all], axis=-1)
    switch = jax.nn.sigmoid(logits[:, experts_all])
    expert_ids = place * experts_here + jnp.arange(experts_here, dtype=jnp.int32)
    named = jnp.any(chosen[None] == expert_ids[:, None, None, None], axis=2)
    before = (own_places[:, None] < own_places[None, :]).astype(BF16)
    rank = jnp.einsum("est,tu->esu", named.astype(BF16), before, preferred_element_type=F32).astype(
        jnp.int32
    )
    rank = jnp.where(named & (rank < capacity), rank, -1)
    local_probs = lax.dynamic_slice_in_dim(route_probs, place * experts_here, experts_here, 1)
    local_probs = local_probs.reshape(ep_count, own_count, experts_here).transpose(2, 0, 1)
    hot = (
        rank[:, :, None, :] == jnp.arange(capacity, dtype=jnp.int32)[None, None, :, None]
    )
    gate_slot = jnp.sum(jnp.where(hot, local_probs[:, :, None, :], 0.0), axis=-1)
    slot_shape = (experts_here, ep_count * capacity, model_width)
    gate_rows = gate_slot.reshape(experts_here, ep_count * capacity, 1)

    s_pre = times(h_two, w_sgu)
    s_gate = s_pre[:, :hidden_width]
    s_up = s_pre[:, hidden_width:]
    sig_shared = jax.nn.sigmoid(s_gate)
    silu_shared = s_gate * sig_shared
    s_hidden = (silu_shared * s_up).astype(BF16)
    s_part = times(s_hidden, w_sdown).astype(BF16)
    grad_blocks = lax.all_gather(after(grad_own_low, h_blocks[-1]), "ep", axis=0)
    flat_rows = select_rows(rank, after(h_two, s_part), capacity)
    flat_rows = flat_rows.reshape(slot_shape)
    gate_pre, up_pre, hidden = expert_up_all(flat_rows, expert_gate, expert_up)
    result = expert_down_all(hidden, expert_down)
    grad_blocks = after(grad_blocks, result)
    grad_low = jnp.take(grad_blocks, order, axis=0).reshape(length, model_width)
    grad_all = grad_low.astype(F32)
    grad_sout = (switch[:, None] * grad_all).astype(BF16)
    grad_shidden = times_trans(grad_sout, w_sdown)
    slope_shared = sig_shared * (1.0 + s_gate * (1.0 - sig_shared))
    grad_s = jnp.concatenate(
        [
            (grad_shidden * s_up * slope_shared).astype(BF16),
            (grad_shidden * silu_shared).astype(BF16),
        ],
        axis=1,
    )
    row_shape = (experts_here, ep_count, capacity, model_width)
    y_part = spread_rows(rank, local_probs, result.reshape(row_shape), switch, s_part)
    y_first = block_of(y_part, 1 % ep_count)
    part_sdown = inner_rows(s_hidden, after(grad_sout, grad_s)).astype(BF16)
    part_sgu = inner_rows(after(h_two, part_sdown), grad_s).astype(BF16)
    raw_sdown = scatter_raw(part_sdown, 1)
    raw_sgu = scatter_raw(part_sgu, 0)
    grad_rows = select_rows(
        rank, after(grad_low, y_first, part_sdown, part_sgu), capacity
    ).reshape(slot_shape)
    grad_gate_pre, grad_up_pre, hidden_gated, grad_gate = expert_back_all(
        grad_rows, expert_down, gate_pre, up_pre, hidden, gate_rows
    )

    routed = []

    def beside_y(step, sent):
        if step == 1:
            return [grad_gate_pre]
        if step == 2:
            part = jnp.einsum(
                "erf,erd->efd", after(hidden_gated, sent), grad_rows, preferred_element_type=F32
            )
            routed.append(part.astype(BF16))
            return routed[:]
        if step == 3:
            routed.append(
                expert_in_all(
                    after(grad_gate_pre, routed[0], sent), grad_up_pre, expert_gate, expert_up
                )
            )
            return routed[1:]
        return []

    layer_own = x1_own + ring_reduce(lambda k: block_of(y_part, k), "ep", y_first, beside_y)
    part_edown, grad_inputs = routed
    raw_edown = scatter_raw(part_edown, 2)
    shared_dot = jnp.sum(grad_all * s_part.astype(F32), axis=-1).reshape(1, ep_count, own_count)
    grad_probs_part = jnp.sum(
        jnp.where(
            hot, grad_gate.reshape(experts_here, ep_count, capacity)[:, :, :, None], 0.0
        ),
        axis=2,
    )
    scalars = jnp.concatenate([grad_probs_part, shared_dot], axis=0)
    home = [scalars[:, 0]]
    for k in range(1, ep_count):
        home.append(
            lax.ppermute(scalars[:, k], "ep", [(j, (j - k) % ep_count) for j in range(ep_count)])
        )
    grad_inputs, layer_own, *home = lax.optimization_barrier((grad_inputs, layer_own, *home))
    home = jnp.stack(home)
    grad_moe = spread_rows(rank, jnp.ones_like(local_probs), grad_inputs.reshape(row_shape))

    grad_probs = jnp.take(
        home[:, :experts_here],
        (jnp.arange(ep_count, dtype=jnp.int32) - place) % ep_count,
        axis=0,
    )
    grad_probs = grad_probs.reshape(experts_all, own_count).T
    probs_own = route_probs[:own_count]
    switch_own = switch[:own_count]
    grad_logit = (
        probs_own * (grad_probs - jnp.sum(probs_own * grad_probs, axis=-1, keepdims=True))
    ).astype(BF16)
    grad_switch = (
        jnp.sum(home[:, experts_here], axis=0) * switch_own * (1.0 - switch_own)
    ).astype(BF16)

    w_small = jnp.concatenate([w_router, w_switch[:, None]], axis=1)
    grad_small = jnp.concatenate([grad_logit, grad_switch[:, None]], axis=1)
    layer_out = layer_own.reshape(row_count, own_count, model_width).astype(BF16)

    def grad_h2_part(k):
        return times_trans(block_of(grad_s, k), w_sgu) + block_of(grad_moe, k)

    grad_h2_first = grad_h2_part(1 % ep_count).astype(BF16)
    forms = (
        ("erd,erf->edf", flat_rows, grad_gate_pre),
        ("erd,erf->edf", flat_rows, grad_up_pre),
    )
    expert_raw = []

    def expert_part(sent):
        form, left_side, right_side = forms[len(expert_raw)]
        left_side, right_side, _ = lax.optimization_barrier((left_side, right_side, sent))
        part = jnp.einsum(form, left_side, right_side, preferred_element_type=F32).astype(BF16)
        expert_raw.append(scatter_raw(part, 1))
        return part

    def beside_h2(step, sent):
        return {1: [raw_sdown], 2: [expert_part, raw_sgu], 3: [expert_part]}.get(step, [])

    grad_h2 = ring_reduce(
        grad_h2_part,
        "ep",
        grad_h2_first,
        lambda step, sent: [
            item(sent) if callable(item) else item for item in beside_h2(step, sent)
        ],
        times_trans(grad_s[2 * own_count :], w_sgu) + grad_moe[2 * own_count :],
    ) + times_trans(grad_small, w_small)
    weighted = grad_h2 * gain_second
    grad_x1 = grad_own_low.astype(F32) + inverse_two * (
        weighted - hat_two * jnp.mean(weighted * hat_two, axis=-1, keepdims=True)
    )
    grad_x1_low = grad_x1.astype(BF16)
    while len(expert_raw) < len(forms):
        expert_part(grad_x1_low)
    grad_attn_blocks = ring_gather(grad_x1_low, "ep")

    gain_two_part = jnp.sum(grad_h2 * hat_two, axis=0)
    small_part = jnp.concatenate([inner_rows(grad_small, h_own), gain_two_part[None, :]], axis=0)
    small_grp = sum_all(small_part, "grp")
    back_tables = (mask_by_key, cosine_table, sine_table, own_count)
    grad_o = [times_trans(block, w_out).astype(BF16) for block in grad_attn_blocks[:-1]]
    some_back = attend_back(after(qkv, small_grp), jnp.concatenate(grad_o, axis=0), *back_tables)
    last_block = after(grad_attn_blocks[-1], *some_back)
    grad_qkv = attend_back(
        qkv, times_trans(last_block, w_out).astype(BF16), *back_tables, some_back
    )
    chunk_width = model_width // grp_count
    grp_place = lax.axis_index("grp")
    qkv_half = 3 * head_width // 2
    grad_h1_first = times_trans(block_of(grad_qkv, 1 % ep_count), w_qkv).astype(BF16)

    def qkv_part(columns, p):
        return inner_rows(columns, grad_qkv[:, p * qkv_half : (p + 1) * qkv_half])

    def out_part(columns, p):
        return inner_rows(o_low[:, p * head_width // 2 : (p + 1) * head_width // 2], columns)

    qkv_left, qkv_columns, qkv_come = halving_send(
        qkv_part, after(columns_h_one, grad_h1_first), "grp", 2
    )
    near_sums = []
    out_sent = []

    def beside_h1(step, sent):
        if step == 1:
            return qkv_left
        if step == 2:
            near_sums.append(halving_near(qkv_part, qkv_columns, qkv_come, sent))
            columns_grad_attn = away_and_near(
                [after(block, *near_sums[0]) for block in grad_attn_blocks], "grp"
            )
            out_sent.extend(halving_send(out_part, columns_grad_attn, "grp", 2))
            return near_sums[0]
        if step == 3:
            near_sums.append(halving_near(out_part, out_sent[1], out_sent[2], sent))
            return near_sums[1]
        return []

    grad_h1 = ring_reduce(
        lambda k: times_trans(block_of(grad_qkv, k), w_qkv),
        "ep",
        grad_h1_first,
        beside_h1,
        times_trans(grad_qkv[2 * own_count :], w_qkv),
    )
    qkv_near, out_near = near_sums
    grad_tokens = grad_x1 + norm_back(x_own, gain_first, grad_h1)
    tokens_grad = grad_tokens.reshape(row_count, own_count, model_width)
    gain_one_part = jnp.sum(grad_h1 * (x_own * inverse_rms(x_own)), axis=0)
    sum_sdown, sum_sgu, sum_edown, sum_egate, sum_eup = (
        raw.astype(F32) for raw in (raw_sdown, raw_sgu, raw_edown, *expert_raw)
    )
    gain_one_part = after(gain_one_part, sum_sdown, sum_sgu, sum_edown)
    last_part = jnp.concatenate([gain_one_part, jnp.sum(grad_qkv.astype(F32), axis=0)])[None, :]
    sum_qkv = jnp.concatenate(halving_rest(qkv_near, "grp", 0, last_part), axis=1)
    sum_out = jnp.concatenate(halving_rest(out_near, "grp", 1, last_part), axis=0)
    last_grp = sum_all(last_part, "grp")
    last_grp, sum_egate, sum_eup = lax.optimization_barrier((last_grp, sum_egate, sum_eup))
    bias_width = head_size // grp_count
    sum_bias = lax.dynamic_slice_in_dim(
        last_grp[:, model_width:].reshape(3 * heads_here, head_size),
        grp_place * bias_width,
        bias_width,
        1,
    )
    small_sum = sum_all(
        lax.dynamic_slice_in_dim(
            jnp.concatenate([small_grp, last_grp[:, :model_width]], axis=0),
            grp_place * chunk_width,
            chunk_width,
            1,
        ),
        "ep",
    )

    def of_heads(values, part):
        begins = range(part * head_size, 3 * head_width, 3 * head_size)
        return jnp.concatenate([values[:, b : b + head_size] for b in begins], axis=1)

    return (
        layer_out,
        tokens_grad,
        small_sum[experts_all + 2],
        of_heads(sum_qkv, 0),
        of_heads(sum_qkv, 1),
        of_heads(sum_qkv, 2),
        sum_bias[0::3],
        sum_bias[1::3],
        sum_bias[2::3],
        sum_out,
        small_sum[experts_all + 1],
        small_sum[:experts_all].T,
        small_sum[experts_all],
        sum_sgu[:, :hidden_width],
        sum_sgu[:, hidden_width:],
        sum_sdown,
        sum_egate,
        sum_eup,
        sum_edown,
    )


def solution(mesh):
    return jax.shard_map(
        per_device,
        mesh=mesh,
        in_specs=(
            P("grp", "ep", None),
            P("grp"),
            P("grp", "ep"),
            P("grp", "ep"),
            P("grp", "ep"),
            P("ep", "grp"),
            P("ep", "grp"),
            P("ep", "grp"),
            P("ep", "grp"),
            P("grp"),
            P("grp", None),
            P("grp"),
            P("grp", "ep"),
            P("grp", "ep"),
            P("ep", "grp"),
            P("ep", None, None),
            P("ep", None, None),
            P("ep", None, None),
            P("grp", "ep", None),
            P("grp", None),
            P("grp", None),
            P("grp", "ep", None),
        ),
        out_specs=(
            P("grp", "ep", None),
            P("grp", "ep", None),
            P("grp"),
            P("grp", "ep"),
            P("grp", "ep"),
            P("grp", "ep"),
            P("ep", "grp"),
            P("ep", "grp"),
            P("ep", "grp"),
            P("ep", "grp"),
            P("grp"),
            P("grp", None),
            P("grp"),
            P("grp", "ep"),
            P("grp", "ep"),
            P("ep", "grp"),
            P("ep", "grp", None),
            P("ep", "grp", None),
            P("ep", None, "grp"),
        ),
        check_vma=False,
    )
```
